32 devices in a mesh: dp: 8 (over z, core), tensor: 4 (over y, x).
Axes of the slice: x: 2, y: 2, z: 4, core: 2. Of those that a mesh axis runs over, the one named last changes fastest.
Arguments:
- tokens: bfloat16 [4096, 2048], P('dp'), may hold values from -6 to 6
- positions: int32 [4096], P('dp'), may hold values from 0 to 255, as said below
- w_qkv: bfloat16 [2048, 3072], P('dp', 'tensor'), may hold values from -4 to 4
- w_out: bfloat16 [2048, 2048], P('tensor', 'dp'), may hold values from -0.5 to 0.5
- w_gate: bfloat16 [2048, 8192], P('dp', 'tensor'), may hold values from -0.125 to 0.125
- w_up: bfloat16 [2048, 8192], P('dp', 'tensor'), may hold values from -0.125 to 0.125
- w_down: bfloat16 [8192, 2048], P('tensor', 'dp'), may hold values from -0.0625 to 0.0625
- gain_attn: bfloat16 [2048], P('dp'), may hold values from 0.5 to 1.5
- gain_ffn: bfloat16 [2048], P('dp'), may hold values from 0.5 to 1.5
- cotangent: bfloat16 [4096, 2048], P('dp'), may hold values from -6 to 6
Outputs:
- output: bfloat16 [4096, 2048], P('dp')
- d_tokens: bfloat16 [4096, 2048], P('dp')
- grad_qkv: float32 [2048, 3072], P('dp', 'tensor')
- grad_out_proj: float32 [2048, 2048], P('tensor', 'dp')
- grad_gate: float32 [2048, 8192], P('dp', 'tensor')
- grad_up: float32 [2048, 8192], P('dp', 'tensor')
- grad_down: float32 [8192, 2048], P('tensor', 'dp')
- grad_gain_attn: float32 [2048], P('dp')
- grad_gain_ffn: float32 [2048], P('dp')
The draws below stay inside these ranges and needn't reach their ends.
Inputs may be any that keep to these rules, and one draw needn't show every extreme that they name: `positions`: each sequence of 256 tokens is a pack of documents; a token's position counts from the first token of its document, which has position 0, and rises by one from token to token inside a document.
All inputs are finite; a program needn't handle non-finite values.
Results may differ from the reference program's by a relative error of at most 0.023.
Values may be sent and summed in bfloat16 or wider, within the bound.
A program may use at most 192 MiB of HBM per device.

```python
import math
import jax
import jax.numpy as jnp
from jax import lax

D = 2048
HEADS = 32
KV_HEADS = 8
HD = 64
FF = 8192
SEQ = 256
QKVW = 3072
QW = 2048
TOK_DEV = 512
TOKENS = 4096
N_DP = 8
N_TENSOR = 4


def draw_tokens(key, part):
    base = jnp.clip(jax.random.normal(key, (TOKENS, D), jnp.float32), -6.0, 6.0)
    return base.astype(jnp.bfloat16)


def draw_w_qkv(key, part):
    groups = HEADS // KV_HEADS
    weights = jnp.clip(jax.random.normal(key, (D, KV_HEADS * (groups + 2) * HD), jnp.float32), -4.0, 4.0) * D ** (-0.5)
    return weights.astype(jnp.bfloat16)


def draw_positions(key, part):
    first, second = jax.random.split(key)
    seq_count = TOKENS // SEQ
    column_index = lax.broadcasted_iota(jnp.int32, (seq_count, SEQ), 1)
    row_index = lax.broadcasted_iota(jnp.int32, (seq_count, SEQ), 0)
    boundary = jax.random.randint(first, (seq_count, SEQ), 0, 32) == 0
    drawn_row = jax.random.randint(second, (), 0, seq_count)
    boundary = jnp.where(column_index == 0, True, jnp.where(row_index == drawn_row, False, boundary))
    marks = jnp.where(boundary, column_index, 0)
    latest = lax.cummax(marks, axis=1)
    return (column_index - latest).reshape(TOKENS).astype(jnp.int32)


def strengthened(array, stream_key, source, target, shards_of, factor):
    def block_of(dim):
        return (jnp.arange(array.shape[dim]) // (array.shape[dim] // shards_of)).reshape((-1,) + (1,) * (array.ndim - 1 - dim))

    one_side = jax.random.permutation(stream_key, shards_of)[block_of(target)]
    other_side = (block_of(target) + shards_of // 2) % shards_of
    return jnp.where((block_of(source) == one_side) | (block_of(source) == other_side), factor * array, array)


def levels(own_key, dims, shards, low, largest):
    level, own = 1.0, jax.random.fold_in(own_key, 6)
    for dim, shards_of in shards:
        draws = jnp.exp(jax.random.uniform(jax.random.fold_in(own, dim), (shards_of,), jnp.float32, low / len(shards), largest / len(shards)))
        level = level * jnp.repeat(draws, dims[dim] // shards_of).reshape([-1 if axis == dim else 1 for axis in range(len(dims))])
    return level


def scatter_about(stream_key, dims, spread, limit, shards=(), kind=jnp.bfloat16):
    level = levels(stream_key, dims, shards, -0.22, 0.18) if shards else 1.0
    values = jax.random.normal(stream_key, dims, jnp.float32) * spread * level
    return jnp.minimum(jnp.maximum(values, -limit), limit).astype(kind)


def bell_draw_with(rng, dims, deviation, reach, pieces, heavy, kind=jnp.bfloat16):
    result = deviation * jax.random.normal(rng, dims, jnp.float32)
    if pieces:
        result = result * levels(rng, dims, pieces, -0.22, 0.18)
    return jnp.clip(strengthened(result, jax.random.fold_in(rng, 3), *heavy), -reach, reach).astype(kind)


def setup_inputs(seed: int = 0) -> dict:
    streams_of = jax.random.split(jax.random.key(seed), 11)
    tokens = draw_tokens(jax.random.fold_in(streams_of[10], 71), 0)
    positions = draw_positions(jax.random.fold_in(streams_of[10], 71), 0)
    w_qkv = draw_w_qkv(jax.random.fold_in(streams_of[10], 71), 0)
    w_out = scatter_about(streams_of[3], (QW, D), (QW // 16) ** -0.5, 0.5, ((0, 4), (1, 8)))
    w_gate = scatter_about(streams_of[4], (D, FF), D ** -0.5, 0.125, ((0, 8), (1, 4)))
    w_up = scatter_about(streams_of[5], (D, FF), D ** -0.5, 0.125, ((0, 8), (1, 4)))
    w_down = scatter_about(streams_of[6], (FF, D), FF ** -0.5, 0.0625, ((0, 4), (1, 8)))
    gain_attn = jnp.clip(1.0 + 0.1 * jax.random.normal(streams_of[7], (D,), jnp.float32), 0.5, 1.5).astype(jnp.bfloat16)
    gain_ffn = jnp.clip(1.0 + 0.1 * jax.random.normal(streams_of[8], (D,), jnp.float32), 0.5, 1.5).astype(jnp.bfloat16)
    cotangent = bell_draw_with(streams_of[9], (TOKENS, D), 1.0, 6.0, ((0, 8),), (0, 1, 8, 2.0))
    return {"tokens": tokens, "positions": positions, "w_qkv": w_qkv, "w_out": w_out, "w_gate": w_gate, "w_up": w_up, "w_down": w_down, "gain_attn": gain_attn, "gain_ffn": gain_ffn, "cotangent": cotangent}


epsilon = 1e-05
rope_base = 500000.0
masked_score = -1e+30

def rotary_tables(positions, head_dim):
    half_dim = head_dim // 2
    exponents = jnp.arange(half_dim, dtype=jnp.float32) * (2.0 / head_dim)
    frequency = jnp.exp(-exponents * math.log(rope_base))
    angles = positions.astype(jnp.float32)[:, None] * frequency[None, :]
    angles = jnp.concatenate([angles, angles], axis=1)
    return (jnp.cos(angles), jnp.sin(angles))

def half_turn(values):
    half_dim = values.shape[-1] // 2
    return jnp.concatenate([-values[..., half_dim:], values[..., :half_dim]], axis=-1)

def back_turn(values):
    half_dim = values.shape[-1] // 2
    return jnp.concatenate([values[..., half_dim:], -values[..., :half_dim]], axis=-1)

def norm_forward(rows, gain):
    scale = lax.rsqrt(lax.optimization_barrier(jnp.mean(rows * rows, axis=-1, keepdims=True)) + epsilon)
    return (scale, (rows * scale * gain).astype(jnp.bfloat16))

def norm_backward(rows, scale, gain, upstream):
    weighted = upstream * gain
    inner = lax.optimization_barrier(jnp.mean(weighted * rows, axis=-1, keepdims=True))
    grad_rows = scale * weighted - rows * (scale * scale * scale) * inner
    grad_gain = lax.optimization_barrier(jnp.sum(upstream * rows * scale, axis=0))
    return (grad_rows, grad_gain)

def causal_mask(length):
    row_index = lax.broadcasted_iota(jnp.int32, (length, length), 0)
    col_index = lax.broadcasted_iota(jnp.int32, (length, length), 1)
    return row_index >= col_index

def attention_forward(joined, cosine, sine, groups, head_dim, length):
    count = joined.shape[0]
    kv_local = joined.shape[1] // ((groups + 2) * head_dim)
    seqs = count // length
    shaped = joined.reshape(seqs, length, kv_local, groups + 2, head_dim)
    cos_five = cosine.reshape(seqs, length, 1, 1, head_dim)
    sin_five = sine.reshape(seqs, length, 1, 1, head_dim)
    turned = shaped[:, :, :, :groups + 1]
    rotated = turned * cos_five + half_turn(turned) * sin_five
    query = rotated[:, :, :, :groups].astype(jnp.bfloat16)
    keys = rotated[:, :, :, groups].astype(jnp.bfloat16)
    values = shaped[:, :, :, groups + 1].astype(jnp.bfloat16)
    scores = jnp.einsum('sikgd,sjkd->skgij', query.astype(jnp.float32), keys.astype(jnp.float32)) * (1.0 / math.sqrt(head_dim))
    scores = jnp.where(causal_mask(length), scores, masked_score)
    peak = lax.optimization_barrier(jnp.max(scores, axis=-1, keepdims=True))
    lse = peak[..., 0] + jnp.log(lax.optimization_barrier(jnp.sum(jnp.exp(scores - peak), axis=-1)))
    probs = jnp.exp(scores - lse[..., None]).astype(jnp.bfloat16)
    attended = jnp.einsum('skgij,sjkd->sikgd', probs.astype(jnp.float32), values.astype(jnp.float32))
    attended = attended.astype(jnp.bfloat16).reshape(count, kv_local * groups * head_dim)
    return (attended, lse, query, keys, values)

def attention_backward(d_attended, attended, lse, query, keys, values, cosine, sine, length):
    seqs, _, kv_local, groups, head_dim = query.shape
    count = seqs * length
    scores = jnp.einsum('sikgd,sjkd->skgij', query.astype(jnp.float32), keys.astype(jnp.float32)) * (1.0 / math.sqrt(head_dim))
    scores = jnp.where(causal_mask(length), scores, masked_score)
    probs = jnp.exp(scores - lse[..., None])
    probs_low = probs.astype(jnp.bfloat16)
    d_five = d_attended.reshape(seqs, length, kv_local, groups, head_dim)
    att_five = attended.reshape(seqs, length, kv_local, groups, head_dim)
    d_values = jnp.einsum('skgij,sikgd->sjkd', probs_low.astype(jnp.float32), d_five.astype(jnp.float32))
    d_probs = jnp.einsum('sikgd,sjkd->skgij', d_five.astype(jnp.float32), values.astype(jnp.float32))
    delta = lax.optimization_barrier(jnp.sum(d_five.astype(jnp.float32) * att_five.astype(jnp.float32), axis=-1))
    delta = jnp.transpose(delta, (0, 2, 3, 1))
    d_scores = (probs * (d_probs - delta[..., None]) * (1.0 / math.sqrt(head_dim))).astype(jnp.bfloat16)
    d_query = jnp.einsum('skgij,sjkd->sikgd', d_scores.astype(jnp.float32), keys.astype(jnp.float32))
    d_keys = jnp.einsum('skgij,sikgd->sjkd', d_scores.astype(jnp.float32), query.astype(jnp.float32))
    cos_five = cosine.reshape(seqs, length, 1, 1, head_dim)
    sin_five = sine.reshape(seqs, length, 1, 1, head_dim)
    d_query = d_query * cos_five + back_turn(d_query * sin_five)
    d_keys = d_keys * cos_five[:, :, :, 0] + back_turn(d_keys * sin_five[:, :, :, 0])
    d_joined = jnp.concatenate([d_query, d_keys[:, :, :, None], d_values[:, :, :, None]], axis=3)
    return d_joined.astype(jnp.bfloat16).reshape(count, kv_local * (groups + 2) * head_dim)

def reference(tokens, positions, w_qkv, w_out, w_gate, w_up, w_down, gain_attn, gain_ffn, cotangent):
    groups = HEADS // KV_HEADS
    gain_first = gain_attn.astype(jnp.float32)
    gain_second = gain_ffn.astype(jnp.float32)
    qkv_split = w_qkv.astype(jnp.float32).reshape(D, N_TENSOR, QKVW // N_TENSOR)
    out_split = w_out.astype(jnp.float32).reshape(N_TENSOR, QW // N_TENSOR, D)
    gate_split = w_gate.astype(jnp.float32).reshape(D, N_TENSOR, FF // N_TENSOR)
    up_split = w_up.astype(jnp.float32).reshape(D, N_TENSOR, FF // N_TENSOR)
    down_split = w_down.astype(jnp.float32).reshape(N_TENSOR, FF // N_TENSOR, D)

    def block(carry, inputs):
        rows_low, place, upstream = inputs
        count = rows_low.shape[0]
        rows = rows_low.astype(jnp.float32)
        scale_attn, normed_attn = norm_forward(rows, gain_first)
        joined = jnp.dot(normed_attn, w_qkv, preferred_element_type=jnp.float32)
        cosine, sine = rotary_tables(place, HD)
        attended, lse, query, keys, values = attention_forward(joined, cosine, sine, groups, HD, SEQ)
        attn_partial = jnp.einsum('btk,tkd->btd', attended.astype(jnp.float32).reshape(count, N_TENSOR, QW // N_TENSOR), out_split).astype(jnp.bfloat16)
        attn_mix = lax.optimization_barrier(jnp.sum(attn_partial.astype(jnp.float32), axis=1))
        resid = rows + attn_mix
        scale_ffn, normed_ffn = norm_forward(resid, gain_second)
        gate = jnp.dot(normed_ffn, w_gate, preferred_element_type=jnp.float32)
        up = jnp.dot(normed_ffn, w_up, preferred_element_type=jnp.float32)
        sigma = jax.nn.sigmoid(gate)
        hidden = (gate * sigma * up).astype(jnp.bfloat16)
        ffn_partial = jnp.einsum('btk,tkd->btd', hidden.astype(jnp.float32).reshape(count, N_TENSOR, FF // N_TENSOR), down_split).astype(jnp.bfloat16)
        ffn_mix = lax.optimization_barrier(jnp.sum(ffn_partial.astype(jnp.float32), axis=1))
        output = (resid + ffn_mix).astype(jnp.bfloat16)
        d_hidden = jnp.dot(upstream, w_down.T, preferred_element_type=jnp.float32)
        grad_down = jnp.dot(hidden.T, upstream, preferred_element_type=jnp.float32)
        d_up = (d_hidden * gate * sigma).astype(jnp.bfloat16)
        d_gate = (d_hidden * up * sigma * (1.0 + gate * (1.0 - sigma))).astype(jnp.bfloat16)
        grad_gate = jnp.dot(normed_ffn.T, d_gate, preferred_element_type=jnp.float32)
        grad_up = jnp.dot(normed_ffn.T, d_up, preferred_element_type=jnp.float32)
        ffn_back = jnp.einsum('btk,dtk->btd', d_gate.astype(jnp.float32).reshape(count, N_TENSOR, FF // N_TENSOR), gate_split)
        ffn_back = ffn_back + jnp.einsum('btk,dtk->btd', d_up.astype(jnp.float32).reshape(count, N_TENSOR, FF // N_TENSOR), up_split)
        d_normed_ffn = lax.optimization_barrier(jnp.sum(ffn_back.astype(jnp.bfloat16).astype(jnp.float32), axis=1))
        grad_rows_ffn, grad_gain_ffn = norm_backward(resid, scale_ffn, gain_second, d_normed_ffn)
        d_resid = upstream.astype(jnp.float32) + grad_rows_ffn
        resid_grad = d_resid.astype(jnp.bfloat16)
        grad_out_proj = jnp.dot(attended.T, resid_grad, preferred_element_type=jnp.float32)
        d_attended = jnp.dot(resid_grad, w_out.T, preferred_element_type=jnp.float32).astype(jnp.bfloat16)
        d_joined = attention_backward(d_attended, attended, lse, query, keys, values, cosine, sine, SEQ)
        grad_qkv = jnp.dot(normed_attn.T, d_joined, preferred_element_type=jnp.float32)
        attn_back = jnp.einsum('btc,dtc->btd', d_joined.astype(jnp.float32).reshape(count, N_TENSOR, QKVW // N_TENSOR), qkv_split).astype(jnp.bfloat16)
        d_normed_attn = lax.optimization_barrier(jnp.sum(attn_back.astype(jnp.float32), axis=1))
        grad_rows_attn, grad_gain_attn = norm_backward(rows, scale_attn, gain_first, d_normed_attn)
        d_tokens = (d_resid + grad_rows_attn).astype(jnp.bfloat16)
        terms = (grad_qkv, grad_out_proj, grad_gate, grad_up, grad_down, grad_gain_attn, grad_gain_ffn)
        carry = tuple((total + term for total, term in zip(carry, terms)))
        return (carry, (output, d_tokens))
    start = (jnp.zeros((D, QKVW), jnp.float32), jnp.zeros((QW, D), jnp.float32), jnp.zeros((D, FF), jnp.float32), jnp.zeros((D, FF), jnp.float32), jnp.zeros((FF, D), jnp.float32), jnp.zeros((D,), jnp.float32), jnp.zeros((D,), jnp.float32))
    inputs = (tokens.reshape(N_DP, TOK_DEV, D), positions.reshape(N_DP, TOK_DEV), cotangent.reshape(N_DP, TOK_DEV, D))
    totals, stacked = lax.scan(block, start, inputs)
    output = stacked[0].reshape(TOKENS, D)
    d_tokens = stacked[1].reshape(TOKENS, D)
    return (output, d_tokens, totals[0], totals[1], totals[2], totals[3], totals[4], totals[5], totals[6])
```

```python
import math

import jax
import jax.numpy as jnp
from jax import lax
from jax.sharding import PartitionSpec as P

HEADS = 32
KV_HEADS = 8
HD = 64
SEQ = 256
MICRO = 1


epsilon = 1e-05
rope_base = 500000.0
masked_score = -1e30


def rotary_tables(positions, head_dim):
    half_dim = head_dim // 2
    exponents = jnp.arange(half_dim, dtype=jnp.float32) * (2.0 / head_dim)
    frequency = jnp.exp(-exponents * math.log(rope_base))
    angles = positions.astype(jnp.float32)[:, None] * frequency[None, :]
    angles = jnp.concatenate([angles, angles], axis=1)
    return (jnp.cos(angles), jnp.sin(angles))


def half_turn(values):
    half_dim = values.shape[-1] // 2
    return jnp.concatenate([-values[..., half_dim:], values[..., :half_dim]], axis=-1)


def back_turn(values):
    half_dim = values.shape[-1] // 2
    return jnp.concatenate([values[..., half_dim:], -values[..., :half_dim]], axis=-1)


def norm_forward(rows, gain):
    scale = lax.rsqrt(jnp.mean(rows * rows, axis=-1, keepdims=True) + epsilon)
    return (scale, (rows * scale * gain).astype(jnp.bfloat16))


def norm_backward(rows, scale, gain, upstream):
    weighted = upstream * gain
    inner = jnp.mean(weighted * rows, axis=-1, keepdims=True)
    grad_rows = scale * weighted - rows * (scale * scale * scale) * inner
    grad_gain = jnp.sum(upstream * rows * scale, axis=0)
    return (grad_rows, grad_gain)


def causal_mask(length):
    row_index = lax.broadcasted_iota(jnp.int32, (length, length), 0)
    col_index = lax.broadcasted_iota(jnp.int32, (length, length), 1)
    return row_index >= col_index


def attention_forward(joined, cosine, sine, groups, head_dim, length):
    count = joined.shape[0]
    kv_local = joined.shape[1] // ((groups + 2) * head_dim)
    seqs = count // length
    shaped = joined.reshape(seqs, length, kv_local, groups + 2, head_dim)
    cos_five = cosine.reshape(seqs, length, 1, 1, head_dim)
    sin_five = sine.reshape(seqs, length, 1, 1, head_dim)
    turned = shaped[:, :, :, : groups + 1]
    rotated = turned * cos_five + half_turn(turned) * sin_five
    query = rotated[:, :, :, :groups].astype(jnp.bfloat16)
    keys = rotated[:, :, :, groups].astype(jnp.bfloat16)
    values = shaped[:, :, :, groups + 1].astype(jnp.bfloat16)
    scores = jnp.einsum("sikgd,sjkd->skgij", query, keys, preferred_element_type=jnp.float32) * (
        1.0 / math.sqrt(head_dim)
    )
    scores = jnp.where(causal_mask(length), scores, masked_score)
    peak = jnp.max(scores, axis=-1, keepdims=True)
    lse = peak[..., 0] + jnp.log(jnp.sum(jnp.exp(scores - peak), axis=-1))
    probs = jnp.exp(scores - lse[..., None]).astype(jnp.bfloat16)
    attended = jnp.einsum("skgij,sjkd->sikgd", probs, values, preferred_element_type=jnp.float32)
    attended = attended.astype(jnp.bfloat16).reshape(count, kv_local * groups * head_dim)
    return (attended, lse, query, keys, values)


def attention_backward(d_attended, attended, lse, query, keys, values, cosine, sine, length):
    seqs, _, kv_local, groups, head_dim = query.shape
    count = seqs * length
    scores = jnp.einsum("sikgd,sjkd->skgij", query, keys, preferred_element_type=jnp.float32) * (
        1.0 / math.sqrt(head_dim)
    )
    scores = jnp.where(causal_mask(length), scores, masked_score)
    probs = jnp.exp(scores - lse[..., None])
    probs_low = probs.astype(jnp.bfloat16)
    d_five = d_attended.reshape(seqs, length, kv_local, groups, head_dim)
    att_five = attended.reshape(seqs, length, kv_local, groups, head_dim)
    d_values = jnp.einsum(
        "skgij,sikgd->sjkd", probs_low, d_five, preferred_element_type=jnp.float32
    )
    d_probs = jnp.einsum("sikgd,sjkd->skgij", d_five, values, preferred_element_type=jnp.float32)
    delta = jnp.sum(d_five.astype(jnp.float32) * att_five.astype(jnp.float32), axis=-1)
    delta = jnp.transpose(delta, (0, 2, 3, 1))
    d_scores = (probs * (d_probs - delta[..., None]) * (1.0 / math.sqrt(head_dim))).astype(
        jnp.bfloat16
    )
    d_query = jnp.einsum("skgij,sjkd->sikgd", d_scores, keys, preferred_element_type=jnp.float32)
    d_keys = jnp.einsum("skgij,sikgd->sjkd", d_scores, query, preferred_element_type=jnp.float32)
    cos_five = cosine.reshape(seqs, length, 1, 1, head_dim)
    sin_five = sine.reshape(seqs, length, 1, 1, head_dim)
    d_query = d_query * cos_five + back_turn(d_query * sin_five)
    d_keys = d_keys * cos_five[:, :, :, 0] + back_turn(d_keys * sin_five[:, :, :, 0])
    d_joined = jnp.concatenate([d_query, d_keys[:, :, :, None], d_values[:, :, :, None]], axis=3)
    return d_joined.astype(jnp.bfloat16).reshape(count, kv_local * (groups + 2) * head_dim)


def layer_pass(rows_low, place, upstream, forward_set, backward_set):
    qkv_full, out_full, gate_full, up_full, down_full, gain_one, gain_two = forward_set
    qkv_back, out_back, gate_back, up_back, down_back = backward_set
    groups = HEADS // KV_HEADS
    rows = rows_low.astype(jnp.float32)
    gain_first = gain_one.astype(jnp.float32)
    gain_second = gain_two.astype(jnp.float32)
    scale_attn, normed_attn = norm_forward(rows, gain_first)
    joined = jnp.dot(normed_attn, qkv_full, preferred_element_type=jnp.float32)
    cosine, sine = rotary_tables(place, HD)
    attended, lse, query, keys, values = attention_forward(joined, cosine, sine, groups, HD, SEQ)
    attn_partial = jnp.dot(attended, out_full, preferred_element_type=jnp.float32).astype(
        jnp.bfloat16
    )
    attn_mix = lax.psum(attn_partial, "tensor").astype(jnp.float32)
    resid = rows + attn_mix
    scale_ffn, normed_ffn = norm_forward(resid, gain_second)
    gate = jnp.dot(normed_ffn, gate_full, preferred_element_type=jnp.float32)
    up = jnp.dot(normed_ffn, up_full, preferred_element_type=jnp.float32)
    sigma = jax.nn.sigmoid(gate)
    hidden = (gate * sigma * up).astype(jnp.bfloat16)
    ffn_partial = jnp.dot(hidden, down_full, preferred_element_type=jnp.float32).astype(
        jnp.bfloat16
    )
    ffn_mix = lax.psum(ffn_partial, "tensor").astype(jnp.float32)
    output = (resid + ffn_mix).astype(jnp.bfloat16)
    d_hidden = jnp.dot(upstream, down_back.T, preferred_element_type=jnp.float32)
    grad_down = jnp.dot(hidden.T, upstream, preferred_element_type=jnp.float32)
    d_up = (d_hidden * gate * sigma).astype(jnp.bfloat16)
    d_gate = (d_hidden * up * sigma * (1.0 + gate * (1.0 - sigma))).astype(jnp.bfloat16)
    grad_gate = jnp.dot(normed_ffn.T, d_gate, preferred_element_type=jnp.float32)
    grad_up = jnp.dot(normed_ffn.T, d_up, preferred_element_type=jnp.float32)
    ffn_back = jnp.dot(d_gate, gate_back.T, preferred_element_type=jnp.float32)
    ffn_back = (ffn_back + jnp.dot(d_up, up_back.T, preferred_element_type=jnp.float32)).astype(
        jnp.bfloat16
    )
    d_normed_ffn = lax.psum(ffn_back, "tensor").astype(jnp.float32)
    grad_rows_ffn, grad_gain_ffn = norm_backward(resid, scale_ffn, gain_second, d_normed_ffn)
    d_resid = upstream.astype(jnp.float32) + grad_rows_ffn
    resid_grad = d_resid.astype(jnp.bfloat16)
    grad_out_proj = jnp.dot(attended.T, resid_grad, preferred_element_type=jnp.float32)
    d_attended = jnp.dot(resid_grad, out_back.T, preferred_element_type=jnp.float32).astype(
        jnp.bfloat16
    )
    d_joined = attention_backward(d_attended, attended, lse, query, keys, values, cosine, sine, SEQ)
    grad_qkv = jnp.dot(normed_attn.T, d_joined, preferred_element_type=jnp.float32)
    attn_back = jnp.dot(d_joined, qkv_back.T, preferred_element_type=jnp.float32).astype(
        jnp.bfloat16
    )
    d_normed_attn = lax.psum(attn_back, "tensor").astype(jnp.float32)
    grad_rows_attn, grad_gain_attn = norm_backward(rows, scale_attn, gain_first, d_normed_attn)
    d_tokens = (d_resid + grad_rows_attn).astype(jnp.bfloat16)
    terms = (grad_qkv, grad_out_proj, grad_gate, grad_up, grad_down, grad_gain_attn, grad_gain_ffn)
    return (output, d_tokens, terms)


def local(tokens, positions, w_qkv, w_out, w_gate, w_up, w_down, gain_attn, gain_ffn, cotangent):
    batch_rows = tokens.shape[0] // MICRO
    dp_count = lax.axis_size("dp")
    totals = (
        jnp.zeros((w_qkv.shape[0] * dp_count, w_qkv.shape[1]), jnp.float32),
        jnp.zeros((w_out.shape[0], w_out.shape[1] * dp_count), jnp.float32),
        jnp.zeros((w_gate.shape[0] * dp_count, w_gate.shape[1]), jnp.float32),
        jnp.zeros((w_up.shape[0] * dp_count, w_up.shape[1]), jnp.float32),
        jnp.zeros((w_down.shape[0], w_down.shape[1] * dp_count), jnp.float32),
        jnp.zeros((gain_attn.shape[0] * dp_count,), jnp.float32),
        jnp.zeros((gain_ffn.shape[0] * dp_count,), jnp.float32),
    )
    outputs = []
    input_grads = []
    for micro in range(MICRO):
        lower = micro * batch_rows
        upper = lower + batch_rows
        forward_set = (
            lax.all_gather(w_qkv, "dp", axis=0, tiled=True),
            lax.all_gather(w_out, "dp", axis=1, tiled=True),
            lax.all_gather(w_gate, "dp", axis=0, tiled=True),
            lax.all_gather(w_up, "dp", axis=0, tiled=True),
            lax.all_gather(w_down, "dp", axis=1, tiled=True),
            lax.all_gather(gain_attn, "dp", axis=0, tiled=True),
            lax.all_gather(gain_ffn, "dp", axis=0, tiled=True),
        )
        backward_set = (
            lax.all_gather(w_qkv, "dp", axis=0, tiled=True),
            lax.all_gather(w_out, "dp", axis=1, tiled=True),
            lax.all_gather(w_gate, "dp", axis=0, tiled=True),
            lax.all_gather(w_up, "dp", axis=0, tiled=True),
            lax.all_gather(w_down, "dp", axis=1, tiled=True),
        )
        output, d_tokens, terms = layer_pass(
            tokens[lower:upper],
            positions[lower:upper],
            cotangent[lower:upper],
            forward_set,
            backward_set,
        )
        outputs.append(output)
        input_grads.append(d_tokens)
        totals = tuple((total + term for total, term in zip(totals, terms)))
    owned = (
        lax.psum_scatter(
            totals[0].astype(jnp.bfloat16), "dp", scatter_dimension=0, tiled=True
        ).astype(jnp.float32),
        lax.psum_scatter(
            totals[1].astype(jnp.bfloat16), "dp", scatter_dimension=1, tiled=True
        ).astype(jnp.float32),
        lax.psum_scatter(
            totals[2].astype(jnp.bfloat16), "dp", scatter_dimension=0, tiled=True
        ).astype(jnp.float32),
        lax.psum_scatter(
            totals[3].astype(jnp.bfloat16), "dp", scatter_dimension=0, tiled=True
        ).astype(jnp.float32),
        lax.psum_scatter(
            totals[4].astype(jnp.bfloat16), "dp", scatter_dimension=1, tiled=True
        ).astype(jnp.float32),
        lax.psum_scatter(
            totals[5].astype(jnp.bfloat16), "dp", scatter_dimension=0, tiled=True
        ).astype(jnp.float32),
        lax.psum_scatter(
            totals[6].astype(jnp.bfloat16), "dp", scatter_dimension=0, tiled=True
        ).astype(jnp.float32),
    )
    return (
        jnp.concatenate(outputs, axis=0),
        jnp.concatenate(input_grads, axis=0),
        owned[0],
        owned[1],
        owned[2],
        owned[3],
        owned[4],
        owned[5],
        owned[6],
    )


def solution(mesh):
    return jax.shard_map(
        local,
        mesh=mesh,
        in_specs=(
            P("dp", None),
            P("dp"),
            P("dp", "tensor"),
            P("tensor", "dp"),
            P("dp", "tensor"),
            P("dp", "tensor"),
            P("tensor", "dp"),
            P("dp"),
            P("dp"),
            P("dp", None),
        ),
        out_specs=(
            P("dp", None),
            P("dp", None),
            P("dp", "tensor"),
            P("tensor", "dp"),
            P("dp", "tensor"),
            P("dp", "tensor"),
            P("tensor", "dp"),
            P("dp"),
            P("dp"),
        ),
        check_vma=False,
    )
```

```python
import functools
import math

import jax
import jax.numpy as jnp
from jax import lax
from jax.experimental import pallas as pl
from jax.experimental.pallas import tpu as pltpu
from jax.sharding import PartitionSpec as P

HEADS = 32
KV_HEADS = 8
HD = 64
SEQ = 256


epsilon = 1e-05
rope_base = 500000.0
masked_score = -1e30


def rotary_tables(positions, head_dim):
    half_dim = head_dim // 2
    exponents = jnp.arange(half_dim, dtype=jnp.float32) * (2.0 / head_dim)
    frequency = jnp.exp(-exponents * math.log(rope_base))
    angles = positions.astype(jnp.float32)[:, None] * frequency[None, :]
    angles = jnp.concatenate([angles, angles], axis=1)
    return (jnp.cos(angles), jnp.sin(angles))


def half_turn(values):
    half_dim = values.shape[-1] // 2
    return jnp.concatenate([-values[..., half_dim:], values[..., :half_dim]], axis=-1)


def back_turn(values):
    half_dim = values.shape[-1] // 2
    return jnp.concatenate([values[..., half_dim:], -values[..., :half_dim]], axis=-1)


def norm_forward(rows, gain):
    scale = lax.rsqrt(jnp.mean(rows * rows, axis=-1, keepdims=True) + epsilon)
    return (scale, (rows * scale * gain).astype(jnp.bfloat16))


def norm_backward(rows, scale, gain, upstream):
    weighted = upstream * gain
    inner = jnp.mean(weighted * rows, axis=-1, keepdims=True)
    grad_rows = scale * weighted - rows * (scale * scale * scale) * inner
    grad_gain = jnp.sum(upstream * rows * scale, axis=0)
    return (grad_rows, grad_gain)


def causal_mask(length):
    row_index = lax.broadcasted_iota(jnp.int32, (length, length), 0)
    col_index = lax.broadcasted_iota(jnp.int32, (length, length), 1)
    return row_index >= col_index


def attention_forward(joined, cosine, sine, groups, head_dim, length):
    count = joined.shape[0]
    kv_local = joined.shape[1] // ((groups + 2) * head_dim)
    seqs = count // length
    shaped = joined.reshape(seqs, length, kv_local, groups + 2, head_dim)
    cos_five = cosine.reshape(seqs, length, 1, 1, head_dim)
    sin_five = sine.reshape(seqs, length, 1, 1, head_dim)
    turned = shaped[:, :, :, : groups + 1]
    rotated = turned * cos_five + half_turn(turned) * sin_five
    query = rotated[:, :, :, :groups].astype(jnp.bfloat16)
    keys = rotated[:, :, :, groups].astype(jnp.bfloat16)
    values = shaped[:, :, :, groups + 1].astype(jnp.bfloat16)
    scores = jnp.einsum("sikgd,sjkd->skgij", query, keys, preferred_element_type=jnp.float32) * (
        1.0 / math.sqrt(head_dim)
    )
    scores = jnp.where(causal_mask(length), scores, masked_score)
    peak = jnp.max(scores, axis=-1, keepdims=True)
    lse = peak[..., 0] + jnp.log(jnp.sum(jnp.exp(scores - peak), axis=-1))
    probs = jnp.exp(scores - lse[..., None]).astype(jnp.bfloat16)
    attended = jnp.einsum("skgij,sjkd->sikgd", probs, values, preferred_element_type=jnp.float32)
    attended = attended.astype(jnp.bfloat16).reshape(count, kv_local * groups * head_dim)
    return (attended, lse, query, keys, values)


def attention_backward(d_attended, attended, lse, query, keys, values, cosine, sine, length):
    seqs, _, kv_local, groups, head_dim = query.shape
    count = seqs * length
    scores = jnp.einsum("sikgd,sjkd->skgij", query, keys, preferred_element_type=jnp.float32) * (
        1.0 / math.sqrt(head_dim)
    )
    scores = jnp.where(causal_mask(length), scores, masked_score)
    probs = jnp.exp(scores - lse[..., None])
    probs_low = probs.astype(jnp.bfloat16)
    d_five = d_attended.reshape(seqs, length, kv_local, groups, head_dim)
    att_five = attended.reshape(seqs, length, kv_local, groups, head_dim)
    d_values = jnp.einsum(
        "skgij,sikgd->sjkd", probs_low, d_five, preferred_element_type=jnp.float32
    )
    d_probs = jnp.einsum("sikgd,sjkd->skgij", d_five, values, preferred_element_type=jnp.float32)
    delta = jnp.sum(d_five.astype(jnp.float32) * att_five.astype(jnp.float32), axis=-1)
    delta = jnp.transpose(delta, (0, 2, 3, 1))
    d_scores = (probs * (d_probs - delta[..., None]) * (1.0 / math.sqrt(head_dim))).astype(
        jnp.bfloat16
    )
    d_query = jnp.einsum("skgij,sjkd->sikgd", d_scores, keys, preferred_element_type=jnp.float32)
    d_keys = jnp.einsum("skgij,sikgd->sjkd", d_scores, query, preferred_element_type=jnp.float32)
    cos_five = cosine.reshape(seqs, length, 1, 1, head_dim)
    sin_five = sine.reshape(seqs, length, 1, 1, head_dim)
    d_query = d_query * cos_five + back_turn(d_query * sin_five)
    d_keys = d_keys * cos_five[:, :, :, 0] + back_turn(d_keys * sin_five[:, :, :, 0])
    d_joined = jnp.concatenate([d_query, d_keys[:, :, :, None], d_values[:, :, :, None]], axis=3)
    return d_joined.astype(jnp.bfloat16).reshape(count, kv_local * (groups + 2) * head_dim)


MESH = pl.DeviceIdType.MESH
HBM = pl.BlockSpec(memory_space=pl.ANY)
VMEM = pl.BlockSpec(memory_space=pltpu.VMEM)
DMA = pltpu.SemaphoreType.DMA
bf16 = jnp.bfloat16
f32 = jnp.float32
NT_DIMS = (((1,), (1,)), ((), ()))


def remote(src, dst, send, recv, device):
    return pltpu.make_async_remote_copy(
        src_ref=src, dst_ref=dst, send_sem=send, recv_sem=recv, device_id=device, device_id_type=MESH
    )


def mult(value, factor):
    return pl.multiple_of(value * factor, factor)


def ffn_kernel(
    sizes,
    part,
    tok,
    cot,
    packed,
    gain,
    out,
    rgrad,
    dres,
    grads,
    ggain,
    w,
    ru,
    rd,
    x,
    ct,
    accp,
    accb,
    ht,
    dgt,
    dut,
    resid,
    p1,
    p2,
    sb,
    sbr_b,
    sbr_p,
    rsb,
    own_sem,
    sib_sem,
    ag_send,
    ag_recv,
    rs_send,
    rs_recv,
    credit,
    g_sem,
    loc_sem,
    cot_sem,
    ps_send,
    ps_recv,
    x_send,
    x_recv,
    xs_send,
    xs_recv,
    sb_send,
    sb_recv,
    gat_send,
    gat_recv,
):
    nz, nt, nch, tokens, width, hc = sizes
    ts = tokens // nt
    dp_count = 2 * nz
    d = lax.axis_index("dp")
    t = lax.axis_index("tensor")
    z = d // 2
    c = d % 2
    sib = (2 * z + 1 - c, t)
    above = (d + 2, t)
    below = (d - 2, t)

    def peer(k):
        return lax.rem(t + 1 + k, nt)

    def peer_dev(k):
        return (d, peer(k))

    barrier = pltpu.get_barrier_semaphore()
    for k in range(nt - 1):
        pl.semaphore_signal(barrier, inc=1, device_id=peer_dev(k), device_id_type=MESH)
    pl.semaphore_signal(barrier, inc=1, device_id=sib, device_id_type=MESH)

    @pl.when(z > 0)
    def _():
        pl.semaphore_signal(barrier, inc=1, device_id=below, device_id_type=MESH)

    @pl.when(z < nz - 1)
    def _():
        pl.semaphore_signal(barrier, inc=1, device_id=above, device_id_type=MESH)

    neighbours = jnp.where(z > 0, 1, 0) + jnp.where(z < nz - 1, 1, 0)
    pl.semaphore_wait(barrier, nt + neighbours)

    def rows_of(index):
        return pl.ds(mult(index, ts), ts)

    def half_rows(core, index):
        return pl.ds(pl.multiple_of(core * tokens + index * ts, ts), ts)

    def part_copy(k):
        to = peer(k)
        return remote(
            part.at[rows_of(to)], p1.at[t], ps_send.at[0, k], ps_recv.at[0, k], (d, to)
        )

    def part_wait(k):
        frm = lax.rem(t - 1 - k + nt, nt)
        return remote(part.at[rows_of(t)], p1.at[frm], ps_send.at[0, k], ps_recv.at[0, k], (d, frm))

    for k in range(nt - 1):
        part_copy(k).start()
    own_part = pltpu.make_async_copy(part.at[rows_of(t)], p1.at[t], loc_sem.at[0])
    own_part.start()
    tok_copy = pltpu.make_async_copy(tok.at[rows_of(t)], rsb.at[0], loc_sem.at[1])
    tok_copy.start()

    def own_copy(i):
        return pltpu.make_async_copy(packed.at[i, c], w.at[i, :, z, c], own_sem.at[i])

    def sib_copy(i):
        return remote(packed.at[i, 1 - c], w.at[i, :, z, c], sib_sem.at[0, i], sib_sem.at[1, i], sib)

    def sib_wait(i):
        return remote(packed.at[i, c], w.at[i, :, z, 1 - c], sib_sem.at[0, i], sib_sem.at[1, i], sib)

    for i in range(nch):
        own_copy(i).start()
        sib_copy(i).start()
    cot_own = pltpu.make_async_copy(cot, ct.at[pl.ds(mult(c, tokens), tokens)], cot_sem.at[0])
    cot_sib = remote(cot, ct.at[pl.ds(mult(c, tokens), tokens)], cot_sem.at[1], cot_sem.at[2], sib)
    cot_in = remote(cot, ct.at[pl.ds(mult(1 - c, tokens), tokens)], cot_sem.at[1], cot_sem.at[2], sib)
    cot_own.start()
    cot_sib.start()

    def ag_up(i, s):
        unit = w.at[i, :, z - s]
        return remote(unit, unit, ag_send.at[i, 0, s], ag_recv.at[i, 0, s], above)

    def ag_down(i, s):
        unit = w.at[i, :, z + s]
        return remote(unit, unit, ag_send.at[i, 1, s], ag_recv.at[i, 1, s], below)

    def ag_tick(i, s):
        if s == 0:
            own_copy(i).wait()
            sib_wait(i).wait_recv()
        else:

            @pl.when(z - s >= 0)
            def _():
                unit = w.at[i, :, z - s]
                remote(unit, unit, ag_send.at[i, 0, s - 1], ag_recv.at[i, 0, s - 1], below).wait_recv()

        if s < nz - 1:

            @pl.when((z - s >= 0) & (z < nz - 1))
            def _():
                ag_up(i, s).start()

        if s > 0:

            @pl.when(z + s <= nz - 1)
            def _():
                unit = w.at[i, :, z + s]
                remote(unit, unit, ag_send.at[i, 1, s - 1], ag_recv.at[i, 1, s - 1], above).wait_recv()

        if s < nz - 1:

            @pl.when((z + s <= nz - 1) & (z > 0))
            def _():
                ag_down(i, s).start()

    def ag_finish(i):
        for s in range(nz - 1):

            @pl.when((z - s >= 0) & (z < nz - 1))
            def _():
                ag_up(i, s).wait_send()

            @pl.when((z + s <= nz - 1) & (z > 0))
            def _():
                ag_down(i, s).wait_send()

    def rs_up(i, tau):
        return remote(
            w.at[i, :, nz - 1 + z - tau], ru.at[tau], rs_send.at[0, tau], rs_recv.at[0, tau], above
        )

    def rs_down(i, tau):
        return remote(
            w.at[i, :, tau - (nz - 1 - z)], rd.at[tau], rs_send.at[1, tau], rs_recv.at[1, tau], below
        )

    def add_unit(i, owner, got):
        for kind in range(3):
            for core in range(2):
                a = w[i, kind, owner, core].astype(f32)
                b = got[kind, core].astype(f32)
                w[i, kind, owner, core] = (a + b).astype(bf16)

    def rs_tick(i, tau):
        if tau > 0:

            @pl.when((z <= tau) & (z > 0))
            def _():
                owner = nz - 1 + z - tau
                remote(
                    w.at[i, :, owner], ru.at[tau - 1], rs_send.at[0, tau - 1], rs_recv.at[0, tau - 1], below
                ).wait_recv()
                add_unit(i, owner, ru.at[tau - 1])

        if tau < nz - 1:

            @pl.when(z <= tau)
            def _():
                rs_up(i, tau).start()

        if tau > 0:

            @pl.when((tau >= nz - 1 - z) & (z < nz - 1))
            def _():
                owner = tau - (nz - 1 - z)
                remote(
                    w.at[i, :, owner], rd.at[tau - 1], rs_send.at[1, tau - 1], rs_recv.at[1, tau - 1], above
                ).wait_recv()
                add_unit(i, owner, rd.at[tau - 1])

        if tau < nz - 1:

            @pl.when(tau >= nz - 1 - z)
            def _():
                rs_down(i, tau).start()

    def grad_own(i):
        return pltpu.make_async_copy(w.at[i, :, z, c], grads.at[i, c], g_sem.at[0, i])

    def grad_sib(i):
        return remote(w.at[i, :, z, 1 - c], grads.at[i, c], g_sem.at[1, i], g_sem.at[2, i], sib)

    def grad_in(i):
        return remote(w.at[i, :, z, c], grads.at[i, 1 - c], g_sem.at[1, i], g_sem.at[2, i], sib)

    def rs_finish(i, last):
        grad_own(i).start()
        grad_sib(i).start()
        for tau in range(nz - 1):

            @pl.when(z <= tau)
            def _():
                rs_up(i, tau).wait_send()

            @pl.when(tau >= nz - 1 - z)
            def _():
                rs_down(i, tau).wait_send()

        if not last:
            @pl.when(z > 0)
            def _():
                pl.semaphore_signal(credit.at[0], inc=1, device_id=below, device_id_type=MESH)

            @pl.when(z < nz - 1)
            def _():
                pl.semaphore_signal(credit.at[1], inc=1, device_id=above, device_id_type=MESH)

    def rs_credit():
        @pl.when(z < nz - 1)
        def _():
            pl.semaphore_wait(credit.at[0], 1)

        @pl.when(z > 0)
        def _():
            pl.semaphore_wait(credit.at[1], 1)

    tile = min(256, 2 * tokens)

    def compute(i):
        def rows_step(m, carry):
            rows = pl.ds(mult(m, tile), tile)
            xm = x[rows, :]
            wg = w[i, 0].reshape(width, hc)
            wu = w[i, 1].reshape(width, hc)
            gate = jnp.dot(xm, wg, preferred_element_type=f32)
            up = jnp.dot(xm, wu, preferred_element_type=f32)
            dh = jnp.zeros((tile, hc), f32)
            for k in range(dp_count):
                dh = dh + lax.dot_general(
                    ct[rows, k * hc : (k + 1) * hc],
                    w[i, 2, k // 2, k % 2],
                    NT_DIMS,
                    preferred_element_type=f32,
                )
            sig = jax.nn.sigmoid(gate)
            act = gate * sig
            hidden = (act * up).astype(bf16)
            d_up = (dh * act).astype(bf16)
            d_gate = (dh * up * sig * (1.0 + gate * (1.0 - sig))).astype(bf16)
            ht[:, rows] = hidden.T
            dgt[:, rows] = d_gate.T
            dut[:, rows] = d_up.T
            for k in range(dp_count):
                cols = slice(k * hc, (k + 1) * hc)
                accp[rows, cols] += jnp.dot(hidden, w[i, 2, k // 2, k % 2], preferred_element_type=f32)
                accb[rows, cols] += lax.dot_general(
                    d_gate, w[i, 0, k // 2, k % 2], NT_DIMS, preferred_element_type=f32
                ) + lax.dot_general(d_up, w[i, 1, k // 2, k % 2], NT_DIMS, preferred_element_type=f32)
            return carry

        lax.fori_loop(0, 2 * tokens // tile, rows_step, 0)

        def cols_step(k, carry):
            cols = pl.ds(mult(k, hc), hc)
            xs = x[:, cols]
            chip, core = k // 2, k % 2
            w[i, 0, chip, core] = jnp.dot(dgt[...], xs, preferred_element_type=f32).astype(bf16)
            w[i, 1, chip, core] = jnp.dot(dut[...], xs, preferred_element_type=f32).astype(bf16)
            w[i, 2, chip, core] = jnp.dot(ht[...], ct[:, cols], preferred_element_type=f32).astype(bf16)
            return carry

        lax.fori_loop(0, dp_count, cols_step, 0)

    ag_tick(0, 0)
    tok_copy.wait()
    own_part.wait()
    for k in range(nt - 1):
        part_wait(k).wait_recv()
    total = rsb[0].astype(f32)
    mix = p1[0].astype(f32)
    for k in range(1, nt):
        mix = mix + p1[k].astype(f32)
    total = total + mix
    resid[...] = total
    scale = lax.rsqrt(jnp.mean(total * total, axis=-1, keepdims=True) + epsilon)
    mine = half_rows(c, t)
    x[mine, :] = (total * scale * gain[...]).astype(bf16)

    def x_copy(k):
        return remote(x.at[mine], x.at[mine], x_send.at[k], x_recv.at[k], peer_dev(k))

    def x_wait(k):
        frm = lax.rem(t - 1 - k + nt, nt)
        rows = half_rows(c, frm)
        return remote(x.at[rows], x.at[rows], x_send.at[k], x_recv.at[k], (d, frm))

    def xs_copy(k):
        frm = lax.rem(t - k + nt, nt)
        rows = half_rows(c, frm)
        return remote(x.at[rows], x.at[rows], xs_send.at[k], xs_recv.at[k], sib)

    def xs_wait(k):
        frm = lax.rem(t - k + nt, nt)
        rows = half_rows(1 - c, frm)
        return remote(x.at[rows], x.at[rows], xs_send.at[k], xs_recv.at[k], sib)

    for k in range(nt - 1):
        x_copy(k).start()
    xs_copy(0).start()
    accp[...] = jnp.zeros_like(accp)
    accb[...] = jnp.zeros_like(accb)
    if nz > 1:
        ag_tick(0, 1)
    for k in range(nt - 1):
        x_wait(k).wait_recv()
        xs_copy(k + 1).start()
    for s in range(2, nz):
        ag_tick(0, s)
    ag_finish(0)
    cot_own.wait()
    cot_in.wait_recv()
    for k in range(nt):
        xs_wait(k).wait_recv()

    for i in range(nch):
        more = i + 1 < nch
        if more:
            ag_tick(i + 1, 0)
        compute(i)
        if i > 0:
            rs_credit()
        rs_tick(i, 0)
        if more:
            for s in range(1, nz):
                ag_tick(i + 1, s)
                rs_tick(i, s)
            ag_finish(i + 1)
            rs_finish(i, False)

    def sib_block(acc, got, base, k):
        rows = peer(k)
        sb[k] = acc[half_rows(1 - c, rows), :].astype(bf16)
        return remote(sb.at[k], got.at[k], sb_send.at[base + k], sb_recv.at[base + k], sib)

    def sib_in(got, base, k):
        return remote(sb.at[k], got.at[k], sb_send.at[base + k], sb_recv.at[base + k], sib)

    def block_copy(land, which, k):
        return remote(
            rsb.at[k], land.at[t], ps_send.at[which, k], ps_recv.at[which, k], peer_dev(k)
        )

    def block_wait(land, which, k):
        frm = lax.rem(t - 1 - k + nt, nt)
        return remote(rsb.at[k], land.at[frm], ps_send.at[which, k], ps_recv.at[which, k], (d, frm))

    def gather_copy(ref, which, k):
        return remote(
            rsb.at[nt - 1],
            ref.at[rows_of(t)],
            gat_send.at[which, k],
            gat_recv.at[which, k],
            peer_dev(k),
        )

    def gather_wait(ref, which, k):
        frm = lax.rem(t - 1 - k + nt, nt)
        return remote(
            rsb.at[nt - 1], ref.at[rows_of(frm)], gat_send.at[which, k], gat_recv.at[which, k], (d, frm)
        )

    last = nch - 1
    for k in range(nt - 1):
        part_copy(k).wait_send()
    for k in range(nt):
        sib_block(accb, sbr_b, 0, k).start()
    for k in range(nt):
        sib_in(sbr_b, 0, k).wait_recv()
        summed = accb[half_rows(c, peer(k)), :] + sbr_b[k].astype(f32)
        if k < nt - 1:
            rsb[k] = summed.astype(bf16)
            block_copy(p2, 1, k).start()
        else:
            p2[t] = summed.astype(bf16)
    if nz > 1:
        rs_tick(last, 1)
    for k in range(nt):
        sib_in(sbr_b, 0, k).wait_send()
    for k in range(nt):
        sib_block(accp, sbr_p, nt, k).start()
    for k in range(nt - 1):
        block_wait(p2, 1, k).wait_recv()
    upstream = p2[0].astype(f32)
    for k in range(1, nt):
        upstream = upstream + p2[k].astype(f32)
    rows = resid[...]
    scale = lax.rsqrt(jnp.mean(rows * rows, axis=-1, keepdims=True) + epsilon)
    ggain[...] = jnp.sum(upstream * rows * scale, axis=0, keepdims=True)
    weighted = upstream * gain[...]
    inner = jnp.mean(weighted * rows, axis=-1, keepdims=True)
    grad_rows = scale * weighted - rows * (scale * scale * scale) * inner
    d_resid = ct[mine, :].astype(f32) + grad_rows
    dres[...] = d_resid
    rsb[nt - 1] = d_resid.astype(bf16)
    for k in range(nt - 1):
        gather_copy(rgrad, 0, k).start()
    own_rg = pltpu.make_async_copy(rsb.at[nt - 1], rgrad.at[rows_of(t)], loc_sem.at[0])
    own_rg.start()
    for s in range(2, nz):
        rs_tick(last, s)
    for k in range(nt - 1):
        block_copy(p2, 1, k).wait_send()
    for k in range(nt):
        sib_in(sbr_p, nt, k).wait_recv()
        summed = accp[half_rows(c, peer(k)), :] + sbr_p[k].astype(f32)
        if k < nt - 1:
            rsb[k] = summed.astype(bf16)
            block_copy(p1, 2, k).start()
        else:
            p1[t] = summed.astype(bf16)
    rs_finish(last, True)
    for k in range(nt - 1):
        gather_copy(rgrad, 0, k).wait_send()
    own_rg.wait()
    for k in range(nt - 1):
        block_wait(p1, 2, k).wait_recv()
    total = p1[0].astype(f32)
    for k in range(1, nt):
        total = total + p1[k].astype(f32)
    rsb[nt - 1] = (resid[...] + total).astype(bf16)
    for k in range(nt - 1):
        gather_copy(out, 1, k).start()
    own_out = pltpu.make_async_copy(rsb.at[nt - 1], out.at[rows_of(t)], loc_sem.at[1])
    own_out.start()

    for k in range(nt - 1):
        x_copy(k).wait_send()
        block_copy(p1, 2, k).wait_send()
        gather_copy(out, 1, k).wait_send()
        gather_wait(rgrad, 0, k).wait_recv()
        gather_wait(out, 1, k).wait_recv()
    for k in range(nt):
        xs_copy(k).wait_send()
        sib_in(sbr_p, nt, k).wait_send()
    own_out.wait()
    cot_sib.wait_send()
    for i in range(nch):
        sib_copy(i).wait_send()
        grad_own(i).wait()
        grad_sib(i).wait_send()
        grad_in(i).wait_recv()


def ffn_block(attn_partial, tokens, cotangent, packed, gain, nz, nt):
    count, width = tokens.shape
    nch, _, _, hc, _ = packed.shape
    ts = count // nt
    sizes = (nz, nt, nch, count, width, hc)
    unit = (3, nz, 2, hc, hc)
    recv = (nz - 1, 3, 2, hc, hc)
    return pl.pallas_call(
        functools.partial(ffn_kernel, sizes),
        out_shape=(
            jax.ShapeDtypeStruct((count, width), bf16),
            jax.ShapeDtypeStruct((count, width), bf16),
            jax.ShapeDtypeStruct((ts, width), f32),
            jax.ShapeDtypeStruct((nch, 2, 3, hc, hc), bf16),
            jax.ShapeDtypeStruct((1, width), f32),
        ),
        in_specs=[HBM, HBM, HBM, HBM, VMEM],
        out_specs=(HBM, HBM, VMEM, HBM, VMEM),
        scratch_shapes=[
            pltpu.VMEM((nch,) + unit, bf16),
            pltpu.VMEM(recv, bf16),
            pltpu.VMEM(recv, bf16),
            pltpu.VMEM((2 * count, width), bf16),
            pltpu.VMEM((2 * count, width), bf16),
            pltpu.VMEM((2 * count, width), f32),
            pltpu.VMEM((2 * count, width), f32),
            pltpu.VMEM((hc, 2 * count), bf16),
            pltpu.VMEM((hc, 2 * count), bf16),
            pltpu.VMEM((hc, 2 * count), bf16),
            pltpu.VMEM((ts, width), f32),
            pltpu.VMEM((nt, ts, width), bf16),
            pltpu.VMEM((nt, ts, width), bf16),
            pltpu.VMEM((nt, ts, width), bf16),
            pltpu.VMEM((nt, ts, width), bf16),
            pltpu.VMEM((nt, ts, width), bf16),
            pltpu.VMEM((nt, ts, width), bf16),
            DMA((nch,)),
            DMA((2, nch)),
            DMA((nch, 2, nz)),
            DMA((nch, 2, nz)),
            DMA((2, nz)),
            DMA((2, nz)),
            pltpu.SemaphoreType.REGULAR((2,)),
            DMA((3, nch)),
            DMA((2,)),
            DMA((3,)),
            DMA((3, nt)),
            DMA((3, nt)),
            DMA((nt,)),
            DMA((nt,)),
            DMA((nt,)),
            DMA((nt,)),
            DMA((2 * nt,)),
            DMA((2 * nt,)),
            DMA((2, nt)),
            DMA((2, nt)),
        ],
        compiler_params=pltpu.CompilerParams(
            collective_id=0, has_side_effects=True, vmem_limit_bytes=61 * 2**20
        ),
        name="ffn",
    )(attn_partial, tokens, cotangent, packed, gain)


def tail_kernel(
    sizes, part, tok, dres, gain, dtok, ggain, land, tbuf, obuf, loc_sem, ps_send, ps_recv, gat_send, gat_recv
):
    nt, tokens, width = sizes
    ts = tokens // nt
    d = lax.axis_index("dp")
    t = lax.axis_index("tensor")

    def peer_dev(k):
        return (d, lax.rem(t + 1 + k, nt))

    def from_dev(k):
        return lax.rem(t - 1 - k + nt, nt)

    barrier = pltpu.get_barrier_semaphore()
    for k in range(nt - 1):
        pl.semaphore_signal(barrier, inc=1, device_id=peer_dev(k), device_id_type=MESH)
    pl.semaphore_wait(barrier, nt - 1)

    def rows_of(index):
        return pl.ds(mult(index, ts), ts)

    def part_copy(k):
        to = lax.rem(t + 1 + k, nt)
        return remote(part.at[rows_of(to)], land.at[t], ps_send.at[k], ps_recv.at[k], (d, to))

    def part_wait(k):
        frm = from_dev(k)
        return remote(part.at[rows_of(t)], land.at[frm], ps_send.at[k], ps_recv.at[k], (d, frm))

    def gather_copy(k):
        return remote(obuf, dtok.at[rows_of(t)], gat_send.at[k], gat_recv.at[k], peer_dev(k))

    def gather_wait(k):
        frm = from_dev(k)
        return remote(obuf, dtok.at[rows_of(frm)], gat_send.at[k], gat_recv.at[k], (d, frm))

    for k in range(nt - 1):
        part_copy(k).start()
    own = pltpu.make_async_copy(part.at[rows_of(t)], land.at[t], loc_sem.at[0])
    own.start()
    tok_copy = pltpu.make_async_copy(tok.at[rows_of(t)], tbuf, loc_sem.at[1])
    tok_copy.start()
    tok_copy.wait()
    rows = tbuf[...].astype(f32)
    scale = lax.rsqrt(jnp.mean(rows * rows, axis=-1, keepdims=True) + epsilon)
    own.wait()
    for k in range(nt - 1):
        part_wait(k).wait_recv()
    upstream = land[0].astype(f32)
    for k in range(1, nt):
        upstream = upstream + land[k].astype(f32)
    ggain[...] = jnp.sum(upstream * rows * scale, axis=0, keepdims=True)
    weighted = upstream * gain[...]
    inner = jnp.mean(weighted * rows, axis=-1, keepdims=True)
    grad_rows = scale * weighted - rows * (scale * scale * scale) * inner
    obuf[...] = (dres[...] + grad_rows).astype(bf16)
    for k in range(nt - 1):
        gather_copy(k).start()
    put = pltpu.make_async_copy(obuf, dtok.at[rows_of(t)], loc_sem.at[0])
    put.start()
    for k in range(nt - 1):
        part_copy(k).wait_send()
        gather_copy(k).wait_send()
        gather_wait(k).wait_recv()
    put.wait()


def tail_block(attn_back, tokens, dres, gain, nt):
    count, width = tokens.shape
    ts = count // nt
    return pl.pallas_call(
        functools.partial(tail_kernel, (nt, count, width)),
        out_shape=(
            jax.ShapeDtypeStruct((count, width), bf16),
            jax.ShapeDtypeStruct((1, width), f32),
        ),
        in_specs=[HBM, HBM, VMEM, VMEM],
        out_specs=(HBM, VMEM),
        scratch_shapes=[
            pltpu.VMEM((nt, ts, width), bf16),
            pltpu.VMEM((ts, width), bf16),
            pltpu.VMEM((ts, width), bf16),
            DMA((2,)),
            DMA((nt,)),
            DMA((nt,)),
            DMA((nt,)),
            DMA((nt,)),
        ],
        compiler_params=pltpu.CompilerParams(
            collective_id=1, has_side_effects=True, vmem_limit_bytes=24 * 2**20
        ),
        name="tail",
    )(attn_back, tokens, dres, gain)


def local(tokens, positions, w_qkv, w_out, w_gate, w_up, w_down, gain_attn, gain_ffn, cotangent):
    dp_count = lax.axis_size("dp")
    nt = lax.axis_size("tensor")
    nz = dp_count // 2
    shard, hid = w_gate.shape
    nch = hid // (2 * shard)
    groups = HEADS // KV_HEADS

    qkv_full = lax.all_gather(w_qkv, "dp", axis=0, tiled=True)
    out_full = lax.all_gather(w_out, "dp", axis=1, tiled=True)
    gains = lax.all_gather(jnp.stack([gain_attn, gain_ffn]), "dp", axis=1, tiled=True).astype(f32)
    gain_first, gain_second = gains[:1], gains[1:]

    packed = jnp.stack(
        [
            w_gate.reshape(shard, nch, 2, shard).transpose(1, 2, 0, 3),
            w_up.reshape(shard, nch, 2, shard).transpose(1, 2, 0, 3),
            w_down.reshape(nch, 2, shard, shard),
        ],
        axis=2,
    )

    rows = tokens.astype(f32)
    scale_attn, normed_attn = norm_forward(rows, gain_first)
    joined = jnp.dot(normed_attn, qkv_full, preferred_element_type=f32)
    cosine, sine = rotary_tables(positions, HD)
    attended, lse, query, keys, values = attention_forward(joined, cosine, sine, groups, HD, SEQ)
    attn_partial = jnp.dot(attended, out_full, preferred_element_type=f32).astype(bf16)

    output, resid_grad, dres, grads, gain_ffn_part = ffn_block(
        attn_partial, tokens, cotangent, packed, gain_second, nz, nt
    )

    grad_out_proj = jnp.dot(attended.T, resid_grad, preferred_element_type=f32).astype(bf16)
    grad_out_proj = lax.psum_scatter(grad_out_proj, "dp", scatter_dimension=1, tiled=True)
    d_attended = jnp.dot(resid_grad, out_full.T, preferred_element_type=f32).astype(bf16)
    d_joined = attention_backward(d_attended, attended, lse, query, keys, values, cosine, sine, SEQ)
    grad_qkv = jnp.dot(normed_attn.T, d_joined, preferred_element_type=f32).astype(bf16)
    grad_qkv = lax.psum_scatter(grad_qkv, "dp", scatter_dimension=0, tiled=True)
    attn_back = jnp.dot(d_joined, qkv_full.T, preferred_element_type=f32).astype(bf16)
    d_tokens, gain_attn_part = tail_block(attn_back, tokens, dres, gain_first, nt)

    gain_grads = lax.psum(jnp.concatenate([gain_attn_part, gain_ffn_part]), ("dp", "tensor"))
    mine = lax.axis_index("dp") * shard
    gain_grads = lax.dynamic_slice(gain_grads, (0, mine), (2, shard))

    grads = grads.astype(f32)
    grad_gate = grads[:, :, 0].transpose(3, 0, 1, 2).reshape(shard, hid)
    grad_up = grads[:, :, 1].transpose(3, 0, 1, 2).reshape(shard, hid)
    grad_down = grads[:, :, 2].reshape(hid, shard)
    return (
        output,
        d_tokens,
        grad_qkv.astype(f32),
        grad_out_proj.astype(f32),
        grad_gate,
        grad_up,
        grad_down,
        gain_grads[0],
        gain_grads[1],
    )


def solution(mesh):
    return jax.shard_map(
        local,
        mesh=mesh,
        in_specs=(
            P("dp", None),
            P("dp"),
            P("dp", "tensor"),
            P("tensor", "dp"),
            P("dp", "tensor"),
            P("dp", "tensor"),
            P("tensor", "dp"),
            P("dp"),
            P("dp"),
            P("dp", None),
        ),
        out_specs=(
            P("dp", None),
            P("dp", None),
            P("dp", "tensor"),
            P("tensor", "dp"),
            P("dp", "tensor"),
            P("dp", "tensor"),
            P("tensor", "dp"),
            P("dp"),
            P("dp"),
        ),
        check_vma=False,
    )
```

```python
import functools
import math

import jax
import jax.numpy as jnp
from jax import lax
from jax.experimental import pallas as pl
from jax.experimental.pallas import tpu as pltpu
from jax.sharding import PartitionSpec as P

HEADS = 32
KV_HEADS = 8
HD = 64
SEQ = 256
GROUPS = HEADS // KV_HEADS
LANES = 128

epsilon = 1e-05
rope_base = 500000.0
masked_score = -1e30

MESH = pl.DeviceIdType.MESH
HBM = pl.BlockSpec(memory_space=pl.ANY)
VMEM = pl.BlockSpec(memory_space=pltpu.VMEM)
bf16 = jnp.bfloat16
f32 = jnp.float32
NT_DIMS = (((1,), (1,)), ((), ()))


def rotary_tables(positions):
    half = HD // 2
    exponents = jnp.arange(half, dtype=f32) * (2.0 / HD)
    frequency = jnp.exp(-exponents * math.log(rope_base))
    angles = positions.astype(f32)[:, None] * frequency[None, :]
    cosine, sine = jnp.cos(angles), jnp.sin(angles)
    reps = LANES // HD
    return (
        jnp.concatenate([cosine, cosine] * reps, axis=1),
        jnp.concatenate([-sine, sine] * reps, axis=1),
    )


def remote(src, dst, send, recv, device):
    return pltpu.make_async_remote_copy(
        src_ref=src, dst_ref=dst, send_sem=send, recv_sem=recv, device_id=device, device_id_type=MESH
    )


def mult(value, factor):
    return pl.multiple_of(value * factor, factor)


def dot(a, b):
    return jnp.dot(a, b, preferred_element_type=f32)


def dot_nt(a, b):
    return lax.dot_general(a, b, NT_DIMS, preferred_element_type=f32)


class Sems:
    def __init__(self):
        self.count = 0
        self.ref = None

    def take(self, *dims):
        base = self.count
        self.count += math.prod(dims)

        def at(*index):
            flat = 0
            for size, place in zip(dims, index):
                flat = flat * size + place
            return self.ref.at[base + flat]

        return at


def semaphores(nz, nt, nch):
    s = Sems()
    names = {
        "own": s.take(nch),
        "sib_s": s.take(nch),
        "sib_r": s.take(nch),
        "ag_s": s.take(nch, 2, nz),
        "ag_r": s.take(nch, 2, nz),
        "qown": s.take(2),
        "qa_s": s.take(2, 2, nz),
        "qa_r": s.take(2, 2, nz),
        "qs_s": s.take(2, nz),
        "qs_r": s.take(2, nz),
        "rs_s": s.take(2, nz),
        "rs_r": s.take(2, nz),
        "as_s": s.take(3),
        "as_r": s.take(3),
        "ar_s": s.take(3, 2, nz),
        "ar_r": s.take(3, 2, nz),
        "fin_s": s.take(nch),
        "fin_r": s.take(nch),
        "put": s.take(8),
        "cot": s.take(3),
        "tok": s.take(3),
        "ps_s": s.take(4, nt),
        "ps_r": s.take(4, nt),
        "x_s": s.take(nt),
        "x_r": s.take(nt),
        "xs_s": s.take(nt),
        "xs_r": s.take(nt),
        "sb_s": s.take(2, nt),
        "sb_r": s.take(2, nt),
        "ga_s": s.take(3, nt),
        "ga_r": s.take(3, nt),
        "gg_s": s.take(nt),
        "gg_r": s.take(nt),
        "loc": s.take(4),
    }
    return s, names


def layer_kernel(
    sizes,
    tok,
    cot,
    packed,
    packed_attn,
    packed_gain,
    cosine,
    sine,
    out,
    dtok,
    g_qkv,
    g_out,
    g_gate,
    g_up,
    g_down,
    g_gains,
    w,
    ru,
    rd,
    x,
    ct,
    accp,
    accb,
    ht,
    dgt,
    dut,
    resid,
    p1,
    p2,
    sbr_b,
    sbr_p,
    rsb,
    aw,
    qkvb,
    att,
    datt,
    fs,
    st,
    gw,
    gv,
    gg,
    gsib,
    gru,
    grd,
    gt,
    sem_ref,
    credit,
):
    nz, nt, nch, tokens, width, hc = sizes
    sems, S = semaphores(nz, nt, nch)
    sems.ref = sem_ref
    ts = tokens // nt
    dps = 2 * nz
    d = lax.axis_index("dp")
    t = lax.axis_index("tensor")
    z = d // 2
    c = d % 2
    sib = (2 * z + 1 - c, t)
    above = (d + 2, t)
    below = (d - 2, t)
    has_above = z < nz - 1
    has_below = z > 0
    seqs = tokens // SEQ
    kv_local = aw_cols(hc) // ((GROUPS + 2) * HD)
    head_cols = (GROUPS + 2) * HD

    def peer(k):
        return lax.rem(t + 1 + k, nt)

    def source(k):
        return lax.rem(t - 1 - k + nt, nt)

    barrier = pltpu.get_barrier_semaphore()
    for k in range(nt - 1):
        pl.semaphore_signal(barrier, inc=1, device_id=(d, peer(k)), device_id_type=MESH)
    pl.semaphore_signal(barrier, inc=1, device_id=sib, device_id_type=MESH)

    @pl.when(has_below)
    def _():
        pl.semaphore_signal(barrier, inc=1, device_id=below, device_id_type=MESH)

    @pl.when(has_above)
    def _():
        pl.semaphore_signal(barrier, inc=1, device_id=above, device_id_type=MESH)

    neighbours = jnp.where(has_below, 1, 0) + jnp.where(has_above, 1, 0)
    pl.semaphore_wait(barrier, nt + neighbours)

    def slot(index):
        return pl.ds(mult(index, ts), ts)

    def core_rows(core):
        return pl.ds(mult(core, tokens), tokens)

    def half_rows(core, index):
        return pl.ds(pl.multiple_of(core * tokens + index * ts, ts), ts)

    def own_copy(i):
        return pltpu.make_async_copy(packed.at[i, c], w.at[i, z, c], S["own"](i))

    def sib_copy(i):
        return remote(packed.at[i, 1 - c], w.at[i, z, c], S["sib_s"](i), S["sib_r"](i), sib)

    def sib_wait(i):
        return remote(packed.at[i, c], w.at[i, z, 1 - c], S["sib_s"](i), S["sib_r"](i), sib)

    qown = (
        pltpu.make_async_copy(packed_attn, aw.at[z, c], S["qown"](0)),
        pltpu.make_async_copy(packed_gain, gw.at[z, c], S["qown"](1)),
    )
    for copy in qown:
        copy.start()
    tok_all = pltpu.make_async_copy(tok, p2, S["tok"](0))
    tok_all.start()

    def q_ref(part, u, core):
        return (aw if part == 0 else gw).at[u, core]

    def q_line(part, s, direction):
        u = z - s if direction == 0 else z + s
        ref = q_ref(part, u, c)
        return remote(
            ref, ref, S["qa_s"](part, direction, s), S["qa_r"](part, direction, s), (above, below)[direction]
        )

    def q_arrive(part, s, direction):
        u = z - s if direction == 0 else z + s
        ref = q_ref(part, u, c)
        return remote(
            ref,
            ref,
            S["qa_s"](part, direction, s - 1),
            S["qa_r"](part, direction, s - 1),
            (below, above)[direction],
        )

    def q_sib(part, u):
        ref = q_ref(part, u, c)
        return remote(ref, ref, S["qs_s"](part, u), S["qs_r"](part, u), sib)

    def q_sib_in(part, u):
        ref = q_ref(part, u, 1 - c)
        return remote(ref, ref, S["qs_s"](part, u), S["qs_r"](part, u), sib)

    def line_valid(s, direction):
        return z - s >= 0 if direction == 0 else z + s <= nz - 1

    def line_sends(s, direction):
        return line_valid(s, direction) & (has_above if direction == 0 else has_below)

    def q_tick(s):
        if s == 0:
            for part in range(2):
                qown[part].wait()
        for direction in range(2):
            if s > 0:

                @pl.when(line_valid(s, direction))
                def _():
                    for part in range(2):
                        q_arrive(part, s, direction).wait_recv()

            if s < nz - 1:

                @pl.when(line_sends(s, direction))
                def _():
                    for part in range(2):
                        q_line(part, s, direction).start()

            if s > 0:

                @pl.when(line_valid(s, direction))
                def _():
                    for part in range(2):
                        q_sib(part, z - s if direction == 0 else z + s).start()

        if s == 0:
            for part in range(2):
                q_sib(part, z).start()

    def q_finish():
        for s in range(nz - 1):
            for direction in range(2):

                @pl.when(line_sends(s, direction))
                def _():
                    for part in range(2):
                        q_line(part, s, direction).wait_send()

        for u in range(nz):
            for part in range(2):
                q_sib_in(part, u).wait_recv()

    def ag_line(i, s, direction):
        unit = w.at[i, z - s if direction == 0 else z + s]
        return remote(
            unit, unit, S["ag_s"](i, direction, s), S["ag_r"](i, direction, s), (above, below)[direction]
        )

    def ag_arrive(i, s, direction):
        unit = w.at[i, z - s if direction == 0 else z + s]
        return remote(
            unit,
            unit,
            S["ag_s"](i, direction, s - 1),
            S["ag_r"](i, direction, s - 1),
            (below, above)[direction],
        )

    def ag_tick(i, s):
        if s == 0:
            own_copy(i).wait()
            sib_wait(i).wait_recv()
        for direction in range(2):
            if s > 0:

                @pl.when(line_valid(s, direction))
                def _():
                    ag_arrive(i, s, direction).wait_recv()

            if s < nz - 1:

                @pl.when(line_sends(s, direction))
                def _():
                    ag_line(i, s, direction).start()

    def ag_finish(i):
        for s in range(nz - 1):
            for direction in range(2):

                @pl.when(line_sends(s, direction))
                def _():
                    ag_line(i, s, direction).wait_send()

    def rs_owner(tau, direction):
        return nz - 1 + z - tau if direction == 0 else tau - (nz - 1 - z)

    def rs_valid(tau, direction):
        return z <= tau if direction == 0 else tau >= nz - 1 - z

    def rs_line(i, tau, direction):
        return remote(
            w.at[i, rs_owner(tau, direction)],
            (ru, rd)[direction].at[tau],
            S["rs_s"](direction, tau),
            S["rs_r"](direction, tau),
            (above, below)[direction],
        )

    def rs_tick(i, tau):
        for direction in range(2):
            got = (ru, rd)[direction]
            if tau > 0:

                @pl.when(rs_valid(tau, direction) & (has_below, has_above)[direction])
                def _():
                    owner = rs_owner(tau, direction)
                    remote(
                        w.at[i, owner],
                        got.at[tau - 1],
                        S["rs_s"](direction, tau - 1),
                        S["rs_r"](direction, tau - 1),
                        (below, above)[direction],
                    ).wait_recv()

                    def add(k, carry):
                        core, kind = k // 3, k % 3
                        a = w[i, owner, core, kind].astype(f32)
                        b = got[tau - 1, core, kind].astype(f32)
                        w[i, owner, core, kind] = (a + b).astype(bf16)
                        return carry

                    lax.fori_loop(0, 6, add, 0)

            if tau < nz - 1:

                @pl.when(rs_valid(tau, direction))
                def _():
                    rs_line(i, tau, direction).start()

    def give_credit():
        @pl.when(has_below)
        def _():
            pl.semaphore_signal(credit.at[0], inc=1, device_id=below, device_id_type=MESH)

        @pl.when(has_above)
        def _():
            pl.semaphore_signal(credit.at[1], inc=1, device_id=above, device_id_type=MESH)

    def take_credit():
        @pl.when(has_above)
        def _():
            pl.semaphore_wait(credit.at[0], 1)

        @pl.when(has_below)
        def _():
            pl.semaphore_wait(credit.at[1], 1)

    def fin_sib(i):
        return remote(w.at[i, z, 1 - c], fs.at[i], S["fin_s"](i), S["fin_r"](i), sib)

    def fin_in(i):
        return remote(w.at[i, z, c], fs.at[i], S["fin_s"](i), S["fin_r"](i), sib)

    def put_piece(i, half, piece):
        cols = pl.ds(mult(2 * i + half, hc), hc)
        st[0] = piece[0].astype(f32).T
        st[1] = piece[1].astype(f32).T
        st[2] = piece[2].astype(f32)
        puts = (
            pltpu.make_async_copy(st.at[0], g_gate.at[:, cols], S["put"](0)),
            pltpu.make_async_copy(st.at[1], g_up.at[:, cols], S["put"](1)),
            pltpu.make_async_copy(st.at[2], g_down.at[cols], S["put"](2)),
        )
        for copy in puts:
            copy.start()
        for copy in puts:
            copy.wait()

    def rs_finish(i):
        fin_sib(i).start()
        put_piece(i, c, w.at[i, z, c])
        for tau in range(nz - 1):
            for direction in range(2):

                @pl.when(rs_valid(tau, direction))
                def _():
                    rs_line(i, tau, direction).wait_send()

        give_credit()

    def fin_finish(i):
        fin_sib(i).wait_send()
        fin_in(i).wait_recv()
        put_piece(i, 1 - c, fs.at[i])

    tile = min(256, 2 * tokens)

    def compute(i):
        first = i == 0

        def rows_step(m, carry):
            rows = pl.ds(mult(m, tile), tile)
            xm = x[rows, :]
            gate = dot(xm, w[i, :, :, 0].reshape(width, hc))
            up = dot(xm, w[i, :, :, 1].reshape(width, hc))
            dh = jnp.zeros((tile, hc), f32)
            for k in range(dps):
                dh = dh + dot_nt(ct[rows, k * hc : (k + 1) * hc], w[i, k // 2, k % 2, 2])
            sig = jax.nn.sigmoid(gate)
            act = gate * sig
            hidden = (act * up).astype(bf16)
            d_up = (dh * act).astype(bf16)
            d_gate = (dh * up * sig * (1.0 + gate * (1.0 - sig))).astype(bf16)
            ht[:, rows] = hidden.T
            dgt[:, rows] = d_gate.T
            dut[:, rows] = d_up.T
            for k in range(dps):
                cols = slice(k * hc, (k + 1) * hc)
                fwd = dot(hidden, w[i, k // 2, k % 2, 2])
                back = dot_nt(d_gate, w[i, k // 2, k % 2, 0]) + dot_nt(d_up, w[i, k // 2, k % 2, 1])
                if first:
                    accp[rows, cols] = fwd.astype(bf16)
                    accb[rows, cols] = back
                else:
                    accp[rows, cols] = (accp[rows, cols].astype(f32) + fwd).astype(bf16)
                    accb[rows, cols] += back
            return carry

        lax.fori_loop(0, 2 * tokens // tile, rows_step, 0)

        def cols_step(k, carry):
            cols = pl.ds(mult(k, hc), hc)
            xs = x[:, cols]
            chip, core = k // 2, k % 2
            w[i, chip, core, 0] = dot(dgt[...], xs).astype(bf16)
            w[i, chip, core, 1] = dot(dut[...], xs).astype(bf16)
            w[i, chip, core, 2] = dot(ht[...], ct[:, cols]).astype(bf16)
            return carry

        lax.fori_loop(0, dps, cols_step, 0)

    lane = lax.broadcasted_iota(jnp.int32, (1, LANES), 1)
    low_head = lane < HD
    low_half = lane % HD < HD // 2

    def turn(u, cos, sin):
        swapped = jnp.where(low_half, pltpu.roll(u, LANES - HD // 2, 1), pltpu.roll(u, HD // 2, 1))
        return u * cos + swapped * sin

    def turn_back(g, cos, sin):
        v = g * sin
        swapped = jnp.where(low_half, pltpu.roll(v, LANES - HD // 2, 1), pltpu.roll(v, HD // 2, 1))
        return g * cos + swapped

    def tables(rows, with_values):
        cos, sin = cosine[rows, :], sine[rows, :]
        if with_values:
            cos, sin = jnp.where(low_head, cos, 1.0), jnp.where(low_head, sin, 0.0)
        return cos, sin

    step = 32

    def norm_rows(src, dst, base, grad_sum):
        def body(m, carry):
            rows = pl.ds(mult(m, step), step)
            v = src[rows, :].astype(f32)
            scale = lax.rsqrt(jnp.mean(v * v, axis=-1, keepdims=True) + epsilon)
            v = v * scale
            dst[pl.ds(pl.multiple_of(base + m * step, step), step), :] = (v * gv[0:1, :]).astype(bf16)
            if grad_sum is None:
                return carry
            up = grad_sum(rows)
            return carry + jnp.sum(up * v, axis=0, keepdims=True)

        start = 0 if grad_sum is None else jnp.zeros((1, width), f32)
        return lax.fori_loop(0, tokens // step, body, start)

    chunks = aw_cols(hc) // LANES
    per_block = hc // LANES
    atile = min(256, tokens)

    def joined():
        def body(m, carry):
            rows = pl.ds(mult(m, atile), atile)
            src = pl.ds(pl.multiple_of(c * tokens + m * atile, atile), atile)
            xm = x[src, :]
            for j in range(3):
                block = dot(xm, aw[:, :, j].reshape(width, hc))
                for q in range(per_block):
                    index = j * per_block + q
                    cos, sin = tables(rows, index % 3 == 2)
                    u = block[:, q * LANES : (q + 1) * LANES]
                    qkvb[rows, index * LANES : (index + 1) * LANES] = turn(u, cos, sin).astype(bf16)
            return carry

        lax.fori_loop(0, tokens // atile, body, 0)

    row_id = lax.broadcasted_iota(jnp.int32, (SEQ, SEQ), 0)
    col_id = lax.broadcasted_iota(jnp.int32, (SEQ, SEQ), 1)
    keep = row_id >= col_id
    inv_root = 1.0 / math.sqrt(HD)

    def doubled(rows, base):
        kv = qkvb[rows, pl.ds(pl.multiple_of(base + GROUPS * HD, LANES), LANES)].astype(f32)
        other = pltpu.roll(kv, HD, 1)
        kk = jnp.where(low_head, kv, other).astype(bf16)
        vv = jnp.where(low_head, other, kv).astype(bf16)
        return kk, vv

    def softmax(qm, kk):
        scores = jnp.where(keep, dot_nt(qm, kk) * inv_root, masked_score)
        e = jnp.exp(scores - jnp.max(scores, axis=-1, keepdims=True))
        return e * (1.0 / jnp.sum(e, axis=-1, keepdims=True))

    def place(n):
        s, h = n // kv_local, n % kv_local
        rows = pl.ds(mult(s, SEQ), SEQ)
        return rows, h * head_cols, h * GROUPS * HD

    def heads_forward():
        def body(n, carry):
            rows, base, qbase = place(n)
            kk, vv = doubled(rows, base)
            for pair in range(GROUPS // 2):
                qp = qkvb[rows, pl.ds(pl.multiple_of(base + pair * LANES, LANES), LANES)]
                halves = []
                for half in range(2):
                    mask = low_head if half == 0 else ~low_head
                    qm = jnp.where(mask, qp.astype(f32), 0.0).astype(bf16)
                    halves.append(dot(softmax(qm, kk).astype(bf16), vv))
                att[rows, pl.ds(pl.multiple_of(qbase + pair * LANES, LANES), LANES)] = jnp.where(
                    low_head, halves[0], halves[1]
                ).astype(bf16)
            return carry

        lax.fori_loop(0, seqs * kv_local, body, 0)

    def heads_backward():
        def body(n, carry):
            rows, base, qbase = place(n)
            kk, vv = doubled(rows, base)
            dkk = jnp.zeros((SEQ, LANES), f32)
            dvv = jnp.zeros((SEQ, LANES), f32)
            cos, sin = tables(rows, False)
            for pair in range(GROUPS // 2):
                cols = pl.ds(pl.multiple_of(base + pair * LANES, LANES), LANES)
                acols = pl.ds(pl.multiple_of(qbase + pair * LANES, LANES), LANES)
                qp = qkvb[rows, cols].astype(f32)
                dp = datt[rows, acols].astype(f32)
                prod = dp * att[rows, acols].astype(f32)
                halves = []
                for half in range(2):
                    mask = low_head if half == 0 else ~low_head
                    qm = jnp.where(mask, qp, 0.0).astype(bf16)
                    dm = jnp.where(mask, dp, 0.0).astype(bf16)
                    probs = softmax(qm, kk)
                    delta = jnp.sum(jnp.where(mask, prod, 0.0), axis=-1, keepdims=True)
                    ds = (probs * (dot_nt(dm, vv) - delta) * inv_root).astype(bf16)
                    halves.append(dot(ds, kk))
                    dkk = dkk + dot(ds.T, qm)
                    dvv = dvv + dot(probs.astype(bf16).T, dm)
                dq = jnp.where(low_head, halves[0], halves[1])
                qkvb[rows, cols] = turn_back(dq, cos, sin).astype(bf16)
            dkk = dkk + pltpu.roll(dkk, HD, 1)
            dvv = dvv + pltpu.roll(dvv, HD, 1)
            cos, sin = tables(rows, True)
            qkvb[rows, pl.ds(pl.multiple_of(base + GROUPS * HD, LANES), LANES)] = turn_back(
                jnp.where(low_head, dkk, dvv), cos, sin
            ).astype(bf16)
            return carry

        lax.fori_loop(0, seqs * kv_local, body, 0)

    def out_weight(k):
        return aw[k // 2, k % 2, 3:5].reshape(2 * hc, hc)

    def attention_partial():
        def body(k, carry):
            cols = pl.ds(mult(k, hc), hc)
            rsb[:, cols] = dot(att[...], out_weight(k)).astype(bf16)
            return carry

        lax.fori_loop(0, dps, body, 0)

    def scatter(src, base, land, which, k):
        rows = pl.ds(pl.multiple_of(base + peer(k) * ts, ts), ts)
        return remote(
            src.at[rows], land.at[slot(t)], S["ps_s"](which, k), S["ps_r"](which, k), (d, peer(k))
        )

    def block(land, which, k):
        return remote(
            rsb.at[slot(k)], land.at[slot(t)], S["ps_s"](which, k), S["ps_r"](which, k), (d, peer(k))
        )

    def landed(land, which, k):
        frm = source(k)
        return remote(
            rsb.at[slot(k)], land.at[slot(frm)], S["ps_s"](which, k), S["ps_r"](which, k), (d, frm)
        )

    def summed(land, rows0):
        total = land[pl.ds(pl.multiple_of(rows0, step), step), :].astype(f32)
        for k in range(1, nt):
            total = total + land[pl.ds(pl.multiple_of(k * ts + rows0, step), step), :].astype(f32)
        return total

    def spread(src, dst, which, k):
        return remote(src, dst, S["ga_s"](which, k), S["ga_r"](which, k), (d, peer(k)))

    def spread_in(src, dst, which, k):
        return remote(src, dst, S["ga_s"](which, k), S["ga_r"](which, k), (d, source(k)))

    q_tick(0)
    for i in range(nch):
        own_copy(i).start()
        sib_copy(i).start()
    cot_own = pltpu.make_async_copy(cot, ct.at[core_rows(c)], S["cot"](0))
    cot_sib = remote(cot, ct.at[core_rows(c)], S["cot"](1), S["cot"](2), sib)
    cot_in = remote(cot, ct.at[core_rows(1 - c)], S["cot"](1), S["cot"](2), sib)
    cot_own.start()
    cot_sib.start()
    for s in range(1, nz):
        if s == nz - 1:
            ag_tick(0, 0)
        q_tick(s)
    if nz == 1:
        ag_tick(0, 0)
    q_finish()
    for k in range(dps):
        gv[:, k * hc : (k + 1) * hc] = gw[k // 2, k % 2].astype(f32)
    tok_all.wait()
    norm_rows(p2, x, c * tokens, None)
    joined()
    heads_forward()
    if nz > 1:
        ag_tick(0, 1)
    attention_partial()
    for k in range(nt - 1):
        scatter(rsb, 0, p1, 0, k).start()
    p1[slot(t), :] = rsb[slot(t), :]
    if nz > 2:
        ag_tick(0, 2)
    if nz > 3:
        ag_tick(1, 0)
    for k in range(nt - 1):
        landed(p1, 0, k).wait_recv()
    mine = half_rows(c, t)

    def second_norm(m, carry):
        rows = pl.ds(mult(m, step), step)
        trow = pl.ds(pl.multiple_of(t * ts + m * step, step), step)
        total = p2[trow, :].astype(f32) + summed(p1, m * step)
        resid[rows, :] = total
        scale = lax.rsqrt(jnp.mean(total * total, axis=-1, keepdims=True) + epsilon)
        x[pl.ds(pl.multiple_of(c * tokens + t * ts + m * step, step), step), :] = (
            total * scale * gv[1:2, :]
        ).astype(bf16)
        return carry

    lax.fori_loop(0, ts // step, second_norm, 0)

    def x_copy(k):
        return remote(x.at[mine], x.at[mine], S["x_s"](k), S["x_r"](k), (d, peer(k)))

    def x_in(k):
        rows = half_rows(c, source(k))
        return remote(x.at[rows], x.at[rows], S["x_s"](k), S["x_r"](k), (d, source(k)))

    def xs_copy(k):
        rows = half_rows(c, lax.rem(t - k + nt, nt))
        return remote(x.at[rows], x.at[rows], S["xs_s"](k), S["xs_r"](k), sib)

    def xs_in(k):
        rows = half_rows(1 - c, lax.rem(t - k + nt, nt))
        return remote(x.at[rows], x.at[rows], S["xs_s"](k), S["xs_r"](k), sib)

    for k in range(nt - 1):
        x_copy(k).start()
    xs_copy(0).start()
    for s in range(3, nz):
        ag_tick(0, s)
    ag_finish(0)
    if nz <= 3:
        ag_tick(1, 0)
    for k in range(nt - 1):
        x_in(k).wait_recv()
        xs_copy(k + 1).start()
    cot_own.wait()
    cot_in.wait_recv()
    for k in range(nt):
        xs_in(k).wait_recv()

    for i in range(nch):
        more = i + 1 < nch
        if i > 0 and more:
            ag_tick(i + 1, 0)
        compute(i)
        if i > 0:
            take_credit()
        rs_tick(i, 0)
        if more:
            for s in range(1, nz):
                ag_tick(i + 1, s)
                rs_tick(i, s)
            ag_finish(i + 1)
            if i > 0:
                fin_finish(i - 1)
            rs_finish(i)

    last = nch - 1
    other = (1 - c) * tokens

    def sib_b(k):
        rows = half_rows(1 - c, peer(k))
        return remote(x.at[rows], sbr_b.at[slot(k)], S["sb_s"](0, k), S["sb_r"](0, k), sib)

    def sib_p(k):
        rows = half_rows(1 - c, peer(k))
        return remote(accp.at[rows], sbr_p.at[slot(k)], S["sb_s"](1, k), S["sb_r"](1, k), sib)

    for u in range(nz):
        for part in range(2):
            q_sib(part, u).wait_send()
    for k in range(nt - 1):
        x_copy(k).wait_send()
        scatter(rsb, 0, p1, 0, k).wait_send()
    for k in range(nt):
        xs_copy(k).wait_send()
    for k in range(nt):
        rows = half_rows(1 - c, peer(k))
        x[rows, :] = accb[rows, :].astype(bf16)
        sib_b(k).start()
    for k in range(nt):
        remote(x.at[half_rows(c, peer(k))], sbr_b.at[slot(k)], S["sb_s"](0, k), S["sb_r"](0, k), sib).wait_recv()
        part = accb[half_rows(c, peer(k)), :] + sbr_b[slot(k), :].astype(f32)
        if k < nt - 1:
            rsb[slot(k), :] = part.astype(bf16)
            block(p2, 1, k).start()
        else:
            p2[slot(t), :] = part.astype(bf16)
    if nz > 1:
        rs_tick(last, 1)
    for k in range(nt - 1):
        landed(p2, 1, k).wait_recv()

    def second_back(m, carry):
        rows = pl.ds(mult(m, step), step)
        place_ = pl.ds(pl.multiple_of(c * tokens + t * ts + m * step, step), step)
        up = summed(p2, m * step)
        v = resid[rows, :]
        scale = lax.rsqrt(jnp.mean(v * v, axis=-1, keepdims=True) + epsilon)
        weighted = up * gv[1:2, :]
        inner = jnp.mean(weighted * v, axis=-1, keepdims=True)
        grad = ct[place_, :].astype(f32) + scale * weighted - v * (scale * scale * scale) * inner
        accb[rows, :] = grad
        x[place_, :] = grad.astype(bf16)
        return carry + jnp.sum(up * v * scale, axis=0, keepdims=True)

    gain_two = lax.fori_loop(0, ts // step, second_back, jnp.zeros((1, width), f32))
    for k in range(nt - 1):
        spread(x.at[mine], x.at[mine], 0, k).start()
    for k in range(nt):
        sib_p(k).start()
    for s in range(2, nz):
        rs_tick(last, s)
    if nch > 1:
        fin_finish(last - 1)
    rs_finish(last)
    take_credit()

    for k in range(nt - 1):
        rows = half_rows(c, source(k))
        spread_in(x.at[rows], x.at[rows], 0, k).wait_recv()

    def d_attended(m, carry):
        rows = pl.ds(mult(m, atile), atile)
        src = pl.ds(pl.multiple_of(c * tokens + m * atile, atile), atile)
        for j in range(2):
            total = jnp.zeros((atile, hc), f32)
            for k in range(dps):
                total = total + dot_nt(x[src, k * hc : (k + 1) * hc], aw[k // 2, k % 2, 3 + j])
            datt[rows, j * hc : (j + 1) * hc] = total.astype(bf16)
        for j in range(2):
            (ht, dgt)[j][:, rows] = att[rows, j * hc : (j + 1) * hc].T
        return carry

    lax.fori_loop(0, tokens // atile, d_attended, 0)

    def out_grads(k, carry):
        xs = x[core_rows(c), pl.ds(mult(k, hc), hc)]
        for j in range(2):
            aw[k // 2, k % 2, 3 + j] = dot((ht, dgt)[j][:, :tokens], xs).astype(bf16)
        return carry

    lax.fori_loop(0, dps, out_grads, 0)

    def a_src(part, u, core):
        return (aw.at[u, core, 3:5], aw.at[u, core, 0:3], gg.at[u, core])[part]

    def a_sib_ref(part):
        return (w.at[0, :, 1, 0:2], w.at[0, :, 0], gsib)[part]

    def a_sib(part):
        src = (aw.at[:, 1 - c, 3:5], aw.at[:, 1 - c, 0:3], gg.at[:, 1 - c])[part]
        return remote(src, a_sib_ref(part), S["as_s"](part), S["as_r"](part), sib)

    def a_land(part, direction, tau):
        line = (ru, rd)[direction]
        return (line.at[tau, 1, 0:2], line.at[tau, 0], (gru, grd)[direction].at[tau])[part]

    def a_line(part, tau, direction):
        return remote(
            a_src(part, rs_owner(tau, direction), c),
            a_land(part, direction, tau),
            S["ar_s"](part, direction, tau),
            S["ar_r"](part, direction, tau),
            (above, below)[direction],
        )

    def a_add(part, owner, got):
        if part == 2:
            gg[owner, c] = gg[owner, c] + got[...]
            return
        base, count = ((3, 2), (0, 3))[part]
        for j in range(count):
            both = aw[owner, c, base + j].astype(f32) + got[j].astype(f32)
            aw[owner, c, base + j] = both.astype(bf16)

    def a_pair(part):
        a_sib(part).wait_recv()

        def body(u, carry):
            a_add(part, u, (w.at[0, u, 1, 0:2], w.at[0, u, 0], gsib.at[u])[part])
            return carry

        lax.fori_loop(0, nz, body, 0)

    def a_tick(part, tau):
        for direction in range(2):
            if tau > 0:

                @pl.when(rs_valid(tau, direction) & (has_below, has_above)[direction])
                def _():
                    owner = rs_owner(tau, direction)
                    remote(
                        a_src(part, owner, c),
                        a_land(part, direction, tau - 1),
                        S["ar_s"](part, direction, tau - 1),
                        S["ar_r"](part, direction, tau - 1),
                        (below, above)[direction],
                    ).wait_recv()
                    a_add(part, owner, a_land(part, direction, tau - 1))

            if tau < nz - 1:

                @pl.when(rs_valid(tau, direction))
                def _():
                    a_line(part, tau, direction).start()

    def a_finish(part):
        a_sib(part).wait_send()
        for tau in range(nz - 1):
            for direction in range(2):

                @pl.when(rs_valid(tau, direction))
                def _():
                    a_line(part, tau, direction).wait_send()

    a_sib(0).start()
    tok_again = pltpu.make_async_copy(tok, sbr_b, S["tok"](1))
    tok_again.start()
    for k in range(nt - 1):
        block(p2, 1, k).wait_send()
    for k in range(nt):
        remote(accp.at[half_rows(c, peer(k))], sbr_p.at[slot(k)], S["sb_s"](1, k), S["sb_r"](1, k), sib).wait_recv()
        part = accp[half_rows(c, peer(k)), :].astype(f32) + sbr_p[slot(k), :].astype(f32)
        if k < nt - 1:
            rsb[slot(k), :] = part.astype(bf16)
            block(p1, 2, k).start()
        else:
            p1[slot(t), :] = part.astype(bf16)
    a_pair(0)
    a_tick(0, 0)
    heads_backward()
    for k in range(nt):
        sib_b(k).wait_send()

    def attn_back(k, carry):
        total = jnp.zeros((tokens, hc), f32)
        for j in range(3):
            total = total + dot_nt(qkvb[:, j * hc : (j + 1) * hc], aw[k // 2, k % 2, j])
        x[pl.ds(mult(1 - c, tokens), tokens), pl.ds(mult(k, hc), hc)] = total.astype(bf16)
        return carry

    lax.fori_loop(0, dps, attn_back, 0)
    for k in range(nt - 1):
        scatter(x, other, p2, 3, k).start()
    p2[slot(t), :] = x[half_rows(1 - c, t), :]
    if nz > 1:
        a_tick(0, 1)
    tok_again.wait()

    def own_back(rows):
        return x[pl.ds(pl.multiple_of(other + rows.start, step), step), :].astype(f32)

    gain_one = norm_rows(sbr_b, sbr_p, 0, own_back)
    for k in range(dps):
        cols = slice(k * hc, (k + 1) * hc)
        gg[k // 2, k % 2] = jnp.concatenate(
            [gain_one[:, cols], gain_two[:, cols], jnp.zeros((6, hc), f32)], axis=0
        )
    a_sib(2).start()
    for m in range(tokens // atile):
        for j in range(3):
            (ht, dgt, dut)[j][:, tokens + m * atile : tokens + (m + 1) * atile] = qkvb[
                m * atile : (m + 1) * atile, j * hc : (j + 1) * hc
            ].T

    def qkv_grads(k, carry):
        xs = sbr_p[:, pl.ds(mult(k, hc), hc)]
        for j in range(3):
            aw[k // 2, k % 2, j] = dot((ht, dgt, dut)[j][:, tokens:], xs).astype(bf16)
        return carry

    lax.fori_loop(0, dps, qkv_grads, 0)
    a_sib(1).start()
    if nz > 2:
        a_tick(0, 2)
    a_pair(1)
    a_pair(2)
    a_tick(1, 0)
    a_tick(2, 0)
    for s in range(3, nz):
        a_tick(0, s)

    for k in range(nt - 1):
        landed(p1, 2, k).wait_recv()

    def finish_output(m, carry):
        rows = pl.ds(mult(m, step), step)
        where = pl.ds(pl.multiple_of(c * tokens + t * ts + m * step, step), step)
        accp[where, :] = (resid[rows, :] + summed(p1, m * step)).astype(bf16)
        return carry

    lax.fori_loop(0, ts // step, finish_output, 0)
    for k in range(nt - 1):
        spread(accp.at[mine], out.at[slot(t)], 1, k).start()
    put_out = pltpu.make_async_copy(accp.at[mine], out.at[slot(t)], S["loc"](0))
    put_out.start()

    for k in range(nt - 1):
        landed(p2, 3, k).wait_recv()
    for k in range(nt):
        sib_p(k).wait_send()
    theirs = half_rows(1 - c, t)

    def finish_tokens(m, carry):
        rows = pl.ds(mult(m, step), step)
        up = summed(p2, m * step)
        v = sbr_b[pl.ds(pl.multiple_of(t * ts + m * step, step), step), :].astype(f32)
        scale = lax.rsqrt(jnp.mean(v * v, axis=-1, keepdims=True) + epsilon)
        weighted = up * gv[0:1, :]
        inner = jnp.mean(weighted * v, axis=-1, keepdims=True)
        grad = accb[rows, :] + scale * weighted - v * (scale * scale * scale) * inner
        accp[pl.ds(pl.multiple_of(other + t * ts + m * step, step), step), :] = grad.astype(bf16)
        return carry

    lax.fori_loop(0, ts // step, finish_tokens, 0)
    for k in range(nt - 1):
        spread(accp.at[theirs], dtok.at[slot(t)], 2, k).start()
    put_tok = pltpu.make_async_copy(accp.at[theirs], dtok.at[slot(t)], S["loc"](1))
    put_tok.start()
    fin_finish(last)
    for s in range(1, nz):
        a_tick(2, s)
        a_tick(1, s)

    def gain_copy(k):
        return remote(gg.at[z, c], gt.at[t], S["gg_s"](k), S["gg_r"](k), (d, peer(k)))

    def gain_in(k):
        return remote(gg.at[z, c], gt.at[source(k)], S["gg_s"](k), S["gg_r"](k), (d, source(k)))

    for k in range(nt - 1):
        gain_copy(k).start()
    gt[t] = gg[z, c]

    base = ts
    for j in range(3):
        accb[base : base + hc, j * hc : (j + 1) * hc] = aw[z, c, j].astype(f32).T
    for j in range(2):
        accb[base + hc + j * hc : base + 2 * hc + j * hc, 0:hc] = aw[z, c, 3 + j].astype(f32)
    put_qkv = pltpu.make_async_copy(
        accb.at[base : base + hc, 0 : 3 * hc], g_qkv, S["loc"](2)
    )
    put_o = pltpu.make_async_copy(
        accb.at[base + hc : base + 3 * hc, 0:hc], g_out, S["loc"](3)
    )
    put_qkv.start()
    put_o.start()
    for k in range(nt - 1):
        gain_in(k).wait_recv()
    total = gt[0]
    for k in range(1, nt):
        total = total + gt[k]
    g_gains[...] = total

    for i in range(nch):
        sib_copy(i).wait_send()
    cot_sib.wait_send()
    for part in range(3):
        a_finish(part)
    for k in range(nt - 1):
        gain_copy(k).wait_send()
        block(p1, 2, k).wait_send()
        scatter(x, other, p2, 3, k).wait_send()
        spread(x.at[mine], x.at[mine], 0, k).wait_send()
        spread(accp.at[mine], out.at[slot(t)], 1, k).wait_send()
        spread(accp.at[theirs], dtok.at[slot(t)], 2, k).wait_send()
        spread_in(accp.at[mine], out.at[slot(source(k))], 1, k).wait_recv()
        spread_in(accp.at[theirs], dtok.at[slot(source(k))], 2, k).wait_recv()
    put_out.wait()
    put_tok.wait()
    put_qkv.wait()
    put_o.wait()


def aw_cols(shard):
    return 3 * shard


def layer(tokens, cotangent, packed, packed_attn, packed_gain, cosine, sine, nz, nt, hid):
    count, width = tokens.shape
    nch, _, _, hc, _ = packed.shape
    ts = count // nt
    sizes = (nz, nt, nch, count, width, hc)
    sems, _ = semaphores(nz, nt, nch)
    V = pltpu.VMEM
    recv = (nz - 1, 2, 3, hc, hc)
    S = jax.ShapeDtypeStruct
    return pl.pallas_call(
        functools.partial(layer_kernel, sizes),
        out_shape=(
            S((count, width), bf16),
            S((count, width), bf16),
            S((hc, 3 * hc), f32),
            S((2 * hc, hc), f32),
            S((hc, hid), f32),
            S((hc, hid), f32),
            S((hid, hc), f32),
            S((8, hc), f32),
        ),
        in_specs=[HBM, HBM, HBM, HBM, HBM, VMEM, VMEM],
        out_specs=(HBM, HBM, HBM, HBM, HBM, HBM, HBM, VMEM),
        scratch_shapes=[
            V((nch, nz, 2, 3, hc, hc), bf16),
            V(recv, bf16),
            V(recv, bf16),
            V((2 * count, width), bf16),
            V((2 * count, width), bf16),
            V((2 * count, width), bf16),
            V((2 * count, width), f32),
            V((hc, 2 * count), bf16),
            V((hc, 2 * count), bf16),
            V((hc, 2 * count), bf16),
            V((ts, width), f32),
            V((count, width), bf16),
            V((count, width), bf16),
            V((count, width), bf16),
            V((count, width), bf16),
            V((count, width), bf16),
            V((nz, 2, 5, hc, hc), bf16),
            V((count, 3 * hc), bf16),
            V((count, 2 * hc), bf16),
            V((count, 2 * hc), bf16),
            V((nch, 3, hc, hc), bf16),
            V((3, hc, hc), f32),
            V((nz, 2, 16, hc), bf16),
            V((16, width), f32),
            V((nz, 2, 8, hc), f32),
            V((nz, 8, hc), f32),
            V((nz - 1, 8, hc), f32),
            V((nz - 1, 8, hc), f32),
            V((nt, 8, hc), f32),
            pltpu.SemaphoreType.DMA((sems.count,)),
            pltpu.SemaphoreType.REGULAR((2,)),
        ],
        compiler_params=pltpu.CompilerParams(
            collective_id=0, has_side_effects=True, vmem_limit_bytes=63 * 2**20
        ),
        name="layer",
    )(tokens, cotangent, packed, packed_attn, packed_gain, cosine, sine)


def local(tokens, positions, w_qkv, w_out, w_gate, w_up, w_down, gain_attn, gain_ffn, cotangent):
    nz = lax.axis_size("dp") // 2
    nt = lax.axis_size("tensor")
    shard, hid = w_gate.shape
    nch = hid // (2 * shard)
    packed = jnp.stack(
        [
            w_gate.reshape(shard, nch, 2, shard).transpose(1, 2, 0, 3),
            w_up.reshape(shard, nch, 2, shard).transpose(1, 2, 0, 3),
            w_down.reshape(nch, 2, shard, shard),
        ],
        axis=2,
    )
    packed_attn = jnp.concatenate(
        [w_qkv.reshape(shard, 3, shard).transpose(1, 0, 2), w_out.reshape(2, shard, shard)]
    )
    packed_gain = jnp.concatenate([jnp.stack([gain_attn, gain_ffn]), jnp.zeros((14, shard), bf16)])
    cosine, sine = rotary_tables(positions)
    output, d_tokens, g_qkv, g_out, g_gate, g_up, g_down, g_gains = layer(
        tokens, cotangent, packed, packed_attn, packed_gain, cosine, sine, nz, nt, hid
    )
    return output, d_tokens, g_qkv, g_out, g_gate, g_up, g_down, g_gains[0], g_gains[1]


def solution(mesh):
    return jax.shard_map(
        local,
        mesh=mesh,
        in_specs=(
            P("dp", None),
            P("dp"),
            P("dp", "tensor"),
            P("tensor", "dp"),
            P("dp", "tensor"),
            P("dp", "tensor"),
            P("tensor", "dp"),
            P("dp"),
            P("dp"),
            P("dp", None),
        ),
        out_specs=(
            P("dp", None),
            P("dp", None),
            P("dp", "tensor"),
            P("tensor", "dp"),
            P("dp", "tensor"),
            P("dp", "tensor"),
            P("tensor", "dp"),
            P("dp"),
            P("dp"),
        ),
        check_vma=False,
    )
```

```python
import functools
import math

import jax
import jax.numpy as jnp
from jax import lax
from jax.experimental import pallas as pl
from jax.experimental.pallas import tpu as pltpu
from jax.sharding import PartitionSpec as P

HEADS = 32
KV_HEADS = 8
HD = 64
SEQ = 256
GROUPS = HEADS // KV_HEADS
LANES = 128

epsilon = 1e-05
rope_base = 500000.0
masked_score = -1e30

MESH = pl.DeviceIdType.MESH
HBM = pl.BlockSpec(memory_space=pl.ANY)
VMEM = pl.BlockSpec(memory_space=pltpu.VMEM)
bf16 = jnp.bfloat16
f32 = jnp.float32
NT_DIMS = (((1,), (1,)), ((), ()))


def remote(src, dst, send, recv, device):
    return pltpu.make_async_remote_copy(
        src_ref=src, dst_ref=dst, send_sem=send, recv_sem=recv, device_id=device, device_id_type=MESH
    )


def mult(value, factor):
    return pl.multiple_of(value * factor, factor)


def dot(a, b):
    return jnp.dot(a, b, preferred_element_type=f32)


def dot_nt(a, b):
    return lax.dot_general(a, b, NT_DIMS, preferred_element_type=f32)


class Sems:
    def __init__(self):
        self.count = 0
        self.ref = None

    def take(self, *dims):
        base = self.count
        self.count += math.prod(dims)

        def at(*index):
            flat = 0
            for size, place in zip(dims, index):
                flat = flat * size + place
            return self.ref.at[base + flat]

        return at


def semaphores(nz, nt, nch):
    s = Sems()
    names = {
        "own": s.take(nch, 3),
        "sib_s": s.take(nch, 3),
        "sib_r": s.take(nch, 3),
        "ag_s": s.take(nch, 2, nz),
        "ag_r": s.take(nch, 2, nz),
        "qown": s.take(5),
        "qa_s": s.take(2, 2, nz),
        "qa_r": s.take(2, 2, nz),
        "qs_s": s.take(2, nz),
        "qs_r": s.take(2, nz),
        "rs_s": s.take(2, nz),
        "rs_r": s.take(2, nz),
        "as_s": s.take(3),
        "as_r": s.take(3),
        "ar_s": s.take(3, 2, nz),
        "ar_r": s.take(3, 2, nz),
        "fin_s": s.take(nch),
        "fin_r": s.take(nch),
        "put": s.take(8),
        "cot": s.take(3),
        "tok": s.take(3),
        "ps_s": s.take(4, max(nt, 6)),
        "ps_r": s.take(4, max(nt, 6)),
        "xs_s": s.take(nt),
        "xs_r": s.take(nt),
        "sb_s": s.take(2, nt),
        "sb_r": s.take(2, nt),
        "ga_s": s.take(4, max(nt, 6)),
        "ga_r": s.take(4, max(nt, 6)),
        "gg_s": s.take(nt),
        "gg_r": s.take(nt),
        "loc": s.take(5),
    }
    return s, names


def layer_kernel(
    sizes,
    tok,
    cot,
    w_qkv,
    w_out,
    w_gate,
    w_up,
    w_down,
    pos,
    gain_a,
    gain_f,
    out,
    dtok,
    g_qkv,
    g_out,
    g_gate,
    g_up,
    g_down,
    g_gains,
    w,
    ru,
    rd,
    x,
    ct,
    accp,
    accb,
    acco,
    ht,
    dgt,
    dut,
    resid,
    p1,
    p2,
    sbr_b,
    sbr_p,
    rsb,
    aw,
    qkvb,
    att,
    datt,
    fs,
    st,
    gw,
    gv,
    gg,
    gsib,
    gru,
    grd,
    gt,
    cosine,
    sine,
    sem_ref,
    credit,
):
    nz, nt, nch, tokens, width, hc = sizes
    sems, S = semaphores(nz, nt, nch)
    sems.ref = sem_ref
    ts = tokens // nt
    dps = 2 * nz
    d = lax.axis_index("dp")
    t = lax.axis_index("tensor")
    z = d // 2
    c = d % 2
    sib = (2 * z + 1 - c, t)
    above = (d + 2, t)
    below = (d - 2, t)
    has_above = z < nz - 1
    has_below = z > 0
    seqs = tokens // SEQ
    kv_local = aw_cols(hc) // ((GROUPS + 2) * HD)
    head_cols = (GROUPS + 2) * HD

    def peer(k):
        return lax.rem(t + 1 + k, nt)

    def source(k):
        return lax.rem(t - 1 - k + nt, nt)

    barrier = pltpu.get_barrier_semaphore()
    for k in range(nt - 1):
        pl.semaphore_signal(barrier, inc=1, device_id=(d, peer(k)), device_id_type=MESH)
    pl.semaphore_signal(barrier, inc=1, device_id=sib, device_id_type=MESH)

    @pl.when(has_below)
    def _():
        pl.semaphore_signal(barrier, inc=1, device_id=below, device_id_type=MESH)

    @pl.when(has_above)
    def _():
        pl.semaphore_signal(barrier, inc=1, device_id=above, device_id_type=MESH)

    neighbours = jnp.where(has_below, 1, 0) + jnp.where(has_above, 1, 0)
    pl.semaphore_wait(barrier, nt + neighbours)

    def slot(index):
        return pl.ds(mult(index, ts), ts)

    def core_rows(core):
        return pl.ds(mult(core, tokens), tokens)

    def half_rows(core, index):
        return pl.ds(pl.multiple_of(core * tokens + index * ts, ts), ts)

    def ffn_source(i, core, kind):
        cols = pl.ds(mult(2 * i + core, hc), hc)
        return (w_gate.at[:, cols], w_up.at[:, cols], w_down.at[cols])[kind]

    def own_copy(i, kind):
        return pltpu.make_async_copy(ffn_source(i, c, kind), w.at[i, z, c, kind], S["own"](i, kind))

    def sib_copy(i, kind):
        return remote(
            ffn_source(i, 1 - c, kind), w.at[i, z, c, kind], S["sib_s"](i, kind), S["sib_r"](i, kind), sib
        )

    def sib_wait(i, kind):
        return remote(
            ffn_source(i, c, kind), w.at[i, z, 1 - c, kind], S["sib_s"](i, kind), S["sib_r"](i, kind), sib
        )

    qown = [
        pltpu.make_async_copy(w_qkv.at[:, j * hc : (j + 1) * hc], aw.at[z, c, j], S["qown"](j))
        for j in range(3)
    ] + [
        pltpu.make_async_copy(w_out.at[j * hc : (j + 1) * hc], aw.at[z, c, 3 + j], S["qown"](3 + j))
        for j in range(2)
    ]
    for copy in qown:
        copy.start()
    row16 = lax.broadcasted_iota(jnp.int32, (16, hc), 0)
    gw[z, c] = jnp.where(
        row16 == 0,
        gain_a[...].astype(f32).reshape(1, hc),
        jnp.where(row16 == 1, gain_f[...].astype(f32).reshape(1, hc), 0.0),
    ).astype(bf16)
    tok_all = pltpu.make_async_copy(tok, p2, S["tok"](0))
    tok_all.start()

    def q_ref(part, u, core):
        return (aw if part == 0 else gw).at[u, core]

    def q_line(part, s, direction):
        u = z - s if direction == 0 else z + s
        ref = q_ref(part, u, c)
        return remote(
            ref, ref, S["qa_s"](part, direction, s), S["qa_r"](part, direction, s), (above, below)[direction]
        )

    def q_arrive(part, s, direction):
        u = z - s if direction == 0 else z + s
        ref = q_ref(part, u, c)
        return remote(
            ref,
            ref,
            S["qa_s"](part, direction, s - 1),
            S["qa_r"](part, direction, s - 1),
            (below, above)[direction],
        )

    def q_sib(part, u):
        ref = q_ref(part, u, c)
        return remote(ref, ref, S["qs_s"](part, u), S["qs_r"](part, u), sib)

    def q_sib_in(part, u):
        ref = q_ref(part, u, 1 - c)
        return remote(ref, ref, S["qs_s"](part, u), S["qs_r"](part, u), sib)

    def line_valid(s, direction):
        return z - s >= 0 if direction == 0 else z + s <= nz - 1

    def line_sends(s, direction):
        return line_valid(s, direction) & (has_above if direction == 0 else has_below)

    def q_tick(s):
        if s == 0:
            for copy in qown:
                copy.wait()
        for direction in range(2):
            if s > 0:

                @pl.when(line_valid(s, direction))
                def _():
                    for part in range(2):
                        q_arrive(part, s, direction).wait_recv()

            if s < nz - 1:

                @pl.when(line_sends(s, direction))
                def _():
                    for part in range(2):
                        q_line(part, s, direction).start()

            if s > 0:

                @pl.when(line_valid(s, direction))
                def _():
                    for part in range(2):
                        q_sib(part, z - s if direction == 0 else z + s).start()

        if s == 0:
            for part in range(2):
                q_sib(part, z).start()

    def q_finish():
        for s in range(nz - 1):
            for direction in range(2):

                @pl.when(line_sends(s, direction))
                def _():
                    for part in range(2):
                        q_line(part, s, direction).wait_send()

        for u in range(nz):
            for part in range(2):
                q_sib_in(part, u).wait_recv()

    def ag_line(i, s, direction):
        unit = w.at[i, z - s if direction == 0 else z + s]
        return remote(
            unit, unit, S["ag_s"](i, direction, s), S["ag_r"](i, direction, s), (above, below)[direction]
        )

    def ag_arrive(i, s, direction):
        unit = w.at[i, z - s if direction == 0 else z + s]
        return remote(
            unit,
            unit,
            S["ag_s"](i, direction, s - 1),
            S["ag_r"](i, direction, s - 1),
            (below, above)[direction],
        )

    def ag_tick(i, s):
        if s == 0:
            for kind in range(3):
                own_copy(i, kind).wait()
                sib_wait(i, kind).wait_recv()
        for direction in range(2):
            if s > 0:

                @pl.when(line_valid(s, direction))
                def _():
                    ag_arrive(i, s, direction).wait_recv()

            if s < nz - 1:

                @pl.when(line_sends(s, direction))
                def _():
                    ag_line(i, s, direction).start()

    def ag_finish(i):
        for s in range(nz - 1):
            for direction in range(2):

                @pl.when(line_sends(s, direction))
                def _():
                    ag_line(i, s, direction).wait_send()

    def rs_owner(tau, direction):
        return nz - 1 + z - tau if direction == 0 else tau - (nz - 1 - z)

    def rs_valid(tau, direction):
        return z <= tau if direction == 0 else tau >= nz - 1 - z

    def rs_line(i, tau, direction):
        return remote(
            w.at[i, rs_owner(tau, direction)],
            (ru, rd)[direction].at[tau],
            S["rs_s"](direction, tau),
            S["rs_r"](direction, tau),
            (above, below)[direction],
        )

    def rs_tick(i, tau):
        for direction in range(2):
            got = (ru, rd)[direction]
            if tau > 0:

                @pl.when(rs_valid(tau, direction) & (has_below, has_above)[direction])
                def _():
                    owner = rs_owner(tau, direction)
                    remote(
                        w.at[i, owner],
                        got.at[tau - 1],
                        S["rs_s"](direction, tau - 1),
                        S["rs_r"](direction, tau - 1),
                        (below, above)[direction],
                    ).wait_recv()

                    def add(k, carry):
                        core, kind = k // 3, k % 3
                        a = w[i, owner, core, kind].astype(f32)
                        b = got[tau - 1, core, kind].astype(f32)
                        w[i, owner, core, kind] = (a + b).astype(bf16)
                        return carry

                    lax.fori_loop(0, 6, add, 0)

            if tau < nz - 1:

                @pl.when(rs_valid(tau, direction))
                def _():
                    rs_line(i, tau, direction).start()

    def give_credit():
        @pl.when(has_below)
        def _():
            pl.semaphore_signal(credit.at[0], inc=1, device_id=below, device_id_type=MESH)

        @pl.when(has_above)
        def _():
            pl.semaphore_signal(credit.at[1], inc=1, device_id=above, device_id_type=MESH)

    def take_credit():
        @pl.when(has_above)
        def _():
            pl.semaphore_wait(credit.at[0], 1)

        @pl.when(has_below)
        def _():
            pl.semaphore_wait(credit.at[1], 1)

    def fin_sib(i):
        return remote(w.at[i, z, 1 - c], fs.at[i], S["fin_s"](i), S["fin_r"](i), sib)

    def fin_in(i):
        return remote(w.at[i, z, c], fs.at[i], S["fin_s"](i), S["fin_r"](i), sib)

    def put_piece(i, half, piece):
        cols = pl.ds(mult(2 * i + half, hc), hc)
        st[0] = piece[0].astype(f32).T
        st[1] = piece[1].astype(f32).T
        st[2] = piece[2].astype(f32)
        puts = (
            pltpu.make_async_copy(st.at[0], g_gate.at[:, cols], S["put"](0)),
            pltpu.make_async_copy(st.at[1], g_up.at[:, cols], S["put"](1)),
            pltpu.make_async_copy(st.at[2], g_down.at[cols], S["put"](2)),
        )
        for copy in puts:
            copy.start()
        for copy in puts:
            copy.wait()

    def rs_finish(i):
        fin_sib(i).start()
        put_piece(i, c, w.at[i, z, c])
        for tau in range(nz - 1):
            for direction in range(2):

                @pl.when(rs_valid(tau, direction))
                def _():
                    rs_line(i, tau, direction).wait_send()

        give_credit()

    def fin_finish(i):
        fin_sib(i).wait_send()
        fin_in(i).wait_recv()
        put_piece(i, 1 - c, fs.at[i])

    tile = min(256, tokens)

    def rows_pass(i, core):
        first = i == 0

        def rows_step(m, carry):
            local_rows = pl.ds(mult(m, tile), tile)
            rows = pl.ds(pl.multiple_of(core * tokens + m * tile, tile), tile)
            xm = x[rows, :]
            gate = dot(xm, w[i, :, :, 0].reshape(width, hc))
            up = dot(xm, w[i, :, :, 1].reshape(width, hc))
            dh = jnp.zeros((tile, hc), f32)
            for k in range(dps):
                dh = dh + dot_nt(ct[rows, k * hc : (k + 1) * hc], w[i, k // 2, k % 2, 2])
            sig = jax.nn.sigmoid(gate)
            act = gate * sig
            hidden = (act * up).astype(bf16)
            d_up = (dh * act).astype(bf16)
            d_gate = (dh * up * sig * (1.0 + gate * (1.0 - sig))).astype(bf16)
            ht[:, rows] = hidden.T
            dgt[:, rows] = d_gate.T
            dut[:, rows] = d_up.T
            mine_too = core is c
            for k in range(dps):
                cols = slice(k * hc, (k + 1) * hc)
                fwd = dot(hidden, w[i, k // 2, k % 2, 2])
                back = dot_nt(d_gate, w[i, k // 2, k % 2, 0]) + dot_nt(d_up, w[i, k // 2, k % 2, 1])
                if not first:
                    fwd = accp[rows, cols].astype(f32) + fwd
                    back = (accb if mine_too else acco)[local_rows, cols].astype(f32) + back
                accp[rows, cols] = fwd.astype(bf16)
                if mine_too:
                    accb[local_rows, cols] = back
                else:
                    acco[local_rows, cols] = back.astype(bf16)
            return carry

        lax.fori_loop(0, tokens // tile, rows_step, 0)

    def cols_pass(i):
        def cols_step(k, carry):
            cols = pl.ds(mult(k, hc), hc)
            xs = x[:, cols]
            chip, core = k // 2, k % 2
            w[i, chip, core, 0] = dot(dgt[...], xs).astype(bf16)
            w[i, chip, core, 1] = dot(dut[...], xs).astype(bf16)
            w[i, chip, core, 2] = dot(ht[...], ct[:, cols]).astype(bf16)
            return carry

        lax.fori_loop(0, dps, cols_step, 0)

    lane = lax.broadcasted_iota(jnp.int32, (1, LANES), 1)
    low_head = lane < HD
    low_half = lane % HD < HD // 2

    def turn(u, cos, sin):
        swapped = jnp.where(low_half, pltpu.roll(u, LANES - HD // 2, 1), pltpu.roll(u, HD // 2, 1))
        return u * cos + swapped * sin

    def turn_back(g, cos, sin):
        v = g * sin
        swapped = jnp.where(low_half, pltpu.roll(v, LANES - HD // 2, 1), pltpu.roll(v, HD // 2, 1))
        return g * cos + swapped

    def tables(rows, with_values):
        cos, sin = cosine[rows, :], sine[rows, :]
        if with_values:
            cos, sin = jnp.where(low_head, cos, 1.0), jnp.where(low_head, sin, 0.0)
        return cos, sin

    step = 32

    def norm_rows(src, dst, base, grad_sum):
        def body(m, carry):
            rows = pl.ds(mult(m, step), step)
            v = src[rows, :].astype(f32)
            scale = lax.rsqrt(jnp.mean(v * v, axis=-1, keepdims=True) + epsilon)
            v = v * scale
            dst[pl.ds(pl.multiple_of(base + m * step, step), step), :] = (v * gv[0:1, :]).astype(bf16)
            if grad_sum is None:
                return carry
            up = grad_sum(rows)
            return carry + jnp.sum(up * v, axis=0, keepdims=True)

        start = 0 if grad_sum is None else jnp.zeros((1, width), f32)
        return lax.fori_loop(0, tokens // step, body, start)

    chunks = aw_cols(hc) // LANES
    per_block = hc // LANES
    atile = min(256, tokens)

    def joined():
        def body(m, carry):
            rows = pl.ds(mult(m, atile), atile)
            src = pl.ds(pl.multiple_of(c * tokens + m * atile, atile), atile)
            xm = x[src, :]
            for j in range(3):
                block = dot(xm, aw[:, :, j].reshape(width, hc))
                for q in range(per_block):
                    index = j * per_block + q
                    cos, sin = tables(rows, index % 3 == 2)
                    u = block[:, q * LANES : (q + 1) * LANES]
                    qkvb[rows, index * LANES : (index + 1) * LANES] = turn(u, cos, sin).astype(bf16)
            return carry

        lax.fori_loop(0, tokens // atile, body, 0)

    row_id = lax.broadcasted_iota(jnp.int32, (SEQ, SEQ), 0)
    col_id = lax.broadcasted_iota(jnp.int32, (SEQ, SEQ), 1)
    keep = row_id >= col_id
    inv_root = 1.0 / math.sqrt(HD)

    def doubled(rows, base):
        kv = qkvb[rows, pl.ds(pl.multiple_of(base + GROUPS * HD, LANES), LANES)].astype(f32)
        other = pltpu.roll(kv, HD, 1)
        kk = jnp.where(low_head, kv, other).astype(bf16)
        vv = jnp.where(low_head, other, kv).astype(bf16)
        return kk, vv

    def softmax(qm, kk):
        scores = jnp.where(keep, dot_nt(qm, kk) * inv_root, masked_score)
        e = jnp.exp(scores - jnp.max(scores, axis=-1, keepdims=True))
        return e * (1.0 / jnp.sum(e, axis=-1, keepdims=True))

    def place(n):
        s, h = n // kv_local, n % kv_local
        rows = pl.ds(mult(s, SEQ), SEQ)
        return rows, h * head_cols, h * GROUPS * HD

    def heads_forward():
        def body(n, carry):
            rows, base, qbase = place(n)
            kk, vv = doubled(rows, base)
            for pair in range(GROUPS // 2):
                qp = qkvb[rows, pl.ds(pl.multiple_of(base + pair * LANES, LANES), LANES)]
                halves = []
                for half in range(2):
                    mask = low_head if half == 0 else ~low_head
                    qm = jnp.where(mask, qp.astype(f32), 0.0).astype(bf16)
                    halves.append(dot(softmax(qm, kk).astype(bf16), vv))
                att[rows, pl.ds(pl.multiple_of(qbase + pair * LANES, LANES), LANES)] = jnp.where(
                    low_head, halves[0], halves[1]
                ).astype(bf16)
            return carry

        lax.fori_loop(0, seqs * kv_local, body, 0)

    def heads_backward():
        def body(n, carry):
            rows, base, qbase = place(n)
            kk, vv = doubled(rows, base)
            dkk = jnp.zeros((SEQ, LANES), f32)
            dvv = jnp.zeros((SEQ, LANES), f32)
            cos, sin = tables(rows, False)
            for pair in range(GROUPS // 2):
                cols = pl.ds(pl.multiple_of(base + pair * LANES, LANES), LANES)
                acols = pl.ds(pl.multiple_of(qbase + pair * LANES, LANES), LANES)
                qp = qkvb[rows, cols].astype(f32)
                dp = datt[rows, acols].astype(f32)
                prod = dp * att[rows, acols].astype(f32)
                halves = []
                for half in range(2):
                    mask = low_head if half == 0 else ~low_head
                    qm = jnp.where(mask, qp, 0.0).astype(bf16)
                    dm = jnp.where(mask, dp, 0.0).astype(bf16)
                    probs = softmax(qm, kk)
                    delta = jnp.sum(jnp.where(mask, prod, 0.0), axis=-1, keepdims=True)
                    ds = (probs * (dot_nt(dm, vv) - delta) * inv_root).astype(bf16)
                    halves.append(dot(ds, kk))
                    dkk = dkk + dot(ds.T, qm)
                    dvv = dvv + dot(probs.astype(bf16).T, dm)
                dq = jnp.where(low_head, halves[0], halves[1])
                qkvb[rows, cols] = turn_back(dq, cos, sin).astype(bf16)
            dkk = dkk + pltpu.roll(dkk, HD, 1)
            dvv = dvv + pltpu.roll(dvv, HD, 1)
            cos, sin = tables(rows, True)
            qkvb[rows, pl.ds(pl.multiple_of(base + GROUPS * HD, LANES), LANES)] = turn_back(
                jnp.where(low_head, dkk, dvv), cos, sin
            ).astype(bf16)
            return carry

        lax.fori_loop(0, seqs * kv_local, body, 0)

    def out_weight(k):
        return aw[k // 2, k % 2, 3:5].reshape(2 * hc, hc)

    def attention_partial():
        def body(k, carry):
            cols = pl.ds(mult(k, hc), hc)
            rsb[:, cols] = dot(att[...], out_weight(k)).astype(bf16)
            return carry

        lax.fori_loop(0, dps, body, 0)

    square = nt == 4
    xp, yp, dg = t ^ 1, t ^ 2, t ^ 3
    half = ts // 2

    def part_rows(base, index, upper):
        return pl.ds(pl.multiple_of(base + index * ts + upper * half, half), half)

    def slice_rows(base, index):
        return pl.ds(pl.multiple_of(base + index * ts, ts), ts)

    def reduce_copy(src, base, land, which, n):
        rows = (
            part_rows(base, xp, 0),
            part_rows(base, dg, 0),
            part_rows(base, yp, 1),
            part_rows(base, dg, 1),
            part_rows(base, yp, 0),
            part_rows(base, xp, 1),
        )[n]
        to = (xp, xp, yp, yp, yp, xp)[n]
        return remote(
            src.at[rows],
            land.at[pl.ds(n * half, half)],
            S["ps_s"](which, n),
            S["ps_r"](which, n),
            (d, to),
        )

    def reduce_direct(src, base, land, which, k, arriving):
        frm = source(k)
        return remote(
            src.at[slice_rows(base, peer(k))],
            land.at[slot(frm if arriving else t)],
            S["ps_s"](which, k),
            S["ps_r"](which, k),
            (d, frm if arriving else peer(k)),
        )

    def reduce_start(src, base, land, which):
        if square:
            for n in range(4):
                reduce_copy(src, base, land, which, n).start()
        else:
            for k in range(nt - 1):
                reduce_direct(src, base, land, which, k, False).start()

    def reduce_mid(src, base, land, which):
        if not square:
            return
        for n, index, upper in ((1, yp, 0), (3, xp, 1)):
            reduce_copy(src, base, land, which, n).wait_recv()
            rows = part_rows(base, index, upper)
            both = src[rows, :].astype(f32) + land[n * half : (n + 1) * half, :].astype(f32)
            src[rows, :] = both.astype(bf16)
            reduce_copy(src, base, land, which, 4 if n == 1 else 5).start()

    def reduce_wait(src, base, land, which):
        if square:
            for n in (0, 2, 4, 5):
                reduce_copy(src, base, land, which, n).wait_recv()
        else:
            for k in range(nt - 1):
                reduce_direct(src, base, land, which, k, True).wait_recv()

    def reduce_end(src, base, land, which):
        if square:
            for n in range(6):
                reduce_copy(src, base, land, which, n).wait_send()
        else:
            for k in range(nt - 1):
                reduce_direct(src, base, land, which, k, False).wait_send()

    def summed(src, base, land, m):
        total = src[pl.ds(pl.multiple_of(base + t * ts + m * step, step), step), :].astype(f32)
        if square:
            upper = m // (half // step)
            inner = (m % (half // step)) * step
            for first in (2 * upper * half, (4 + upper) * half):
                total = total + land[pl.ds(pl.multiple_of(first + inner, step), step), :].astype(f32)
        else:
            for k in range(nt - 1):
                rows = pl.ds(pl.multiple_of(source(k) * ts + m * step, step), step)
                total = total + land[rows, :].astype(f32)
        return total

    def spread_copy(src, src_base, dst, dst_base, which, n):
        index, upper, to = (
            (t, 0, xp),
            (t, 1, xp),
            (t, 1, yp),
            (t, 0, yp),
            (xp, 0, yp),
            (yp, 1, xp),
        )[n]
        from_rows = part_rows(src_base, t, upper) if n < 4 else part_rows(dst_base, index, upper)
        return remote(
            (src if n < 4 else dst).at[from_rows],
            dst.at[part_rows(dst_base, index, upper)],
            S["ga_s"](which, n),
            S["ga_r"](which, n),
            (d, to),
        )

    def spread_arrive(src, src_base, dst, dst_base, which, n):
        index, upper, frm = (
            (xp, 0, xp),
            (xp, 1, xp),
            (yp, 1, yp),
            (yp, 0, yp),
            (dg, 0, yp),
            (dg, 1, xp),
        )[n]
        return remote(
            src.at[part_rows(src_base, t, upper)],
            dst.at[part_rows(dst_base, index, upper)],
            S["ga_s"](which, n),
            S["ga_r"](which, n),
            (d, frm),
        )

    def spread_direct(src, src_base, dst, dst_base, which, k, arriving):
        frm = source(k)
        return remote(
            src.at[slice_rows(src_base, t)],
            dst.at[slice_rows(dst_base, frm if arriving else t)],
            S["ga_s"](which, k),
            S["ga_r"](which, k),
            (d, frm if arriving else peer(k)),
        )

    def spread_start(*args):
        if square:
            for n in range(4):
                spread_copy(*args, n).start()
        else:
            for k in range(nt - 1):
                spread_direct(*args, k, False).start()

    def spread_mid(*args):
        if square:
            for n, onward in ((0, 4), (2, 5)):
                spread_arrive(*args, n).wait_recv()
                spread_copy(*args, onward).start()

    def spread_wait(*args):
        if square:
            for n in (1, 3, 4, 5):
                spread_arrive(*args, n).wait_recv()
        else:
            for k in range(nt - 1):
                spread_direct(*args, k, True).wait_recv()

    def spread_end(*args):
        if square:
            for n in range(6):
                spread_copy(*args, n).wait_send()
        else:
            for k in range(nt - 1):
                spread_direct(*args, k, False).wait_send()

    q_tick(0)
    for i in range(nch):
        for kind in range(3):
            own_copy(i, kind).start()
            sib_copy(i, kind).start()
    cot_own = pltpu.make_async_copy(cot, ct.at[core_rows(c)], S["cot"](0))
    cot_sib = remote(cot, ct.at[core_rows(c)], S["cot"](1), S["cot"](2), sib)
    cot_in = remote(cot, ct.at[core_rows(1 - c)], S["cot"](1), S["cot"](2), sib)
    cot_own.start()
    cot_sib.start()
    quarter = HD // 2
    exponent = lax.broadcasted_iota(jnp.int32, (quarter, 1), 0).astype(f32) * (2.0 / HD)
    angles = jnp.exp(exponent * -math.log(rope_base)) * pos[...].astype(f32)
    cos_rows, sin_rows = jnp.cos(angles), jnp.sin(angles)
    cosine[...] = jnp.concatenate([cos_rows] * (LANES // quarter), axis=0).T
    sine[...] = jnp.concatenate([-sin_rows, sin_rows] * (LANES // HD), axis=0).T
    for s in range(1, nz):
        if s == nz - 1:
            ag_tick(0, 0)
        q_tick(s)
    if nz == 1:
        ag_tick(0, 0)
    q_finish()
    for k in range(dps):
        gv[:, k * hc : (k + 1) * hc] = gw[k // 2, k % 2].astype(f32)
    tok_all.wait()
    norm_rows(p2, x, c * tokens, None)
    joined()
    heads_forward()
    if nz > 1:
        ag_tick(0, 1)
    attention_partial()
    first_sum = (rsb, 0, p1, 0)
    reduce_start(*first_sum)
    if nz > 2:
        ag_tick(0, 2)
    reduce_mid(*first_sum)
    if nz > 3:
        ag_tick(1, 0)
    reduce_wait(*first_sum)
    mine = half_rows(c, t)

    def second_norm(m, carry):
        rows = pl.ds(mult(m, step), step)
        trow = pl.ds(pl.multiple_of(t * ts + m * step, step), step)
        total = p2[trow, :].astype(f32) + summed(rsb, 0, p1, m)
        resid[rows, :] = total
        scale = lax.rsqrt(jnp.mean(total * total, axis=-1, keepdims=True) + epsilon)
        x[pl.ds(pl.multiple_of(c * tokens + t * ts + m * step, step), step), :] = (
            total * scale * gv[1:2, :]
        ).astype(bf16)
        return carry

    lax.fori_loop(0, ts // step, second_norm, 0)
    x_spread = (x, c * tokens, x, c * tokens, 3)

    def xs_index(k):
        if square:
            return (t, xp, yp, dg)[k]
        return lax.rem(t - k + nt, nt)

    def xs_copy(k):
        rows = half_rows(c, xs_index(k))
        return remote(x.at[rows], x.at[rows], S["xs_s"](k), S["xs_r"](k), sib)

    def xs_in(k):
        rows = half_rows(1 - c, xs_index(k))
        return remote(x.at[rows], x.at[rows], S["xs_s"](k), S["xs_r"](k), sib)

    spread_start(*x_spread)
    xs_copy(0).start()
    spread_mid(*x_spread)
    if square:
        spread_arrive(*x_spread, 1).wait_recv()
        xs_copy(1).start()
        spread_arrive(*x_spread, 3).wait_recv()
        xs_copy(2).start()
    for s in range(3, nz):
        ag_tick(0, s)
    ag_finish(0)
    if nz <= 3:
        ag_tick(1, 0)
    if square:
        for n in (4, 5):
            spread_arrive(*x_spread, n).wait_recv()
        xs_copy(3).start()
    else:
        for k in range(nt - 1):
            spread_direct(*x_spread, k, True).wait_recv()
            xs_copy(k + 1).start()
    cot_own.wait()
    cot_in.wait_recv()
    for k in range(nt):
        xs_in(k).wait_recv()

    last = nch - 1
    other = (1 - c) * tokens
    for i in range(last):
        if i > 0:
            ag_tick(i + 1, 0)
        rows_pass(i, 1 - c)
        rows_pass(i, c)
        cols_pass(i)
        if i > 0:
            take_credit()
        rs_tick(i, 0)
        for s in range(1, nz):
            ag_tick(i + 1, s)
            rs_tick(i, s)
        ag_finish(i + 1)
        if i > 0:
            fin_finish(i - 1)
        rs_finish(i)

    def sib_b(k):
        return remote(acco.at[slot(k)], sbr_b.at[slot(k)], S["sb_s"](0, k), S["sb_r"](0, k), sib)

    def sib_p(k):
        return remote(
            accp.at[half_rows(1 - c, k)], sbr_p.at[slot(k)], S["sb_s"](1, k), S["sb_r"](1, k), sib
        )

    for u in range(nz):
        for part in range(2):
            q_sib(part, u).wait_send()
    spread_end(*x_spread)
    reduce_end(*first_sum)
    for k in range(nt):
        xs_copy(k).wait_send()
    rows_pass(last, 1 - c)
    for k in range(nt):
        sib_b(k).start()
    rows_pass(last, c)
    for k in range(nt):
        sib_b(k).wait_recv()

    def pair_b(m, carry):
        rows = pl.ds(mult(m, step), step)
        rsb[rows, :] = (accb[rows, :] + sbr_b[rows, :].astype(f32)).astype(bf16)
        return carry

    lax.fori_loop(0, tokens // step, pair_b, 0)
    back_sum = (rsb, 0, p2, 1)
    reduce_start(*back_sum)
    cols_pass(last)
    if last > 0:
        take_credit()
    rs_tick(last, 0)
    for k in range(nt):
        sib_p(k).start()
    reduce_mid(*back_sum)
    if nz > 1:
        rs_tick(last, 1)
    reduce_wait(*back_sum)

    def second_back(m, carry):
        rows = pl.ds(mult(m, step), step)
        place_ = pl.ds(pl.multiple_of(c * tokens + t * ts + m * step, step), step)
        up = summed(rsb, 0, p2, m)
        v = resid[rows, :]
        scale = lax.rsqrt(jnp.mean(v * v, axis=-1, keepdims=True) + epsilon)
        weighted = up * gv[1:2, :]
        inner = jnp.mean(weighted * v, axis=-1, keepdims=True)
        grad = ct[place_, :].astype(f32) + scale * weighted - v * (scale * scale * scale) * inner
        accb[rows, :] = grad
        x[place_, :] = grad.astype(bf16)
        return carry + jnp.sum(up * v * scale, axis=0, keepdims=True)

    gain_two = lax.fori_loop(0, ts // step, second_back, jnp.zeros((1, width), f32))
    rg_spread = (x, c * tokens, x, c * tokens, 0)
    spread_start(*rg_spread)
    spread_mid(*rg_spread)
    if nz > 2:
        rs_tick(last, 2)
    reduce_end(*back_sum)
    for k in range(nt):
        sib_p(k).wait_recv()

    def pair_p(m, carry):
        rows = pl.ds(mult(m, step), step)
        here = pl.ds(pl.multiple_of(c * tokens + m * step, step), step)
        rsb[rows, :] = (accp[here, :].astype(f32) + sbr_p[rows, :].astype(f32)).astype(bf16)
        return carry

    lax.fori_loop(0, tokens // step, pair_p, 0)

    spread_wait(*rg_spread)
    out_sum = (rsb, 0, p1, 2)
    reduce_start(*out_sum)

    def d_attended(m, carry):
        rows = pl.ds(mult(m, atile), atile)
        src = pl.ds(pl.multiple_of(c * tokens + m * atile, atile), atile)
        for j in range(2):
            total = jnp.zeros((atile, hc), f32)
            for k in range(dps):
                total = total + dot_nt(x[src, k * hc : (k + 1) * hc], aw[k // 2, k % 2, 3 + j])
            datt[rows, j * hc : (j + 1) * hc] = total.astype(bf16)
        for j in range(2):
            (ht, dgt)[j][:, rows] = att[rows, j * hc : (j + 1) * hc].T
        return carry

    lax.fori_loop(0, tokens // atile, d_attended, 0)

    def out_grads(k, carry):
        xs = x[core_rows(c), pl.ds(mult(k, hc), hc)]
        for j in range(2):
            aw[k // 2, k % 2, 3 + j] = dot((ht, dgt)[j][:, :tokens], xs).astype(bf16)
        return carry

    lax.fori_loop(0, dps, out_grads, 0)

    def a_src(part, u, core):
        return (aw.at[u, core, 3:5], aw.at[u, core, 0:3], gg.at[u, core])[part]

    def a_sib_ref(part):
        return (w.at[0, :, 1, 0:2], w.at[0, :, 0], gsib)[part]

    def a_sib(part):
        src = (aw.at[:, 1 - c, 3:5], aw.at[:, 1 - c, 0:3], gg.at[:, 1 - c])[part]
        return remote(src, a_sib_ref(part), S["as_s"](part), S["as_r"](part), sib)

    def a_land(part, direction, tau):
        line = (ru, rd)[direction]
        return (line.at[tau, 1, 0:2], line.at[tau, 0], (gru, grd)[direction].at[tau])[part]

    def a_line(part, tau, direction):
        return remote(
            a_src(part, rs_owner(tau, direction), c),
            a_land(part, direction, tau),
            S["ar_s"](part, direction, tau),
            S["ar_r"](part, direction, tau),
            (above, below)[direction],
        )

    def a_add(part, owner, got):
        if part == 2:
            gg[owner, c] = gg[owner, c] + got[...]
            return
        base, count = ((3, 2), (0, 3))[part]
        for j in range(count):
            both = aw[owner, c, base + j].astype(f32) + got[j].astype(f32)
            aw[owner, c, base + j] = both.astype(bf16)

    def a_pair(part):
        a_sib(part).wait_recv()

        def body(u, carry):
            a_add(part, u, (w.at[0, u, 1, 0:2], w.at[0, u, 0], gsib.at[u])[part])
            return carry

        lax.fori_loop(0, nz, body, 0)

    def a_tick(part, tau):
        for direction in range(2):
            if tau > 0:

                @pl.when(rs_valid(tau, direction) & (has_below, has_above)[direction])
                def _():
                    owner = rs_owner(tau, direction)
                    remote(
                        a_src(part, owner, c),
                        a_land(part, direction, tau - 1),
                        S["ar_s"](part, direction, tau - 1),
                        S["ar_r"](part, direction, tau - 1),
                        (below, above)[direction],
                    ).wait_recv()
                    a_add(part, owner, a_land(part, direction, tau - 1))

            if tau < nz - 1:

                @pl.when(rs_valid(tau, direction))
                def _():
                    a_line(part, tau, direction).start()

    def a_finish(part):
        a_sib(part).wait_send()
        for tau in range(nz - 1):
            for direction in range(2):

                @pl.when(rs_valid(tau, direction))
                def _():
                    a_line(part, tau, direction).wait_send()

    a_sib(0).start()
    tok_again = pltpu.make_async_copy(tok, sbr_b, S["tok"](1))
    tok_again.start()
    for s in range(3, nz):
        rs_tick(last, s)
    if nch > 1:
        fin_finish(last - 1)
    rs_finish(last)
    take_credit()
    a_pair(0)
    a_tick(0, 0)
    heads_backward()

    def attn_back(k, carry):
        total = jnp.zeros((tokens, hc), f32)
        for j in range(3):
            total = total + dot_nt(qkvb[:, j * hc : (j + 1) * hc], aw[k // 2, k % 2, j])
        x[pl.ds(mult(1 - c, tokens), tokens), pl.ds(mult(k, hc), hc)] = total.astype(bf16)
        return carry

    lax.fori_loop(0, dps, attn_back, 0)
    tail_sum = (x, other, p2, 3)
    reduce_start(*tail_sum)
    reduce_mid(*out_sum)
    if nz > 1:
        a_tick(0, 1)
    tok_again.wait()

    def own_back(rows):
        return x[pl.ds(pl.multiple_of(other + rows.start, step), step), :].astype(f32)

    gain_one = norm_rows(sbr_b, sbr_p, 0, own_back)
    for k in range(dps):
        cols = slice(k * hc, (k + 1) * hc)
        gg[k // 2, k % 2] = jnp.concatenate(
            [gain_one[:, cols], gain_two[:, cols], jnp.zeros((6, hc), f32)], axis=0
        )
    a_sib(2).start()
    for m in range(tokens // atile):
        for j in range(3):
            (ht, dgt, dut)[j][:, tokens + m * atile : tokens + (m + 1) * atile] = qkvb[
                m * atile : (m + 1) * atile, j * hc : (j + 1) * hc
            ].T

    def qkv_grads(k, carry):
        xs = sbr_p[:, pl.ds(mult(k, hc), hc)]
        for j in range(3):
            aw[k // 2, k % 2, j] = dot((ht, dgt, dut)[j][:, tokens:], xs).astype(bf16)
        return carry

    lax.fori_loop(0, dps, qkv_grads, 0)
    a_sib(1).start()
    if nz > 2:
        a_tick(0, 2)
    a_pair(1)
    a_pair(2)
    a_tick(1, 0)
    a_tick(2, 0)
    for s in range(3, nz):
        a_tick(0, s)

    reduce_mid(*tail_sum)
    reduce_wait(*out_sum)

    def finish_output(m, carry):
        rows = pl.ds(mult(m, step), step)
        where = pl.ds(pl.multiple_of(c * tokens + t * ts + m * step, step), step)
        accp[where, :] = (resid[rows, :] + summed(rsb, 0, p1, m)).astype(bf16)
        return carry

    lax.fori_loop(0, ts // step, finish_output, 0)
    out_spread = (accp, c * tokens, out, 0, 1)
    spread_start(*out_spread)
    put_out = pltpu.make_async_copy(accp.at[mine], out.at[slot(t)], S["loc"](0))
    put_out.start()

    reduce_wait(*tail_sum)
    for k in range(nt):
        sib_p(k).wait_send()
    theirs = half_rows(1 - c, t)

    def finish_tokens(m, carry):
        rows = pl.ds(mult(m, step), step)
        up = summed(x, other, p2, m)
        v = sbr_b[pl.ds(pl.multiple_of(t * ts + m * step, step), step), :].astype(f32)
        scale = lax.rsqrt(jnp.mean(v * v, axis=-1, keepdims=True) + epsilon)
        weighted = up * gv[0:1, :]
        inner = jnp.mean(weighted * v, axis=-1, keepdims=True)
        grad = accb[rows, :] + scale * weighted - v * (scale * scale * scale) * inner
        accp[pl.ds(pl.multiple_of(other + t * ts + m * step, step), step), :] = grad.astype(bf16)
        return carry

    lax.fori_loop(0, ts // step, finish_tokens, 0)
    tok_spread = (accp, other, dtok, 0, 2)
    spread_start(*tok_spread)
    put_tok = pltpu.make_async_copy(accp.at[theirs], dtok.at[slot(t)], S["loc"](1))
    put_tok.start()
    spread_mid(*out_spread)
    spread_mid(*tok_spread)
    fin_finish(last)
    for s in range(1, nz):
        a_tick(2, s)
        a_tick(1, s)

    def gain_copy(k):
        return remote(gg.at[z, c], gt.at[t], S["gg_s"](k), S["gg_r"](k), (d, peer(k)))

    def gain_in(k):
        return remote(gg.at[z, c], gt.at[source(k)], S["gg_s"](k), S["gg_r"](k), (d, source(k)))

    for k in range(nt - 1):
        gain_copy(k).start()
    gt[t] = gg[z, c]

    base = ts
    for j in range(3):
        accb[base : base + hc, j * hc : (j + 1) * hc] = aw[z, c, j].astype(f32).T
    for j in range(2):
        accb[base : base + hc, (3 + j) * hc : (4 + j) * hc] = aw[z, c, 3 + j].astype(f32)
    put_qkv = pltpu.make_async_copy(accb.at[base : base + hc, 0 : 3 * hc], g_qkv, S["loc"](2))
    put_o = [
        pltpu.make_async_copy(
            accb.at[base : base + hc, (3 + j) * hc : (4 + j) * hc],
            g_out.at[j * hc : (j + 1) * hc],
            S["loc"](3 + j),
        )
        for j in range(2)
    ]
    put_qkv.start()
    for copy in put_o:
        copy.start()
    for k in range(nt - 1):
        gain_in(k).wait_recv()
    total = gt[0]
    for k in range(1, nt):
        total = total + gt[k]
    g_gains[...] = total

    for i in range(nch):
        for kind in range(3):
            sib_copy(i, kind).wait_send()
    cot_sib.wait_send()
    for part in range(3):
        a_finish(part)
    for k in range(nt - 1):
        gain_copy(k).wait_send()
    for k in range(nt):
        sib_b(k).wait_send()
    reduce_end(*out_sum)
    reduce_end(*tail_sum)
    spread_wait(*out_spread)
    spread_wait(*tok_spread)
    for args in (rg_spread, out_spread, tok_spread):
        spread_end(*args)
    put_out.wait()
    put_tok.wait()
    put_qkv.wait()
    for copy in put_o:
        copy.wait()


def aw_cols(shard):
    return 3 * shard


def layer(tokens, cotangent, weights, positions, gain_a, gain_f, nz, nt):
    count, width = tokens.shape
    hc, hid = weights[2].shape
    nch = hid // (2 * hc)
    ts = count // nt
    sizes = (nz, nt, nch, count, width, hc)
    sems, _ = semaphores(nz, nt, nch)
    V = pltpu.VMEM
    recv = (nz - 1, 2, 3, hc, hc)
    S = jax.ShapeDtypeStruct
    return pl.pallas_call(
        functools.partial(layer_kernel, sizes),
        out_shape=(
            S((count, width), bf16),
            S((count, width), bf16),
            S((hc, 3 * hc), f32),
            S((2 * hc, hc), f32),
            S((hc, hid), f32),
            S((hc, hid), f32),
            S((hid, hc), f32),
            S((8, hc), f32),
        ),
        in_specs=[HBM] * 7 + [VMEM] * 3,
        out_specs=(HBM, HBM, HBM, HBM, HBM, HBM, HBM, VMEM),
        scratch_shapes=[
            V((nch, nz, 2, 3, hc, hc), bf16),
            V(recv, bf16),
            V(recv, bf16),
            V((2 * count, width), bf16),
            V((2 * count, width), bf16),
            V((2 * count, width), bf16),
            V((count, width), f32),
            V((count, width), bf16),
            V((hc, 2 * count), bf16),
            V((hc, 2 * count), bf16),
            V((hc, 2 * count), bf16),
            V((ts, width), f32),
            V((count, width), bf16),
            V((count, width), bf16),
            V((count, width), bf16),
            V((count, width), bf16),
            V((count, width), bf16),
            V((nz, 2, 5, hc, hc), bf16),
            V((count, 3 * hc), bf16),
            V((count, 2 * hc), bf16),
            V((count, 2 * hc), bf16),
            V((nch, 3, hc, hc), bf16),
            V((3, hc, hc), f32),
            V((nz, 2, 16, hc), bf16),
            V((16, width), f32),
            V((nz, 2, 8, hc), f32),
            V((nz, 8, hc), f32),
            V((nz - 1, 8, hc), f32),
            V((nz - 1, 8, hc), f32),
            V((nt, 8, hc), f32),
            V((count, LANES), f32),
            V((count, LANES), f32),
            pltpu.SemaphoreType.DMA((sems.count,)),
            pltpu.SemaphoreType.REGULAR((2,)),
        ],
        compiler_params=pltpu.CompilerParams(
            collective_id=0, has_side_effects=True, vmem_limit_bytes=63 * 2**20
        ),
        name="layer",
    )(tokens, cotangent, *weights, positions, gain_a, gain_f)


def copy_kernel(count, parts, *refs):
    sources, gains = refs[:count], refs[count]
    results, gain_outs = refs[count + 1 : 2 * count + 1], refs[2 * count + 1 : 2 * count + 3]
    held, sem = refs[2 * count + 3 : 3 * count + 3], refs[-1]
    loads, stores = [], []
    for n in range(count):
        rows = sources[n].shape[0] // parts
        for k in range(parts):
            at = pl.ds(k * rows, rows)
            place = sem.at[n * parts + k]
            loads.append(pltpu.make_async_copy(sources[n].at[at], held[n].at[at], place))
            stores.append(pltpu.make_async_copy(held[n].at[at], results[n].at[at], place))
    for copy in loads:
        copy.start()
    for n in range(2):
        gain_outs[n][...] = gains[n, :]
    for load, store in zip(loads, stores):
        load.wait()
        store.start()
    for copy in stores:
        copy.wait()


def copied(arrays, gains):
    count, parts = len(arrays), 2
    shapes = [jax.ShapeDtypeStruct(a.shape, a.dtype) for a in arrays]
    return pl.pallas_call(
        functools.partial(copy_kernel, count, parts),
        out_shape=shapes + [jax.ShapeDtypeStruct(gains.shape[1:], f32)] * 2,
        in_specs=[HBM] * count + [VMEM],
        out_specs=[HBM] * count + [VMEM] * 2,
        scratch_shapes=[pltpu.VMEM(a.shape, a.dtype) for a in arrays]
        + [pltpu.SemaphoreType.DMA((count * parts,))],
        compiler_params=pltpu.CompilerParams(vmem_limit_bytes=60 * 2**20),
        name="results",
    )(*arrays, gains)


def local(tokens, positions, w_qkv, w_out, w_gate, w_up, w_down, gain_attn, gain_ffn, cotangent):
    nz = lax.axis_size("dp") // 2
    nt = lax.axis_size("tensor")
    results = layer(
        tokens,
        cotangent,
        (w_qkv, w_out, w_gate, w_up, w_down),
        positions.reshape(1, -1),
        gain_attn,
        gain_ffn,
        nz,
        nt,
    )
    return tuple(copied(results[:-1], results[-1]))


def solution(mesh):
    return jax.shard_map(
        local,
        mesh=mesh,
        in_specs=(
            P("dp", None),
            P("dp"),
            P("dp", "tensor"),
            P("tensor", "dp"),
            P("dp", "tensor"),
            P("dp", "tensor"),
            P("tensor", "dp"),
            P("dp"),
            P("dp"),
            P("dp", None),
        ),
        out_specs=(
            P("dp", None),
            P("dp", None),
            P("dp", "tensor"),
            P("tensor", "dp"),
            P("dp", "tensor"),
            P("dp", "tensor"),
            P("tensor", "dp"),
            P("dp"),
            P("dp"),
        ),
        check_vma=False,
    )
```

```python
import functools
import math

import jax
import jax.numpy as jnp
from jax import lax
from jax.experimental import pallas as pl
from jax.experimental.pallas import tpu as pltpu
from jax.sharding import PartitionSpec as P

HEADS = 32
KV_HEADS = 8
HD = 64
SEQ = 256
GROUPS = HEADS // KV_HEADS
LANES = 128

epsilon = 1e-05
rope_base = 500000.0
masked_score = -1e30

MESH = pl.DeviceIdType.MESH
HBM = pl.BlockSpec(memory_space=pl.ANY)
VMEM = pl.BlockSpec(memory_space=pltpu.VMEM)
bf16 = jnp.bfloat16
f32 = jnp.float32
NT_DIMS = (((1,), (1,)), ((), ()))


def remote(src, dst, send, recv, device):
    return pltpu.make_async_remote_copy(
        src_ref=src, dst_ref=dst, send_sem=send, recv_sem=recv, device_id=device, device_id_type=MESH
    )


def mult(value, factor):
    return pl.multiple_of(value * factor, factor)


def dot(a, b):
    return jnp.dot(a, b, preferred_element_type=f32)


def dot_nt(a, b):
    return lax.dot_general(a, b, NT_DIMS, preferred_element_type=f32)


def sums_plan(nz, nch):
    last = nch - 1
    if (nz, nch) != (4, 4):
        plan = {}
        for r in range(last + nz):
            hops = [(i, r - i, "all") for i in range(nch) if 0 <= r - i < nz]
            place = ("after", r) if r <= last else 1
            plan.setdefault(place, []).extend(hops)
        return plan
    return {
        ("after", 0): [(0, 0, "all")],
        ("middle", 0): [(0, 1, "all")],
        ("before", 1): [(0, 2, "inner")],
        ("after", 1): [(1, 0, "all")],
        ("before", 2): [(0, 3, "mid"), (1, 1, "all")],
        ("after", 2): [(2, 0, "all")],
        ("before", 3): [("edge", 0), (1, 2, "inner"), (2, 1, "all")],
        ("after", 3): [(3, 0, "all")],
        1: [(0, 3, "end"), ("edge", 1), (1, 3, "mid"), (2, 2, "inner"), (3, 1, "all")],
        2: [(1, 3, "end"), ("edge", 2), (2, 3, "mid"), (3, 2, "inner")],
        3: [(2, 3, "end"), ("edge", 3), (3, 3, "mid")],
        4: [(3, 3, "end")],
    }


class Sems:
    def __init__(self):
        self.count = 0
        self.ref = None

    def take(self, *dims):
        base = self.count
        self.count += math.prod(dims)

        def at(*index):
            flat = 0
            for size, place in zip(dims, index):
                flat = flat * size + place
            return self.ref.at[base + flat]

        return at


def semaphores(nz, nt, nch):
    s = Sems()
    names = {
        "own": s.take(nch, 3),
        "sib_s": s.take(nch, 3),
        "sib_r": s.take(nch, 3),
        "ag_s": s.take(nch, 2, nz),
        "ag_r": s.take(nch, 2, nz),
        "qown": s.take(5),
        "qa_s": s.take(2, 2, nz),
        "qa_r": s.take(2, 2, nz),
        "qs_s": s.take(2, nz),
        "qs_r": s.take(2, nz),
        "rs_s": s.take(2, nz),
        "rs_r": s.take(2, nz),
        "as_s": s.take(3),
        "as_r": s.take(3),
        "ar_s": s.take(3, 2, nz),
        "ar_r": s.take(3, 2, nz),
        "fin_s": s.take(nch),
        "fin_r": s.take(nch),
        "put": s.take(8),
        "cot": s.take(3),
        "tok": s.take(3),
        "ps_s": s.take(4, max(nt, 6)),
        "ps_r": s.take(4, max(nt, 6)),
        "xs_s": s.take(nt),
        "xs_r": s.take(nt),
        "sb_s": s.take(2, nt),
        "sb_r": s.take(2, nt),
        "ga_s": s.take(4, max(nt, 6)),
        "ga_r": s.take(4, max(nt, 6)),
        "gg_s": s.take(nt),
        "gg_r": s.take(nt),
        "loc": s.take(5),
    }
    return s, names


def layer_kernel(
    sizes,
    tok,
    cot,
    w_qkv,
    w_out,
    w_gate,
    w_up,
    w_down,
    pos,
    gain_a,
    gain_f,
    out,
    dtok,
    g_qkv,
    g_out,
    g_gate,
    g_up,
    g_down,
    g_gains,
    w,
    ru,
    rd,
    x,
    ct,
    accp,
    accb,
    acco,
    ht,
    dgt,
    dut,
    resid,
    p1,
    p2,
    sbr_b,
    sbr_p,
    rsb,
    aw,
    qkvb,
    att,
    datt,
    fs,
    st,
    gw,
    gv,
    gg,
    gsib,
    gru,
    grd,
    gt,
    cosine,
    sine,
    sem_ref,
    credit,
):
    nz, nt, nch, tokens, width, hc = sizes
    sems, S = semaphores(nz, nt, nch)
    sems.ref = sem_ref
    ts = tokens // nt
    dps = 2 * nz
    d = lax.axis_index("dp")
    t = lax.axis_index("tensor")
    z = d // 2
    c = d % 2
    sib = (2 * z + 1 - c, t)
    above = (d + 2, t)
    below = (d - 2, t)
    has_above = z < nz - 1
    has_below = z > 0
    seqs = tokens // SEQ
    kv_local = aw_cols(hc) // ((GROUPS + 2) * HD)
    head_cols = (GROUPS + 2) * HD

    def peer(k):
        return lax.rem(t + 1 + k, nt)

    def source(k):
        return lax.rem(t - 1 - k + nt, nt)

    barrier = pltpu.get_barrier_semaphore()
    for k in range(nt - 1):
        pl.semaphore_signal(barrier, inc=1, device_id=(d, peer(k)), device_id_type=MESH)
    pl.semaphore_signal(barrier, inc=1, device_id=sib, device_id_type=MESH)

    @pl.when(has_below)
    def _():
        pl.semaphore_signal(barrier, inc=1, device_id=below, device_id_type=MESH)

    @pl.when(has_above)
    def _():
        pl.semaphore_signal(barrier, inc=1, device_id=above, device_id_type=MESH)

    neighbours = jnp.where(has_below, 1, 0) + jnp.where(has_above, 1, 0)
    pl.semaphore_wait(barrier, nt + neighbours)

    def slot(index):
        return pl.ds(mult(index, ts), ts)

    def core_rows(core):
        return pl.ds(mult(core, tokens), tokens)

    def half_rows(core, index):
        return pl.ds(pl.multiple_of(core * tokens + index * ts, ts), ts)

    def ffn_source(i, core, kind):
        cols = pl.ds(mult(2 * i + core, hc), hc)
        return (w_gate.at[:, cols], w_up.at[:, cols], w_down.at[cols])[kind]

    def own_copy(i, kind):
        return pltpu.make_async_copy(ffn_source(i, c, kind), w.at[i, z, c, kind], S["own"](i, kind))

    def sib_copy(i, kind):
        return remote(
            ffn_source(i, 1 - c, kind), w.at[i, z, c, kind], S["sib_s"](i, kind), S["sib_r"](i, kind), sib
        )

    def sib_wait(i, kind):
        return remote(
            ffn_source(i, c, kind), w.at[i, z, 1 - c, kind], S["sib_s"](i, kind), S["sib_r"](i, kind), sib
        )

    qown = [
        pltpu.make_async_copy(w_qkv.at[:, j * hc : (j + 1) * hc], aw.at[z, c, j], S["qown"](j))
        for j in range(3)
    ] + [
        pltpu.make_async_copy(w_out.at[j * hc : (j + 1) * hc], aw.at[z, c, 3 + j], S["qown"](3 + j))
        for j in range(2)
    ]
    for copy in qown:
        copy.start()
    row16 = lax.broadcasted_iota(jnp.int32, (16, hc), 0)
    gw[z, c] = jnp.where(
        row16 == 0,
        gain_a[...].astype(f32).reshape(1, hc),
        jnp.where(row16 == 1, gain_f[...].astype(f32).reshape(1, hc), 0.0),
    ).astype(bf16)
    tok_all = pltpu.make_async_copy(tok, p2, S["tok"](0))
    tok_all.start()

    def q_ref(part, u, core):
        return (aw if part == 0 else gw).at[u, core]

    def q_line(part, s, direction):
        u = z - s if direction == 0 else z + s
        ref = q_ref(part, u, c)
        return remote(
            ref, ref, S["qa_s"](part, direction, s), S["qa_r"](part, direction, s), (above, below)[direction]
        )

    def q_arrive(part, s, direction):
        u = z - s if direction == 0 else z + s
        ref = q_ref(part, u, c)
        return remote(
            ref,
            ref,
            S["qa_s"](part, direction, s - 1),
            S["qa_r"](part, direction, s - 1),
            (below, above)[direction],
        )

    def q_sib(part, u):
        ref = q_ref(part, u, c)
        return remote(ref, ref, S["qs_s"](part, u), S["qs_r"](part, u), sib)

    def q_sib_in(part, u):
        ref = q_ref(part, u, 1 - c)
        return remote(ref, ref, S["qs_s"](part, u), S["qs_r"](part, u), sib)

    def line_valid(s, direction):
        return z - s >= 0 if direction == 0 else z + s <= nz - 1

    def line_sends(s, direction):
        return line_valid(s, direction) & (has_above if direction == 0 else has_below)

    def q_tick(s):
        if s == 0:
            for copy in qown:
                copy.wait()
        for direction in range(2):
            if s > 0:

                @pl.when(line_valid(s, direction))
                def _():
                    for part in range(2):
                        q_arrive(part, s, direction).wait_recv()

            if s < nz - 1:

                @pl.when(line_sends(s, direction))
                def _():
                    for part in range(2):
                        q_line(part, s, direction).start()

            if s > 0:

                @pl.when(line_valid(s, direction))
                def _():
                    for part in range(2):
                        q_sib(part, z - s if direction == 0 else z + s).start()

        if s == 0:
            for part in range(2):
                q_sib(part, z).start()

    def q_finish():
        for s in range(nz - 1):
            for direction in range(2):

                @pl.when(line_sends(s, direction))
                def _():
                    for part in range(2):
                        q_line(part, s, direction).wait_send()

        for u in range(nz):
            for part in range(2):
                q_sib_in(part, u).wait_recv()

    def ag_line(i, s, direction):
        unit = w.at[i, z - s if direction == 0 else z + s]
        return remote(
            unit, unit, S["ag_s"](i, direction, s), S["ag_r"](i, direction, s), (above, below)[direction]
        )

    def ag_arrive(i, s, direction):
        unit = w.at[i, z - s if direction == 0 else z + s]
        return remote(
            unit,
            unit,
            S["ag_s"](i, direction, s - 1),
            S["ag_r"](i, direction, s - 1),
            (below, above)[direction],
        )

    def ag_tick(i, s):
        if s == 0:
            for kind in range(3):
                own_copy(i, kind).wait()
                sib_wait(i, kind).wait_recv()
        for direction in range(2):
            if s > 0:

                @pl.when(line_valid(s, direction))
                def _():
                    ag_arrive(i, s, direction).wait_recv()

            if s < nz - 1:

                @pl.when(line_sends(s, direction))
                def _():
                    ag_line(i, s, direction).start()

    def ag_finish(i):
        for s in range(nz - 1):
            for direction in range(2):

                @pl.when(line_sends(s, direction))
                def _():
                    ag_line(i, s, direction).wait_send()

    def rs_owner(tau, direction):
        return nz - 1 + z - tau if direction == 0 else tau - (nz - 1 - z)

    def rs_valid(tau, direction):
        return z <= tau if direction == 0 else tau >= nz - 1 - z

    def rs_line(i, tau, direction):
        return remote(
            w.at[i, rs_owner(tau, direction)],
            (ru, rd)[direction].at[tau],
            S["rs_s"](direction, tau),
            S["rs_r"](direction, tau),
            (above, below)[direction],
        )

    def slot_credit(direction, tau):
        return credit.at[direction * nz + tau]

    def take_slot(direction, tau):
        pl.semaphore_wait(slot_credit(direction, tau), 1)

    def at_edge(direction):
        return z == (nz - 2, 1)[direction]

    def rs_send(i, tau, direction):
        if i > 0:
            rs_line(i - 1, tau, direction).wait_send()
            take_slot(direction, tau)
        rs_line(i, tau, direction).start()

    def rs_edge(i):
        for direction in range(2):

            @pl.when(at_edge(direction))
            def _():
                rs_send(i, nz - 2, direction)

    def rs_tick(i, tau, which):
        for direction in range(2):
            got = (ru, rd)[direction]
            back = (below, above)[direction]
            here = rs_valid(tau, direction)
            if which == "mid":
                here = here & has_below & has_above
            if which == "end":
                here = here & ~(has_below & has_above)
            if tau > 0:

                @pl.when(here & (has_below, has_above)[direction])
                def _():
                    owner = rs_owner(tau, direction)
                    remote(
                        w.at[i, owner],
                        got.at[tau - 1],
                        S["rs_s"](direction, tau - 1),
                        S["rs_r"](direction, tau - 1),
                        back,
                    ).wait_recv()

                    def add(k, carry):
                        core, kind = k // 3, k % 3
                        a = w[i, owner, core, kind].astype(f32)
                        b = got[tau - 1, core, kind].astype(f32)
                        w[i, owner, core, kind] = (a + b).astype(bf16)
                        return carry

                    lax.fori_loop(0, 6, add, 0)
                    pl.semaphore_signal(
                        slot_credit(direction, tau - 1), inc=1, device_id=back, device_id_type=MESH
                    )

            if tau < nz - 1:

                sends = here
                if which == "inner" and tau == nz - 2:
                    sends = here & ~at_edge(direction)

                @pl.when(sends)
                def _():
                    rs_send(i, tau, direction)

    def rs_end():
        for tau in range(nz - 1):
            for direction in range(2):

                @pl.when(rs_valid(tau, direction))
                def _():
                    rs_line(nch - 1, tau, direction).wait_send()

    def fin_sib(i):
        return remote(w.at[i, z, 1 - c], fs.at[i], S["fin_s"](i), S["fin_r"](i), sib)

    def fin_in(i):
        return remote(w.at[i, z, c], fs.at[i], S["fin_s"](i), S["fin_r"](i), sib)

    def put_piece(i, half, piece):
        cols = pl.ds(mult(2 * i + half, hc), hc)
        st[0] = piece[0].astype(f32).T
        st[1] = piece[1].astype(f32).T
        st[2] = piece[2].astype(f32)
        puts = (
            pltpu.make_async_copy(st.at[0], g_gate.at[:, cols], S["put"](0)),
            pltpu.make_async_copy(st.at[1], g_up.at[:, cols], S["put"](1)),
            pltpu.make_async_copy(st.at[2], g_down.at[cols], S["put"](2)),
        )
        for copy in puts:
            copy.start()
        for copy in puts:
            copy.wait()

    def fin_start(i):
        fin_sib(i).start()
        put_piece(i, c, w.at[i, z, c])

    def fin_finish(i):
        fin_sib(i).wait_send()
        fin_in(i).wait_recv()
        put_piece(i, 1 - c, fs.at[i])

    def free_first():
        pl.semaphore_signal(credit.at[2 * nz], inc=1, device_id=sib, device_id_type=MESH)

    plan = sums_plan(nz, nch)

    def sums(place):
        for step_ in plan.get(place, ()):
            if step_[0] == "edge":
                rs_edge(step_[1])
            else:
                rs_tick(*step_)

    tile = min(256, tokens)

    def rows_pass(i, core):
        first = i == 0

        def rows_step(m, carry):
            local_rows = pl.ds(mult(m, tile), tile)
            rows = pl.ds(pl.multiple_of(core * tokens + m * tile, tile), tile)
            xm = x[rows, :]
            gate = dot(xm, w[i, :, :, 0].reshape(width, hc))
            up = dot(xm, w[i, :, :, 1].reshape(width, hc))
            dh = jnp.zeros((tile, hc), f32)
            for k in range(dps):
                dh = dh + dot_nt(ct[rows, k * hc : (k + 1) * hc], w[i, k // 2, k % 2, 2])
            sig = jax.nn.sigmoid(gate)
            act = gate * sig
            hidden = (act * up).astype(bf16)
            d_up = (dh * act).astype(bf16)
            d_gate = (dh * up * sig * (1.0 + gate * (1.0 - sig))).astype(bf16)
            ht[:, rows] = hidden.T
            dgt[:, rows] = d_gate.T
            dut[:, rows] = d_up.T
            mine_too = core is c
            for k in range(dps):
                cols = slice(k * hc, (k + 1) * hc)
                fwd = dot(hidden, w[i, k // 2, k % 2, 2])
                back = dot_nt(d_gate, w[i, k // 2, k % 2, 0]) + dot_nt(d_up, w[i, k // 2, k % 2, 1])
                if not first:
                    fwd = accp[rows, cols].astype(f32) + fwd
                    back = (accb if mine_too else acco)[local_rows, cols].astype(f32) + back
                accp[rows, cols] = fwd.astype(bf16)
                if mine_too:
                    accb[local_rows, cols] = back
                else:
                    acco[local_rows, cols] = back.astype(bf16)
            return carry

        lax.fori_loop(0, tokens // tile, rows_step, 0)

    def cols_pass(i):
        def cols_step(k, carry):
            cols = pl.ds(mult(k, hc), hc)
            xs = x[:, cols]
            chip, core = k // 2, k % 2
            w[i, chip, core, 0] = dot(dgt[...], xs).astype(bf16)
            w[i, chip, core, 1] = dot(dut[...], xs).astype(bf16)
            w[i, chip, core, 2] = dot(ht[...], ct[:, cols]).astype(bf16)
            return carry

        lax.fori_loop(0, dps, cols_step, 0)

    lane = lax.broadcasted_iota(jnp.int32, (1, LANES), 1)
    low_head = lane < HD
    low_half = lane % HD < HD // 2

    def turn(u, cos, sin):
        swapped = jnp.where(low_half, pltpu.roll(u, LANES - HD // 2, 1), pltpu.roll(u, HD // 2, 1))
        return u * cos + swapped * sin

    def turn_back(g, cos, sin):
        v = g * sin
        swapped = jnp.where(low_half, pltpu.roll(v, LANES - HD // 2, 1), pltpu.roll(v, HD // 2, 1))
        return g * cos + swapped

    def tables(rows, with_values):
        cos, sin = cosine[rows, :], sine[rows, :]
        if with_values:
            cos, sin = jnp.where(low_head, cos, 1.0), jnp.where(low_head, sin, 0.0)
        return cos, sin

    step = 32

    def norm_rows(src, dst, base, grad_sum):
        def body(m, carry):
            rows = pl.ds(mult(m, step), step)
            v = src[rows, :].astype(f32)
            scale = lax.rsqrt(jnp.mean(v * v, axis=-1, keepdims=True) + epsilon)
            v = v * scale
            dst[pl.ds(pl.multiple_of(base + m * step, step), step), :] = (v * gv[0:1, :]).astype(bf16)
            if grad_sum is None:
                return carry
            up = grad_sum(rows)
            return carry + jnp.sum(up * v, axis=0, keepdims=True)

        start = 0 if grad_sum is None else jnp.zeros((1, width), f32)
        return lax.fori_loop(0, tokens // step, body, start)

    chunks = aw_cols(hc) // LANES
    per_block = hc // LANES
    atile = min(256, tokens)

    def joined():
        def body(m, carry):
            rows = pl.ds(mult(m, atile), atile)
            src = pl.ds(pl.multiple_of(c * tokens + m * atile, atile), atile)
            xm = x[src, :]
            for j in range(3):
                block = dot(xm, aw[:, :, j].reshape(width, hc))
                for q in range(per_block):
                    index = j * per_block + q
                    cos, sin = tables(rows, index % 3 == 2)
                    u = block[:, q * LANES : (q + 1) * LANES]
                    qkvb[rows, index * LANES : (index + 1) * LANES] = turn(u, cos, sin).astype(bf16)
            return carry

        lax.fori_loop(0, tokens // atile, body, 0)

    row_id = lax.broadcasted_iota(jnp.int32, (SEQ, SEQ), 0)
    col_id = lax.broadcasted_iota(jnp.int32, (SEQ, SEQ), 1)
    keep = row_id >= col_id
    inv_root = 1.0 / math.sqrt(HD)

    def doubled(rows, base):
        kv = qkvb[rows, pl.ds(pl.multiple_of(base + GROUPS * HD, LANES), LANES)].astype(f32)
        other = pltpu.roll(kv, HD, 1)
        kk = jnp.where(low_head, kv, other).astype(bf16)
        vv = jnp.where(low_head, other, kv).astype(bf16)
        return kk, vv

    def softmax(qm, kk):
        scores = jnp.where(keep, dot_nt(qm, kk) * inv_root, masked_score)
        e = jnp.exp(scores - jnp.max(scores, axis=-1, keepdims=True))
        return e * (1.0 / jnp.sum(e, axis=-1, keepdims=True))

    def place(n):
        s, h = n // kv_local, n % kv_local
        rows = pl.ds(mult(s, SEQ), SEQ)
        return rows, h * head_cols, h * GROUPS * HD

    def heads_forward():
        def body(n, carry):
            rows, base, qbase = place(n)
            kk, vv = doubled(rows, base)
            for pair in range(GROUPS // 2):
                qp = qkvb[rows, pl.ds(pl.multiple_of(base + pair * LANES, LANES), LANES)]
                halves = []
                for half in range(2):
                    mask = low_head if half == 0 else ~low_head
                    qm = jnp.where(mask, qp.astype(f32), 0.0).astype(bf16)
                    halves.append(dot(softmax(qm, kk).astype(bf16), vv))
                att[rows, pl.ds(pl.multiple_of(qbase + pair * LANES, LANES), LANES)] = jnp.where(
                    low_head, halves[0], halves[1]
                ).astype(bf16)
            return carry

        lax.fori_loop(0, seqs * kv_local, body, 0)

    def heads_backward():
        def body(n, carry):
            rows, base, qbase = place(n)
            kk, vv = doubled(rows, base)
            dkk = jnp.zeros((SEQ, LANES), f32)
            dvv = jnp.zeros((SEQ, LANES), f32)
            cos, sin = tables(rows, False)
            for pair in range(GROUPS // 2):
                cols = pl.ds(pl.multiple_of(base + pair * LANES, LANES), LANES)
                acols = pl.ds(pl.multiple_of(qbase + pair * LANES, LANES), LANES)
                qp = qkvb[rows, cols].astype(f32)
                dp = datt[rows, acols].astype(f32)
                prod = dp * att[rows, acols].astype(f32)
                halves = []
                for half in range(2):
                    mask = low_head if half == 0 else ~low_head
                    qm = jnp.where(mask, qp, 0.0).astype(bf16)
                    dm = jnp.where(mask, dp, 0.0).astype(bf16)
                    probs = softmax(qm, kk)
                    delta = jnp.sum(jnp.where(mask, prod, 0.0), axis=-1, keepdims=True)
                    ds = (probs * (dot_nt(dm, vv) - delta) * inv_root).astype(bf16)
                    halves.append(dot(ds, kk))
                    dkk = dkk + dot(ds.T, qm)
                    dvv = dvv + dot(probs.astype(bf16).T, dm)
                dq = jnp.where(low_head, halves[0], halves[1])
                qkvb[rows, cols] = turn_back(dq, cos, sin).astype(bf16)
            dkk = dkk + pltpu.roll(dkk, HD, 1)
            dvv = dvv + pltpu.roll(dvv, HD, 1)
            cos, sin = tables(rows, True)
            qkvb[rows, pl.ds(pl.multiple_of(base + GROUPS * HD, LANES), LANES)] = turn_back(
                jnp.where(low_head, dkk, dvv), cos, sin
            ).astype(bf16)
            return carry

        lax.fori_loop(0, seqs * kv_local, body, 0)

    def out_weight(k):
        return aw[k // 2, k % 2, 3:5].reshape(2 * hc, hc)

    def attention_partial():
        def body(k, carry):
            cols = pl.ds(mult(k, hc), hc)
            rsb[:, cols] = dot(att[...], out_weight(k)).astype(bf16)
            return carry

        lax.fori_loop(0, dps, body, 0)

    square = nt == 4
    xp, yp, dg = t ^ 1, t ^ 2, t ^ 3
    half = ts // 2

    def part_rows(base, index, upper):
        return pl.ds(pl.multiple_of(base + index * ts + upper * half, half), half)

    def slice_rows(base, index):
        return pl.ds(pl.multiple_of(base + index * ts, ts), ts)

    def reduce_copy(src, base, land, which, n):
        rows = (
            part_rows(base, xp, 0),
            part_rows(base, dg, 0),
            part_rows(base, yp, 1),
            part_rows(base, dg, 1),
            part_rows(base, yp, 0),
            part_rows(base, xp, 1),
        )[n]
        to = (xp, xp, yp, yp, yp, xp)[n]
        return remote(
            src.at[rows],
            land.at[pl.ds(n * half, half)],
            S["ps_s"](which, n),
            S["ps_r"](which, n),
            (d, to),
        )

    def reduce_direct(src, base, land, which, k, arriving):
        frm = source(k)
        return remote(
            src.at[slice_rows(base, peer(k))],
            land.at[slot(frm if arriving else t)],
            S["ps_s"](which, k),
            S["ps_r"](which, k),
            (d, frm if arriving else peer(k)),
        )

    def reduce_start(src, base, land, which):
        if square:
            for n in range(4):
                reduce_copy(src, base, land, which, n).start()
        else:
            for k in range(nt - 1):
                reduce_direct(src, base, land, which, k, False).start()

    def reduce_mid(src, base, land, which):
        if not square:
            return
        for n, index, upper in ((1, yp, 0), (3, xp, 1)):
            reduce_copy(src, base, land, which, n).wait_recv()
            rows = part_rows(base, index, upper)
            both = src[rows, :].astype(f32) + land[n * half : (n + 1) * half, :].astype(f32)
            src[rows, :] = both.astype(bf16)
            reduce_copy(src, base, land, which, 4 if n == 1 else 5).start()

    def reduce_wait(src, base, land, which):
        if square:
            for n in (0, 2, 4, 5):
                reduce_copy(src, base, land, which, n).wait_recv()
        else:
            for k in range(nt - 1):
                reduce_direct(src, base, land, which, k, True).wait_recv()

    def reduce_end(src, base, land, which):
        if square:
            for n in range(6):
                reduce_copy(src, base, land, which, n).wait_send()
        else:
            for k in range(nt - 1):
                reduce_direct(src, base, land, which, k, False).wait_send()

    def summed(src, base, land, m):
        total = src[pl.ds(pl.multiple_of(base + t * ts + m * step, step), step), :].astype(f32)
        if square:
            upper = m // (half // step)
            inner = (m % (half // step)) * step
            for first in (2 * upper * half, (4 + upper) * half):
                total = total + land[pl.ds(pl.multiple_of(first + inner, step), step), :].astype(f32)
        else:
            for k in range(nt - 1):
                rows = pl.ds(pl.multiple_of(source(k) * ts + m * step, step), step)
                total = total + land[rows, :].astype(f32)
        return total

    def spread_copy(src, src_base, dst, dst_base, which, n):
        index, upper, to = (
            (t, 0, xp),
            (t, 1, xp),
            (t, 1, yp),
            (t, 0, yp),
            (xp, 0, yp),
            (yp, 1, xp),
        )[n]
        from_rows = part_rows(src_base, t, upper) if n < 4 else part_rows(dst_base, index, upper)
        return remote(
            (src if n < 4 else dst).at[from_rows],
            dst.at[part_rows(dst_base, index, upper)],
            S["ga_s"](which, n),
            S["ga_r"](which, n),
            (d, to),
        )

    def spread_arrive(src, src_base, dst, dst_base, which, n):
        index, upper, frm = (
            (xp, 0, xp),
            (xp, 1, xp),
            (yp, 1, yp),
            (yp, 0, yp),
            (dg, 0, yp),
            (dg, 1, xp),
        )[n]
        return remote(
            src.at[part_rows(src_base, t, upper)],
            dst.at[part_rows(dst_base, index, upper)],
            S["ga_s"](which, n),
            S["ga_r"](which, n),
            (d, frm),
        )

    def spread_direct(src, src_base, dst, dst_base, which, k, arriving):
        frm = source(k)
        return remote(
            src.at[slice_rows(src_base, t)],
            dst.at[slice_rows(dst_base, frm if arriving else t)],
            S["ga_s"](which, k),
            S["ga_r"](which, k),
            (d, frm if arriving else peer(k)),
        )

    def spread_start(*args):
        if square:
            for n in range(4):
                spread_copy(*args, n).start()
        else:
            for k in range(nt - 1):
                spread_direct(*args, k, False).start()

    def spread_mid(*args):
        if square:
            for n, onward in ((0, 4), (2, 5)):
                spread_arrive(*args, n).wait_recv()
                spread_copy(*args, onward).start()

    def spread_wait(*args):
        if square:
            for n in (1, 3, 4, 5):
                spread_arrive(*args, n).wait_recv()
        else:
            for k in range(nt - 1):
                spread_direct(*args, k, True).wait_recv()

    def spread_end(*args):
        if square:
            for n in range(6):
                spread_copy(*args, n).wait_send()
        else:
            for k in range(nt - 1):
                spread_direct(*args, k, False).wait_send()

    q_tick(0)
    for i in range(nch):
        for kind in range(3):
            own_copy(i, kind).start()
            sib_copy(i, kind).start()
    cot_own = pltpu.make_async_copy(cot, ct.at[core_rows(c)], S["cot"](0))
    cot_sib = remote(cot, ct.at[core_rows(c)], S["cot"](1), S["cot"](2), sib)
    cot_in = remote(cot, ct.at[core_rows(1 - c)], S["cot"](1), S["cot"](2), sib)
    cot_own.start()
    cot_sib.start()
    quarter = HD // 2
    exponent = lax.broadcasted_iota(jnp.int32, (quarter, 1), 0).astype(f32) * (2.0 / HD)
    angles = jnp.exp(exponent * -math.log(rope_base)) * pos[...].astype(f32)
    cos_rows, sin_rows = jnp.cos(angles), jnp.sin(angles)
    cosine[...] = jnp.concatenate([cos_rows] * (LANES // quarter), axis=0).T
    sine[...] = jnp.concatenate([-sin_rows, sin_rows] * (LANES // HD), axis=0).T
    for s in range(1, nz):
        if s == nz - 1:
            ag_tick(0, 0)
        q_tick(s)
    if nz == 1:
        ag_tick(0, 0)
    q_finish()
    for k in range(dps):
        gv[:, k * hc : (k + 1) * hc] = gw[k // 2, k % 2].astype(f32)
    tok_all.wait()
    norm_rows(p2, x, c * tokens, None)
    joined()
    heads_forward()
    if nz > 1:
        ag_tick(0, 1)
    attention_partial()
    first_sum = (rsb, 0, p1, 0)
    reduce_start(*first_sum)
    if nz > 2:
        ag_tick(0, 2)
    reduce_mid(*first_sum)
    if nz > 3:
        ag_tick(1, 0)
    reduce_wait(*first_sum)
    mine = half_rows(c, t)

    def second_norm(m, carry):
        rows = pl.ds(mult(m, step), step)
        trow = pl.ds(pl.multiple_of(t * ts + m * step, step), step)
        total = p2[trow, :].astype(f32) + summed(rsb, 0, p1, m)
        resid[rows, :] = total
        scale = lax.rsqrt(jnp.mean(total * total, axis=-1, keepdims=True) + epsilon)
        x[pl.ds(pl.multiple_of(c * tokens + t * ts + m * step, step), step), :] = (
            total * scale * gv[1:2, :]
        ).astype(bf16)
        return carry

    lax.fori_loop(0, ts // step, second_norm, 0)
    x_spread = (x, c * tokens, x, c * tokens, 3)

    def xs_index(k):
        if square:
            return (t, xp, yp, dg)[k]
        return lax.rem(t - k + nt, nt)

    def xs_copy(k):
        rows = half_rows(c, xs_index(k))
        return remote(x.at[rows], x.at[rows], S["xs_s"](k), S["xs_r"](k), sib)

    def xs_in(k):
        rows = half_rows(1 - c, xs_index(k))
        return remote(x.at[rows], x.at[rows], S["xs_s"](k), S["xs_r"](k), sib)

    spread_start(*x_spread)
    xs_copy(0).start()
    spread_mid(*x_spread)
    if square:
        spread_arrive(*x_spread, 1).wait_recv()
        xs_copy(1).start()
        spread_arrive(*x_spread, 3).wait_recv()
        xs_copy(2).start()
    for s in range(3, nz):
        ag_tick(0, s)
    ag_finish(0)
    if nz <= 3:
        ag_tick(1, 0)
    if square:
        for n in (4, 5):
            spread_arrive(*x_spread, n).wait_recv()
        xs_copy(3).start()
    else:
        for k in range(nt - 1):
            spread_direct(*x_spread, k, True).wait_recv()
            xs_copy(k + 1).start()
    cot_own.wait()
    cot_in.wait_recv()
    for k in range(nt):
        xs_in(k).wait_recv()

    last = nch - 1
    other = (1 - c) * tokens
    for i in range(last):
        if i > 0:
            ag_tick(i + 1, 0)
        sums(("before", i))
        rows_pass(i, 1 - c)
        rows_pass(i, c)
        cols_pass(i)
        sums(("after", i))
        for s in range(1, nz):
            ag_tick(i + 1, s)
            if s == nz - 2:
                sums(("middle", i))
        ag_finish(i + 1)

    def sib_b(k):
        return remote(acco.at[slot(k)], sbr_b.at[slot(k)], S["sb_s"](0, k), S["sb_r"](0, k), sib)

    def sib_p(k):
        return remote(
            accp.at[half_rows(1 - c, k)], sbr_p.at[slot(k)], S["sb_s"](1, k), S["sb_r"](1, k), sib
        )

    for u in range(nz):
        for part in range(2):
            q_sib(part, u).wait_send()
    spread_end(*x_spread)
    reduce_end(*first_sum)
    for k in range(nt):
        xs_copy(k).wait_send()
    sums(("before", last))
    rows_pass(last, 1 - c)
    for k in range(nt):
        sib_b(k).start()
    rows_pass(last, c)
    for k in range(nt):
        sib_b(k).wait_recv()

    def pair_b(m, carry):
        rows = pl.ds(mult(m, step), step)
        rsb[rows, :] = (accb[rows, :] + sbr_b[rows, :].astype(f32)).astype(bf16)
        return carry

    lax.fori_loop(0, tokens // step, pair_b, 0)
    back_sum = (rsb, 0, p2, 1)
    reduce_start(*back_sum)
    cols_pass(last)
    sums(("after", last))
    for k in range(nt):
        sib_p(k).start()
    reduce_mid(*back_sum)
    reduce_wait(*back_sum)

    def second_back(m, carry):
        rows = pl.ds(mult(m, step), step)
        place_ = pl.ds(pl.multiple_of(c * tokens + t * ts + m * step, step), step)
        up = summed(rsb, 0, p2, m)
        v = resid[rows, :]
        scale = lax.rsqrt(jnp.mean(v * v, axis=-1, keepdims=True) + epsilon)
        weighted = up * gv[1:2, :]
        inner = jnp.mean(weighted * v, axis=-1, keepdims=True)
        grad = ct[place_, :].astype(f32) + scale * weighted - v * (scale * scale * scale) * inner
        accb[rows, :] = grad
        x[place_, :] = grad.astype(bf16)
        return carry + jnp.sum(up * v * scale, axis=0, keepdims=True)

    gain_two = lax.fori_loop(0, ts // step, second_back, jnp.zeros((1, width), f32))
    rg_spread = (x, c * tokens, x, c * tokens, 0)
    spread_start(*rg_spread)
    spread_mid(*rg_spread)
    reduce_end(*back_sum)
    for k in range(nt):
        sib_p(k).wait_recv()

    def pair_p(m, carry):
        rows = pl.ds(mult(m, step), step)
        here = pl.ds(pl.multiple_of(c * tokens + m * step, step), step)
        rsb[rows, :] = (accp[here, :].astype(f32) + sbr_p[rows, :].astype(f32)).astype(bf16)
        return carry

    lax.fori_loop(0, tokens // step, pair_p, 0)

    spread_wait(*rg_spread)
    out_sum = (rsb, 0, p1, 2)
    reduce_start(*out_sum)
    sums(1)
    fin_start(0)

    def d_attended(m, carry):
        rows = pl.ds(mult(m, atile), atile)
        src = pl.ds(pl.multiple_of(c * tokens + m * atile, atile), atile)
        for j in range(2):
            total = jnp.zeros((atile, hc), f32)
            for k in range(dps):
                total = total + dot_nt(x[src, k * hc : (k + 1) * hc], aw[k // 2, k % 2, 3 + j])
            datt[rows, j * hc : (j + 1) * hc] = total.astype(bf16)
        for j in range(2):
            (ht, dgt)[j][:, rows] = att[rows, j * hc : (j + 1) * hc].T
        return carry

    lax.fori_loop(0, tokens // atile, d_attended, 0)

    def out_grads(k, carry):
        xs = x[core_rows(c), pl.ds(mult(k, hc), hc)]
        for j in range(2):
            aw[k // 2, k % 2, 3 + j] = dot((ht, dgt)[j][:, :tokens], xs).astype(bf16)
        return carry

    lax.fori_loop(0, dps, out_grads, 0)

    def a_src(part, u, core):
        return (aw.at[u, core, 3:5], aw.at[u, core, 0:3], gg.at[u, core])[part]

    def a_sib_ref(part):
        return (w.at[0, :, 1, 0:2], w.at[0, :, 0], gsib)[part]

    def a_sib(part):
        src = (aw.at[:, 1 - c, 3:5], aw.at[:, 1 - c, 0:3], gg.at[:, 1 - c])[part]
        return remote(src, a_sib_ref(part), S["as_s"](part), S["as_r"](part), sib)

    def a_land(part, direction, tau):
        line = (ru, rd)[direction]
        return (line.at[tau, 1, 0:2], line.at[tau, 0], (gru, grd)[direction].at[tau])[part]

    def a_line(part, tau, direction):
        return remote(
            a_src(part, rs_owner(tau, direction), c),
            a_land(part, direction, tau),
            S["ar_s"](part, direction, tau),
            S["ar_r"](part, direction, tau),
            (above, below)[direction],
        )

    def a_add(part, owner, got):
        if part == 2:
            gg[owner, c] = gg[owner, c] + got[...]
            return
        base, count = ((3, 2), (0, 3))[part]
        for j in range(count):
            both = aw[owner, c, base + j].astype(f32) + got[j].astype(f32)
            aw[owner, c, base + j] = both.astype(bf16)

    def a_pair(part):
        a_sib(part).wait_recv()

        def body(u, carry):
            a_add(part, u, (w.at[0, u, 1, 0:2], w.at[0, u, 0], gsib.at[u])[part])
            return carry

        lax.fori_loop(0, nz, body, 0)

    def a_tick(part, tau):
        for direction in range(2):
            if tau > 0:

                @pl.when(rs_valid(tau, direction) & (has_below, has_above)[direction])
                def _():
                    owner = rs_owner(tau, direction)
                    remote(
                        a_src(part, owner, c),
                        a_land(part, direction, tau - 1),
                        S["ar_s"](part, direction, tau - 1),
                        S["ar_r"](part, direction, tau - 1),
                        (below, above)[direction],
                    ).wait_recv()
                    a_add(part, owner, a_land(part, direction, tau - 1))

            if tau < nz - 1:

                @pl.when(rs_valid(tau, direction))
                def _():
                    if part == 0:
                        take_slot(direction, tau)
                    a_line(part, tau, direction).start()

    def a_finish(part):
        a_sib(part).wait_send()
        for tau in range(nz - 1):
            for direction in range(2):

                @pl.when(rs_valid(tau, direction))
                def _():
                    a_line(part, tau, direction).wait_send()

    fin_finish(0)
    free_first()
    pl.semaphore_wait(credit.at[2 * nz], 1)
    a_sib(0).start()
    tok_again = pltpu.make_async_copy(tok, sbr_b, S["tok"](1))
    tok_again.start()
    a_pair(0)
    heads_backward()

    def attn_back(k, carry):
        total = jnp.zeros((tokens, hc), f32)
        for j in range(3):
            total = total + dot_nt(qkvb[:, j * hc : (j + 1) * hc], aw[k // 2, k % 2, j])
        x[pl.ds(mult(1 - c, tokens), tokens), pl.ds(mult(k, hc), hc)] = total.astype(bf16)
        return carry

    lax.fori_loop(0, dps, attn_back, 0)
    tail_sum = (x, other, p2, 3)
    reduce_start(*tail_sum)
    reduce_mid(*out_sum)
    tok_again.wait()

    def own_back(rows):
        return x[pl.ds(pl.multiple_of(other + rows.start, step), step), :].astype(f32)

    gain_one = norm_rows(sbr_b, sbr_p, 0, own_back)
    for k in range(dps):
        cols = slice(k * hc, (k + 1) * hc)
        gg[k // 2, k % 2] = jnp.concatenate(
            [gain_one[:, cols], gain_two[:, cols], jnp.zeros((6, hc), f32)], axis=0
        )
    a_sib(2).start()
    for m in range(tokens // atile):
        for j in range(3):
            (ht, dgt, dut)[j][:, tokens + m * atile : tokens + (m + 1) * atile] = qkvb[
                m * atile : (m + 1) * atile, j * hc : (j + 1) * hc
            ].T

    def qkv_grads(k, carry):
        xs = sbr_p[:, pl.ds(mult(k, hc), hc)]
        for j in range(3):
            aw[k // 2, k % 2, j] = dot((ht, dgt, dut)[j][:, tokens:], xs).astype(bf16)
        return carry

    lax.fori_loop(0, dps, qkv_grads, 0)
    a_sib(1).start()
    a_pair(1)
    a_pair(2)

    reduce_mid(*tail_sum)
    reduce_wait(*out_sum)

    def finish_output(m, carry):
        rows = pl.ds(mult(m, step), step)
        where = pl.ds(pl.multiple_of(c * tokens + t * ts + m * step, step), step)
        accp[where, :] = (resid[rows, :] + summed(rsb, 0, p1, m)).astype(bf16)
        return carry

    lax.fori_loop(0, ts // step, finish_output, 0)
    out_spread = (accp, c * tokens, out, 0, 1)
    spread_start(*out_spread)
    put_out = pltpu.make_async_copy(accp.at[mine], out.at[slot(t)], S["loc"](0))
    put_out.start()

    sums(2)
    for part in range(3):
        a_tick(part, 0)
    fin_start(1)

    reduce_wait(*tail_sum)
    for k in range(nt):
        sib_p(k).wait_send()
    theirs = half_rows(1 - c, t)

    def finish_tokens(m, carry):
        rows = pl.ds(mult(m, step), step)
        up = summed(x, other, p2, m)
        v = sbr_b[pl.ds(pl.multiple_of(t * ts + m * step, step), step), :].astype(f32)
        scale = lax.rsqrt(jnp.mean(v * v, axis=-1, keepdims=True) + epsilon)
        weighted = up * gv[0:1, :]
        inner = jnp.mean(weighted * v, axis=-1, keepdims=True)
        grad = accb[rows, :] + scale * weighted - v * (scale * scale * scale) * inner
        accp[pl.ds(pl.multiple_of(other + t * ts + m * step, step), step), :] = grad.astype(bf16)
        return carry

    lax.fori_loop(0, ts // step, finish_tokens, 0)
    tok_spread = (accp, other, dtok, 0, 2)
    spread_start(*tok_spread)
    put_tok = pltpu.make_async_copy(accp.at[theirs], dtok.at[slot(t)], S["loc"](1))
    put_tok.start()
    fin_finish(1)
    spread_mid(*out_spread)
    spread_mid(*tok_spread)
    sums(3)
    for part in range(3):
        a_tick(part, 1)
    fin_start(2)
    fin_finish(2)
    sums(4)
    for s in range(2, nz):
        for part in range(3):
            a_tick(part, s)
        if s == nz - 2:
            fin_start(3)
    fin_finish(3)

    def gain_copy(k):
        return remote(gg.at[z, c], gt.at[t], S["gg_s"](k), S["gg_r"](k), (d, peer(k)))

    def gain_in(k):
        return remote(gg.at[z, c], gt.at[source(k)], S["gg_s"](k), S["gg_r"](k), (d, source(k)))

    for k in range(nt - 1):
        gain_copy(k).start()
    gt[t] = gg[z, c]

    base = ts
    for j in range(3):
        accb[base : base + hc, j * hc : (j + 1) * hc] = aw[z, c, j].astype(f32).T
    for j in range(2):
        accb[base : base + hc, (3 + j) * hc : (4 + j) * hc] = aw[z, c, 3 + j].astype(f32)
    put_qkv = pltpu.make_async_copy(accb.at[base : base + hc, 0 : 3 * hc], g_qkv, S["loc"](2))
    put_o = [
        pltpu.make_async_copy(
            accb.at[base : base + hc, (3 + j) * hc : (4 + j) * hc],
            g_out.at[j * hc : (j + 1) * hc],
            S["loc"](3 + j),
        )
        for j in range(2)
    ]
    put_qkv.start()
    for copy in put_o:
        copy.start()
    for k in range(nt - 1):
        gain_in(k).wait_recv()
    total = gt[0]
    for k in range(1, nt):
        total = total + gt[k]
    g_gains[...] = total

    for i in range(nch):
        for kind in range(3):
            sib_copy(i, kind).wait_send()
    cot_sib.wait_send()
    for part in range(3):
        a_finish(part)
    for k in range(nt - 1):
        gain_copy(k).wait_send()
    for k in range(nt):
        sib_b(k).wait_send()
    rs_end()
    reduce_end(*out_sum)
    reduce_end(*tail_sum)
    spread_wait(*out_spread)
    spread_wait(*tok_spread)
    for args in (rg_spread, out_spread, tok_spread):
        spread_end(*args)
    put_out.wait()
    put_tok.wait()
    put_qkv.wait()
    for copy in put_o:
        copy.wait()


def aw_cols(shard):
    return 3 * shard


def layer(tokens, cotangent, weights, positions, gain_a, gain_f, nz, nt):
    count, width = tokens.shape
    hc, hid = weights[2].shape
    nch = hid // (2 * hc)
    ts = count // nt
    sizes = (nz, nt, nch, count, width, hc)
    sems, _ = semaphores(nz, nt, nch)
    V = pltpu.VMEM
    recv = (nz - 1, 2, 3, hc, hc)
    S = jax.ShapeDtypeStruct
    return pl.pallas_call(
        functools.partial(layer_kernel, sizes),
        out_shape=(
            S((count, width), bf16),
            S((count, width), bf16),
            S((hc, 3 * hc), f32),
            S((2 * hc, hc), f32),
            S((hc, hid), f32),
            S((hc, hid), f32),
            S((hid, hc), f32),
            S((8, hc), f32),
        ),
        in_specs=[HBM] * 7 + [VMEM] * 3,
        out_specs=(HBM, HBM, HBM, HBM, HBM, HBM, HBM, VMEM),
        scratch_shapes=[
            V((nch, nz, 2, 3, hc, hc), bf16),
            V(recv, bf16),
            V(recv, bf16),
            V((2 * count, width), bf16),
            V((2 * count, width), bf16),
            V((2 * count, width), bf16),
            V((count, width), f32),
            V((count, width), bf16),
            V((hc, 2 * count), bf16),
            V((hc, 2 * count), bf16),
            V((hc, 2 * count), bf16),
            V((ts, width), f32),
            V((count, width), bf16),
            V((count, width), bf16),
            V((count, width), bf16),
            V((count, width), bf16),
            V((count, width), bf16),
            V((nz, 2, 5, hc, hc), bf16),
            V((count, 3 * hc), bf16),
            V((count, 2 * hc), bf16),
            V((count, 2 * hc), bf16),
            V((nch, 3, hc, hc), bf16),
            V((3, hc, hc), f32),
            V((nz, 2, 16, hc), bf16),
            V((16, width), f32),
            V((nz, 2, 8, hc), f32),
            V((nz, 8, hc), f32),
            V((nz - 1, 8, hc), f32),
            V((nz - 1, 8, hc), f32),
            V((nt, 8, hc), f32),
            V((count, LANES), f32),
            V((count, LANES), f32),
            pltpu.SemaphoreType.DMA((sems.count,)),
            pltpu.SemaphoreType.REGULAR((2 * nz + 1,)),
        ],
        compiler_params=pltpu.CompilerParams(
            collective_id=0, has_side_effects=True, vmem_limit_bytes=63 * 2**20
        ),
        name="layer",
    )(tokens, cotangent, *weights, positions, gain_a, gain_f)


def copy_kernel(count, parts, *refs):
    sources, gains = refs[:count], refs[count]
    results, gain_outs = refs[count + 1 : 2 * count + 1], refs[2 * count + 1 : 2 * count + 3]
    held, sem = refs[2 * count + 3 : 3 * count + 3], refs[-1]
    loads, stores = [], []
    for n in range(count):
        rows = sources[n].shape[0] // parts
        for k in range(parts):
            at = pl.ds(k * rows, rows)
            place = sem.at[n * parts + k]
            loads.append(pltpu.make_async_copy(sources[n].at[at], held[n].at[at], place))
            stores.append(pltpu.make_async_copy(held[n].at[at], results[n].at[at], place))
    for copy in loads:
        copy.start()
    for n in range(2):
        gain_outs[n][...] = gains[n, :]
    for load, store in zip(loads, stores):
        load.wait()
        store.start()
    for copy in stores:
        copy.wait()


def copied(arrays, gains):
    count, parts = len(arrays), 2
    shapes = [jax.ShapeDtypeStruct(a.shape, a.dtype) for a in arrays]
    return pl.pallas_call(
        functools.partial(copy_kernel, count, parts),
        out_shape=shapes + [jax.ShapeDtypeStruct(gains.shape[1:], f32)] * 2,
        in_specs=[HBM] * count + [VMEM],
        out_specs=[HBM] * count + [VMEM] * 2,
        scratch_shapes=[pltpu.VMEM(a.shape, a.dtype) for a in arrays]
        + [pltpu.SemaphoreType.DMA((count * parts,))],
        compiler_params=pltpu.CompilerParams(vmem_limit_bytes=60 * 2**20),
        name="results",
    )(*arrays, gains)


def local(tokens, positions, w_qkv, w_out, w_gate, w_up, w_down, gain_attn, gain_ffn, cotangent):
    nz = lax.axis_size("dp") // 2
    nt = lax.axis_size("tensor")
    results = layer(
        tokens,
        cotangent,
        (w_qkv, w_out, w_gate, w_up, w_down),
        positions.reshape(1, -1),
        gain_attn,
        gain_ffn,
        nz,
        nt,
    )
    return tuple(copied(results[:-1], results[-1]))


def solution(mesh):
    return jax.shard_map(
        local,
        mesh=mesh,
        in_specs=(
            P("dp", None),
            P("dp"),
            P("dp", "tensor"),
            P("tensor", "dp"),
            P("dp", "tensor"),
            P("dp", "tensor"),
            P("tensor", "dp"),
            P("dp"),
            P("dp"),
            P("dp", None),
        ),
        out_specs=(
            P("dp", None),
            P("dp", None),
            P("dp", "tensor"),
            P("tensor", "dp"),
            P("dp", "tensor"),
            P("dp", "tensor"),
            P("tensor", "dp"),
            P("dp"),
            P("dp"),
        ),
        check_vma=False,
    )
```

```python
import functools
import math

import jax
import jax.numpy as jnp
from jax import lax
from jax.experimental import pallas as pl
from jax.experimental.pallas import tpu as pltpu
from jax.sharding import PartitionSpec as P

HEADS = 32
KV_HEADS = 8
HD = 64
SEQ = 256
GROUPS = HEADS // KV_HEADS
LANES = 128

epsilon = 1e-05
rope_base = 500000.0
masked_score = -1e30

MESH = pl.DeviceIdType.MESH
HBM = pl.BlockSpec(memory_space=pl.ANY)
VMEM = pl.BlockSpec(memory_space=pltpu.VMEM)
bf16 = jnp.bfloat16
f32 = jnp.float32
NT_DIMS = (((1,), (1,)), ((), ()))


def remote(src, dst, send, recv, device):
    return pltpu.make_async_remote_copy(
        src_ref=src, dst_ref=dst, send_sem=send, recv_sem=recv, device_id=device, device_id_type=MESH
    )


def mult(value, factor):
    return pl.multiple_of(value * factor, factor)


def dot(a, b):
    return jnp.dot(a, b, preferred_element_type=f32)


def dot_nt(a, b):
    return lax.dot_general(a, b, NT_DIMS, preferred_element_type=f32)


def sums_plan(nz, nch):
    last = nch - 1
    if (nz, nch) != (4, 4):
        plan = {}
        for r in range(last + nz):
            hops = [(i, r - i, "all") for i in range(nch) if 0 <= r - i < nz]
            plan.setdefault(4 * r if r <= last else 4 * last + 3, []).extend(hops)
        return plan
    return {
        0: [(0, 0, "all")],
        2: [(0, 1, "all")],
        5: [(0, 2, "inner"), (1, 0, "all")],
        9: [(1, 1, "all"), (2, 0, "all")],
        10: [(0, 3, "mid"), (1, 2, "inner"), (2, 1, "all")],
        11: [("edge", 0)],
        12: [(3, 0, "all")],
        13: [(0, 3, "end"), ("edge", 1)],
        14: [(1, 3, "mid"), (2, 2, "inner")],
        16: [(3, 1, "all")],
        18: [(1, 3, "end"), ("edge", 2), (2, 3, "mid"), (3, 2, "inner")],
        19: [(2, 3, "end"), ("edge", 3)],
        21: [(3, 3, "mid"), (3, 3, "end")],
    }


class Sems:
    def __init__(self):
        self.count = 0
        self.ref = None

    def take(self, *dims):
        base = self.count
        self.count += math.prod(dims)

        def at(*index):
            flat = 0
            for size, place in zip(dims, index):
                flat = flat * size + place
            return self.ref.at[base + flat]

        return at


def semaphores(nz, nt, nch):
    s = Sems()
    names = {
        "own": s.take(nch, 3),
        "sib_s": s.take(nch, 3),
        "sib_r": s.take(nch, 3),
        "ag_s": s.take(nch, 2, nz),
        "ag_r": s.take(nch, 2, nz),
        "qown": s.take(5),
        "qa_s": s.take(2, 2, nz),
        "qa_r": s.take(2, 2, nz),
        "qs_s": s.take(2, nz),
        "qs_r": s.take(2, nz),
        "rs_s": s.take(2, nz),
        "rs_r": s.take(2, nz),
        "as_s": s.take(3),
        "as_r": s.take(3),
        "ar_s": s.take(3, 2, nz),
        "ar_r": s.take(3, 2, nz),
        "fin_s": s.take(nch),
        "fin_r": s.take(nch),
        "put": s.take(8),
        "cot": s.take(3),
        "tok": s.take(3),
        "ps_s": s.take(4, max(nt, 6)),
        "ps_r": s.take(4, max(nt, 6)),
        "xs_s": s.take(nt),
        "xs_r": s.take(nt),
        "sb_s": s.take(2, nt),
        "sb_r": s.take(2, nt),
        "ga_s": s.take(4, max(nt, 6)),
        "ga_r": s.take(4, max(nt, 6)),
        "gg_s": s.take(nt),
        "gg_r": s.take(nt),
        "loc": s.take(5),
    }
    return s, names


def layer_kernel(
    sizes,
    tok,
    cot,
    w_qkv,
    w_out,
    w_gate,
    w_up,
    w_down,
    pos,
    gain_a,
    gain_f,
    out,
    dtok,
    g_qkv,
    g_out,
    g_gate,
    g_up,
    g_down,
    g_gains,
    w,
    ru,
    rd,
    x,
    ct,
    accp,
    accb,
    acco,
    ht,
    dgt,
    dut,
    resid,
    p1,
    p2,
    sbr_b,
    sbr_p,
    rsb,
    aw,
    qkvb,
    att,
    datt,
    fs,
    st,
    gw,
    gv,
    gg,
    gsib,
    gru,
    grd,
    gt,
    cosine,
    sine,
    sem_ref,
    credit,
):
    nz, nt, nch, tokens, width, hc = sizes
    sems, S = semaphores(nz, nt, nch)
    sems.ref = sem_ref
    ts = tokens // nt
    dps = 2 * nz
    d = lax.axis_index("dp")
    t = lax.axis_index("tensor")
    z = d // 2
    c = d % 2
    sib = (2 * z + 1 - c, t)
    above = (d + 2, t)
    below = (d - 2, t)
    has_above = z < nz - 1
    has_below = z > 0
    seqs = tokens // SEQ
    kv_local = aw_cols(hc) // ((GROUPS + 2) * HD)
    head_cols = (GROUPS + 2) * HD

    def peer(k):
        return lax.rem(t + 1 + k, nt)

    def source(k):
        return lax.rem(t - 1 - k + nt, nt)

    barrier = pltpu.get_barrier_semaphore()
    for k in range(nt - 1):
        pl.semaphore_signal(barrier, inc=1, device_id=(d, peer(k)), device_id_type=MESH)
    pl.semaphore_signal(barrier, inc=1, device_id=sib, device_id_type=MESH)

    @pl.when(has_below)
    def _():
        pl.semaphore_signal(barrier, inc=1, device_id=below, device_id_type=MESH)

    @pl.when(has_above)
    def _():
        pl.semaphore_signal(barrier, inc=1, device_id=above, device_id_type=MESH)

    neighbours = jnp.where(has_below, 1, 0) + jnp.where(has_above, 1, 0)
    pl.semaphore_wait(barrier, nt + neighbours)

    def slot(index):
        return pl.ds(mult(index, ts), ts)

    def core_rows(core):
        return pl.ds(mult(core, tokens), tokens)

    def half_rows(core, index):
        return pl.ds(pl.multiple_of(core * tokens + index * ts, ts), ts)

    def ffn_source(i, core, kind):
        cols = pl.ds(mult(2 * i + core, hc), hc)
        return (w_gate.at[:, cols], w_up.at[:, cols], w_down.at[cols])[kind]

    def own_copy(i, kind):
        return pltpu.make_async_copy(ffn_source(i, c, kind), w.at[i, z, c, kind], S["own"](i, kind))

    def sib_copy(i, kind):
        return remote(
            ffn_source(i, 1 - c, kind), w.at[i, z, c, kind], S["sib_s"](i, kind), S["sib_r"](i, kind), sib
        )

    def sib_wait(i, kind):
        return remote(
            ffn_source(i, c, kind), w.at[i, z, 1 - c, kind], S["sib_s"](i, kind), S["sib_r"](i, kind), sib
        )

    qown = [
        pltpu.make_async_copy(w_qkv.at[:, j * hc : (j + 1) * hc], aw.at[z, c, j], S["qown"](j))
        for j in range(3)
    ] + [
        pltpu.make_async_copy(w_out.at[j * hc : (j + 1) * hc], aw.at[z, c, 3 + j], S["qown"](3 + j))
        for j in range(2)
    ]
    for copy in qown:
        copy.start()
    row16 = lax.broadcasted_iota(jnp.int32, (16, hc), 0)
    gw[z, c] = jnp.where(
        row16 == 0,
        gain_a[...].astype(f32).reshape(1, hc),
        jnp.where(row16 == 1, gain_f[...].astype(f32).reshape(1, hc), 0.0),
    ).astype(bf16)
    tok_all = pltpu.make_async_copy(tok, p2, S["tok"](0))
    tok_all.start()

    def q_ref(part, u, core):
        return (aw if part == 0 else gw).at[u, core]

    def q_line(part, s, direction):
        u = z - s if direction == 0 else z + s
        ref = q_ref(part, u, c)
        return remote(
            ref, ref, S["qa_s"](part, direction, s), S["qa_r"](part, direction, s), (above, below)[direction]
        )

    def q_arrive(part, s, direction):
        u = z - s if direction == 0 else z + s
        ref = q_ref(part, u, c)
        return remote(
            ref,
            ref,
            S["qa_s"](part, direction, s - 1),
            S["qa_r"](part, direction, s - 1),
            (below, above)[direction],
        )

    def q_sib(part, u):
        ref = q_ref(part, u, c)
        return remote(ref, ref, S["qs_s"](part, u), S["qs_r"](part, u), sib)

    def q_sib_in(part, u):
        ref = q_ref(part, u, 1 - c)
        return remote(ref, ref, S["qs_s"](part, u), S["qs_r"](part, u), sib)

    def line_valid(s, direction):
        return z - s >= 0 if direction == 0 else z + s <= nz - 1

    def line_sends(s, direction):
        return line_valid(s, direction) & (has_above if direction == 0 else has_below)

    def q_tick(s):
        if s == 0:
            for copy in qown:
                copy.wait()
        for direction in range(2):
            if s > 0:

                @pl.when(line_valid(s, direction))
                def _():
                    for part in range(2):
                        q_arrive(part, s, direction).wait_recv()

            if s < nz - 1:

                @pl.when(line_sends(s, direction))
                def _():
                    for part in range(2):
                        q_line(part, s, direction).start()

            if s > 0:

                @pl.when(line_valid(s, direction))
                def _():
                    for part in range(2):
                        q_sib(part, z - s if direction == 0 else z + s).start()

        if s == 0:
            for part in range(2):
                q_sib(part, z).start()

    def q_finish():
        for s in range(nz - 1):
            for direction in range(2):

                @pl.when(line_sends(s, direction))
                def _():
                    for part in range(2):
                        q_line(part, s, direction).wait_send()

        for u in range(nz):
            for part in range(2):
                q_sib_in(part, u).wait_recv()

    def ag_line(i, s, direction):
        unit = w.at[i, z - s if direction == 0 else z + s]
        return remote(
            unit, unit, S["ag_s"](i, direction, s), S["ag_r"](i, direction, s), (above, below)[direction]
        )

    def ag_arrive(i, s, direction):
        unit = w.at[i, z - s if direction == 0 else z + s]
        return remote(
            unit,
            unit,
            S["ag_s"](i, direction, s - 1),
            S["ag_r"](i, direction, s - 1),
            (below, above)[direction],
        )

    def ag_tick(i, s):
        if s == 0:
            for kind in range(3):
                own_copy(i, kind).wait()
                sib_wait(i, kind).wait_recv()
        for direction in range(2):
            if s > 0:

                @pl.when(line_valid(s, direction))
                def _():
                    ag_arrive(i, s, direction).wait_recv()

            if s < nz - 1:

                @pl.when(line_sends(s, direction))
                def _():
                    ag_line(i, s, direction).start()

    def ag_finish(i):
        for s in range(nz - 1):
            for direction in range(2):

                @pl.when(line_sends(s, direction))
                def _():
                    ag_line(i, s, direction).wait_send()

    def rs_owner(tau, direction):
        return nz - 1 + z - tau if direction == 0 else tau - (nz - 1 - z)

    def rs_valid(tau, direction):
        return z <= tau if direction == 0 else tau >= nz - 1 - z

    def rs_line(i, tau, direction):
        return remote(
            w.at[i, rs_owner(tau, direction)],
            (ru, rd)[direction].at[tau],
            S["rs_s"](direction, tau),
            S["rs_r"](direction, tau),
            (above, below)[direction],
        )

    def slot_credit(direction, tau):
        return credit.at[direction * nz + tau]

    def take_slot(direction, tau):
        pl.semaphore_wait(slot_credit(direction, tau), 1)

    def at_edge(direction):
        return z == (nz - 2, 1)[direction]

    def rs_send(i, tau, direction):
        if i > 0:
            rs_line(i - 1, tau, direction).wait_send()
            take_slot(direction, tau)
        rs_line(i, tau, direction).start()

    def rs_edge(i):
        for direction in range(2):

            @pl.when(at_edge(direction))
            def _():
                rs_send(i, nz - 2, direction)

    def rs_tick(i, tau, which):
        for direction in range(2):
            got = (ru, rd)[direction]
            back = (below, above)[direction]
            here = rs_valid(tau, direction)
            if which == "mid":
                here = here & has_below & has_above
            if which == "end":
                here = here & ~(has_below & has_above)
            if tau > 0:

                @pl.when(here & (has_below, has_above)[direction])
                def _():
                    owner = rs_owner(tau, direction)
                    remote(
                        w.at[i, owner],
                        got.at[tau - 1],
                        S["rs_s"](direction, tau - 1),
                        S["rs_r"](direction, tau - 1),
                        back,
                    ).wait_recv()

                    def add(k, carry):
                        core, kind = k // 3, k % 3
                        a = w[i, owner, core, kind].astype(f32)
                        b = got[tau - 1, core, kind].astype(f32)
                        w[i, owner, core, kind] = (a + b).astype(bf16)
                        return carry

                    lax.fori_loop(0, 6, add, 0)
                    pl.semaphore_signal(
                        slot_credit(direction, tau - 1), inc=1, device_id=back, device_id_type=MESH
                    )

            if tau < nz - 1:

                sends = here
                if which == "inner" and tau == nz - 2:
                    sends = here & ~at_edge(direction)

                @pl.when(sends)
                def _():
                    rs_send(i, tau, direction)

    def rs_end():
        for tau in range(nz - 1):
            for direction in range(2):

                @pl.when(rs_valid(tau, direction))
                def _():
                    rs_line(nch - 1, tau, direction).wait_send()

    def fin_sib(i):
        return remote(w.at[i, z, 1 - c], fs.at[i], S["fin_s"](i), S["fin_r"](i), sib)

    def fin_in(i):
        return remote(w.at[i, z, c], fs.at[i], S["fin_s"](i), S["fin_r"](i), sib)

    def put_piece(i, half, piece):
        cols = pl.ds(mult(2 * i + half, hc), hc)
        st[0] = piece[0].astype(f32).T
        st[1] = piece[1].astype(f32).T
        st[2] = piece[2].astype(f32)
        puts = (
            pltpu.make_async_copy(st.at[0], g_gate.at[:, cols], S["put"](0)),
            pltpu.make_async_copy(st.at[1], g_up.at[:, cols], S["put"](1)),
            pltpu.make_async_copy(st.at[2], g_down.at[cols], S["put"](2)),
        )
        for copy in puts:
            copy.start()
        for copy in puts:
            copy.wait()

    def fin_start(i):
        fin_sib(i).start()
        put_piece(i, c, w.at[i, z, c])

    def fin_finish(i):
        fin_sib(i).wait_send()
        fin_in(i).wait_recv()
        put_piece(i, 1 - c, fs.at[i])

    def free_first():
        pl.semaphore_signal(credit.at[2 * nz], inc=1, device_id=sib, device_id_type=MESH)

    plan = sums_plan(nz, nch)

    def sums(place):
        for step_ in plan.get(place, ()):
            if step_[0] == "edge":
                rs_edge(step_[1])
            else:
                rs_tick(*step_)

    tile = min(256, tokens)

    def rows_pass(i, core):
        first = i == 0

        def rows_step(m, carry):
            local_rows = pl.ds(mult(m, tile), tile)
            rows = pl.ds(pl.multiple_of(core * tokens + m * tile, tile), tile)
            xm = x[rows, :]
            gate = dot(xm, w[i, :, :, 0].reshape(width, hc))
            up = dot(xm, w[i, :, :, 1].reshape(width, hc))
            dh = jnp.zeros((tile, hc), f32)
            for k in range(dps):
                dh = dh + dot_nt(ct[rows, k * hc : (k + 1) * hc], w[i, k // 2, k % 2, 2])
            sig = jax.nn.sigmoid(gate)
            act = gate * sig
            hidden = (act * up).astype(bf16)
            d_up = (dh * act).astype(bf16)
            d_gate = (dh * up * sig * (1.0 + gate * (1.0 - sig))).astype(bf16)
            ht[:, rows] = hidden.T
            dgt[:, rows] = d_gate.T
            dut[:, rows] = d_up.T
            mine_too = core is c
            for k in range(dps):
                cols = slice(k * hc, (k + 1) * hc)
                fwd = dot(hidden, w[i, k // 2, k % 2, 2])
                back = dot_nt(d_gate, w[i, k // 2, k % 2, 0]) + dot_nt(d_up, w[i, k // 2, k % 2, 1])
                if not first:
                    fwd = accp[rows, cols].astype(f32) + fwd
                    back = (accb if mine_too else acco)[local_rows, cols].astype(f32) + back
                accp[rows, cols] = fwd.astype(bf16)
                if mine_too:
                    accb[local_rows, cols] = back
                else:
                    acco[local_rows, cols] = back.astype(bf16)
            return carry

        lax.fori_loop(0, tokens // tile, rows_step, 0)

    def cols_pass(i):
        def cols_step(k, carry):
            cols = pl.ds(mult(k, hc), hc)
            xs = x[:, cols]
            chip, core = k // 2, k % 2
            w[i, chip, core, 0] = dot(dgt[...], xs).astype(bf16)
            w[i, chip, core, 1] = dot(dut[...], xs).astype(bf16)
            w[i, chip, core, 2] = dot(ht[...], ct[:, cols]).astype(bf16)
            return carry

        lax.fori_loop(0, dps, cols_step, 0)

    lane = lax.broadcasted_iota(jnp.int32, (1, LANES), 1)
    low_head = lane < HD
    low_half = lane % HD < HD // 2

    def turn(u, cos, sin):
        swapped = jnp.where(low_half, pltpu.roll(u, LANES - HD // 2, 1), pltpu.roll(u, HD // 2, 1))
        return u * cos + swapped * sin

    def turn_back(g, cos, sin):
        v = g * sin
        swapped = jnp.where(low_half, pltpu.roll(v, LANES - HD // 2, 1), pltpu.roll(v, HD // 2, 1))
        return g * cos + swapped

    def tables(rows, with_values):
        cos, sin = cosine[rows, :], sine[rows, :]
        if with_values:
            cos, sin = jnp.where(low_head, cos, 1.0), jnp.where(low_head, sin, 0.0)
        return cos, sin

    step = 32

    def norm_rows(src, dst, base, grad_sum):
        def body(m, carry):
            rows = pl.ds(mult(m, step), step)
            v = src[rows, :].astype(f32)
            scale = lax.rsqrt(jnp.mean(v * v, axis=-1, keepdims=True) + epsilon)
            v = v * scale
            dst[pl.ds(pl.multiple_of(base + m * step, step), step), :] = (v * gv[0:1, :]).astype(bf16)
            if grad_sum is None:
                return carry
            up = grad_sum(rows)
            return carry + jnp.sum(up * v, axis=0, keepdims=True)

        start = 0 if grad_sum is None else jnp.zeros((1, width), f32)
        return lax.fori_loop(0, tokens // step, body, start)

    chunks = aw_cols(hc) // LANES
    per_block = hc // LANES
    atile = min(256, tokens)

    def joined():
        def body(m, carry):
            rows = pl.ds(mult(m, atile), atile)
            src = pl.ds(pl.multiple_of(c * tokens + m * atile, atile), atile)
            xm = x[src, :]
            for j in range(3):
                block = dot(xm, aw[:, :, j].reshape(width, hc))
                for q in range(per_block):
                    index = j * per_block + q
                    cos, sin = tables(rows, index % 3 == 2)
                    u = block[:, q * LANES : (q + 1) * LANES]
                    qkvb[rows, index * LANES : (index + 1) * LANES] = turn(u, cos, sin).astype(bf16)
            return carry

        lax.fori_loop(0, tokens // atile, body, 0)

    row_id = lax.broadcasted_iota(jnp.int32, (SEQ, SEQ), 0)
    col_id = lax.broadcasted_iota(jnp.int32, (SEQ, SEQ), 1)
    keep = row_id >= col_id
    inv_root = 1.0 / math.sqrt(HD)

    def doubled(rows, base):
        kv = qkvb[rows, pl.ds(pl.multiple_of(base + GROUPS * HD, LANES), LANES)].astype(f32)
        other = pltpu.roll(kv, HD, 1)
        kk = jnp.where(low_head, kv, other).astype(bf16)
        vv = jnp.where(low_head, other, kv).astype(bf16)
        return kk, vv

    def softmax(qm, kk):
        scores = jnp.where(keep, dot_nt(qm, kk) * inv_root, masked_score)
        e = jnp.exp(scores - jnp.max(scores, axis=-1, keepdims=True))
        return e * (1.0 / jnp.sum(e, axis=-1, keepdims=True))

    def place(n):
        s, h = n // kv_local, n % kv_local
        rows = pl.ds(mult(s, SEQ), SEQ)
        return rows, h * head_cols, h * GROUPS * HD

    def heads_forward():
        def body(n, carry):
            rows, base, qbase = place(n)
            kk, vv = doubled(rows, base)
            for pair in range(GROUPS // 2):
                qp = qkvb[rows, pl.ds(pl.multiple_of(base + pair * LANES, LANES), LANES)]
                halves = []
                for half in range(2):
                    mask = low_head if half == 0 else ~low_head
                    qm = jnp.where(mask, qp.astype(f32), 0.0).astype(bf16)
                    halves.append(dot(softmax(qm, kk).astype(bf16), vv))
                att[rows, pl.ds(pl.multiple_of(qbase + pair * LANES, LANES), LANES)] = jnp.where(
                    low_head, halves[0], halves[1]
                ).astype(bf16)
            return carry

        lax.fori_loop(0, seqs * kv_local, body, 0)

    def heads_backward():
        def body(n, carry):
            rows, base, qbase = place(n)
            kk, vv = doubled(rows, base)
            dkk = jnp.zeros((SEQ, LANES), f32)
            dvv = jnp.zeros((SEQ, LANES), f32)
            cos, sin = tables(rows, False)
            for pair in range(GROUPS // 2):
                cols = pl.ds(pl.multiple_of(base + pair * LANES, LANES), LANES)
                acols = pl.ds(pl.multiple_of(qbase + pair * LANES, LANES), LANES)
                qp = qkvb[rows, cols].astype(f32)
                dp = datt[rows, acols].astype(f32)
                prod = dp * att[rows, acols].astype(f32)
                halves = []
                for half in range(2):
                    mask = low_head if half == 0 else ~low_head
                    qm = jnp.where(mask, qp, 0.0).astype(bf16)
                    dm = jnp.where(mask, dp, 0.0).astype(bf16)
                    probs = softmax(qm, kk)
                    delta = jnp.sum(jnp.where(mask, prod, 0.0), axis=-1, keepdims=True)
                    ds = (probs * (dot_nt(dm, vv) - delta) * inv_root).astype(bf16)
                    halves.append(dot(ds, kk))
                    dkk = dkk + dot(ds.T, qm)
                    dvv = dvv + dot(probs.astype(bf16).T, dm)
                dq = jnp.where(low_head, halves[0], halves[1])
                qkvb[rows, cols] = turn_back(dq, cos, sin).astype(bf16)
            dkk = dkk + pltpu.roll(dkk, HD, 1)
            dvv = dvv + pltpu.roll(dvv, HD, 1)
            cos, sin = tables(rows, True)
            qkvb[rows, pl.ds(pl.multiple_of(base + GROUPS * HD, LANES), LANES)] = turn_back(
                jnp.where(low_head, dkk, dvv), cos, sin
            ).astype(bf16)
            return carry

        lax.fori_loop(0, seqs * kv_local, body, 0)

    def out_weight(k):
        return aw[k // 2, k % 2, 3:5].reshape(2 * hc, hc)

    def attention_partial():
        def body(k, carry):
            cols = pl.ds(mult(k, hc), hc)
            rsb[:, cols] = dot(att[...], out_weight(k)).astype(bf16)
            return carry

        lax.fori_loop(0, dps, body, 0)

    square = nt == 4
    xp, yp, dg = t ^ 1, t ^ 2, t ^ 3
    half = ts // 2

    def part_rows(base, index, upper):
        return pl.ds(pl.multiple_of(base + index * ts + upper * half, half), half)

    def slice_rows(base, index):
        return pl.ds(pl.multiple_of(base + index * ts, ts), ts)

    def reduce_copy(src, base, land, which, n):
        rows = (
            part_rows(base, xp, 0),
            part_rows(base, dg, 0),
            part_rows(base, yp, 1),
            part_rows(base, dg, 1),
            part_rows(base, yp, 0),
            part_rows(base, xp, 1),
        )[n]
        to = (xp, xp, yp, yp, yp, xp)[n]
        return remote(
            src.at[rows],
            land.at[pl.ds(n * half, half)],
            S["ps_s"](which, n),
            S["ps_r"](which, n),
            (d, to),
        )

    def reduce_direct(src, base, land, which, k, arriving):
        frm = source(k)
        return remote(
            src.at[slice_rows(base, peer(k))],
            land.at[slot(frm if arriving else t)],
            S["ps_s"](which, k),
            S["ps_r"](which, k),
            (d, frm if arriving else peer(k)),
        )

    def reduce_start(src, base, land, which):
        if square:
            for n in range(4):
                reduce_copy(src, base, land, which, n).start()
        else:
            for k in range(nt - 1):
                reduce_direct(src, base, land, which, k, False).start()

    def reduce_mid(src, base, land, which):
        if not square:
            return
        for n, index, upper in ((1, yp, 0), (3, xp, 1)):
            reduce_copy(src, base, land, which, n).wait_recv()
            rows = part_rows(base, index, upper)
            both = src[rows, :].astype(f32) + land[n * half : (n + 1) * half, :].astype(f32)
            src[rows, :] = both.astype(bf16)
            reduce_copy(src, base, land, which, 4 if n == 1 else 5).start()

    def reduce_wait(src, base, land, which):
        if square:
            for n in (0, 2, 4, 5):
                reduce_copy(src, base, land, which, n).wait_recv()
        else:
            for k in range(nt - 1):
                reduce_direct(src, base, land, which, k, True).wait_recv()

    def reduce_end(src, base, land, which):
        if square:
            for n in range(6):
                reduce_copy(src, base, land, which, n).wait_send()
        else:
            for k in range(nt - 1):
                reduce_direct(src, base, land, which, k, False).wait_send()

    def summed(src, base, land, m):
        total = src[pl.ds(pl.multiple_of(base + t * ts + m * step, step), step), :].astype(f32)
        if square:
            upper = m // (half // step)
            inner = (m % (half // step)) * step
            for first in (2 * upper * half, (4 + upper) * half):
                total = total + land[pl.ds(pl.multiple_of(first + inner, step), step), :].astype(f32)
        else:
            for k in range(nt - 1):
                rows = pl.ds(pl.multiple_of(source(k) * ts + m * step, step), step)
                total = total + land[rows, :].astype(f32)
        return total

    def spread_copy(src, src_base, dst, dst_base, which, n):
        index, upper, to = (
            (t, 0, xp),
            (t, 1, xp),
            (t, 1, yp),
            (t, 0, yp),
            (xp, 0, yp),
            (yp, 1, xp),
        )[n]
        from_rows = part_rows(src_base, t, upper) if n < 4 else part_rows(dst_base, index, upper)
        return remote(
            (src if n < 4 else dst).at[from_rows],
            dst.at[part_rows(dst_base, index, upper)],
            S["ga_s"](which, n),
            S["ga_r"](which, n),
            (d, to),
        )

    def spread_arrive(src, src_base, dst, dst_base, which, n):
        index, upper, frm = (
            (xp, 0, xp),
            (xp, 1, xp),
            (yp, 1, yp),
            (yp, 0, yp),
            (dg, 0, yp),
            (dg, 1, xp),
        )[n]
        return remote(
            src.at[part_rows(src_base, t, upper)],
            dst.at[part_rows(dst_base, index, upper)],
            S["ga_s"](which, n),
            S["ga_r"](which, n),
            (d, frm),
        )

    def spread_direct(src, src_base, dst, dst_base, which, k, arriving):
        frm = source(k)
        return remote(
            src.at[slice_rows(src_base, t)],
            dst.at[slice_rows(dst_base, frm if arriving else t)],
            S["ga_s"](which, k),
            S["ga_r"](which, k),
            (d, frm if arriving else peer(k)),
        )

    def spread_start(*args):
        if square:
            for n in range(4):
                spread_copy(*args, n).start()
        else:
            for k in range(nt - 1):
                spread_direct(*args, k, False).start()

    def spread_mid(*args):
        if square:
            for n, onward in ((0, 4), (2, 5)):
                spread_arrive(*args, n).wait_recv()
                spread_copy(*args, onward).start()

    def spread_wait(*args):
        if square:
            for n in (1, 3, 4, 5):
                spread_arrive(*args, n).wait_recv()
        else:
            for k in range(nt - 1):
                spread_direct(*args, k, True).wait_recv()

    def spread_end(*args):
        if square:
            for n in range(6):
                spread_copy(*args, n).wait_send()
        else:
            for k in range(nt - 1):
                spread_direct(*args, k, False).wait_send()

    q_tick(0)
    for i in range(nch):
        for kind in range(3):
            own_copy(i, kind).start()
            sib_copy(i, kind).start()
    cot_own = pltpu.make_async_copy(cot, ct.at[core_rows(c)], S["cot"](0))
    cot_sib = remote(cot, ct.at[core_rows(c)], S["cot"](1), S["cot"](2), sib)
    cot_in = remote(cot, ct.at[core_rows(1 - c)], S["cot"](1), S["cot"](2), sib)
    cot_own.start()
    cot_sib.start()
    quarter = HD // 2
    exponent = lax.broadcasted_iota(jnp.int32, (quarter, 1), 0).astype(f32) * (2.0 / HD)
    angles = jnp.exp(exponent * -math.log(rope_base)) * pos[...].astype(f32)
    cos_rows, sin_rows = jnp.cos(angles), jnp.sin(angles)
    cosine[...] = jnp.concatenate([cos_rows] * (LANES // quarter), axis=0).T
    sine[...] = jnp.concatenate([-sin_rows, sin_rows] * (LANES // HD), axis=0).T
    for s in range(1, nz):
        if s == nz - 1:
            ag_tick(0, 0)
        q_tick(s)
    if nz == 1:
        ag_tick(0, 0)
    q_finish()
    for k in range(dps):
        gv[:, k * hc : (k + 1) * hc] = gw[k // 2, k % 2].astype(f32)
    tok_all.wait()
    norm_rows(p2, x, c * tokens, None)
    joined()
    heads_forward()
    if nz > 1:
        ag_tick(0, 1)
    attention_partial()
    first_sum = (rsb, 0, p1, 0)
    reduce_start(*first_sum)
    if nz > 2:
        ag_tick(0, 2)
    reduce_mid(*first_sum)
    if nz > 3:
        ag_tick(1, 0)
    reduce_wait(*first_sum)
    mine = half_rows(c, t)

    def second_norm(m, carry):
        rows = pl.ds(mult(m, step), step)
        trow = pl.ds(pl.multiple_of(t * ts + m * step, step), step)
        total = p2[trow, :].astype(f32) + summed(rsb, 0, p1, m)
        resid[rows, :] = total
        scale = lax.rsqrt(jnp.mean(total * total, axis=-1, keepdims=True) + epsilon)
        x[pl.ds(pl.multiple_of(c * tokens + t * ts + m * step, step), step), :] = (
            total * scale * gv[1:2, :]
        ).astype(bf16)
        return carry

    lax.fori_loop(0, ts // step, second_norm, 0)
    x_spread = (x, c * tokens, x, c * tokens, 3)

    def xs_index(k):
        if square:
            return (t, xp, yp, dg)[k]
        return lax.rem(t - k + nt, nt)

    def xs_copy(k):
        rows = half_rows(c, xs_index(k))
        return remote(x.at[rows], x.at[rows], S["xs_s"](k), S["xs_r"](k), sib)

    def xs_in(k):
        rows = half_rows(1 - c, xs_index(k))
        return remote(x.at[rows], x.at[rows], S["xs_s"](k), S["xs_r"](k), sib)

    spread_start(*x_spread)
    xs_copy(0).start()
    spread_mid(*x_spread)
    if square:
        spread_arrive(*x_spread, 1).wait_recv()
        xs_copy(1).start()
        spread_arrive(*x_spread, 3).wait_recv()
        xs_copy(2).start()
    for s in range(3, nz):
        ag_tick(0, s)
    ag_finish(0)
    if nz <= 3:
        ag_tick(1, 0)
    if square:
        for n in (4, 5):
            spread_arrive(*x_spread, n).wait_recv()
        xs_copy(3).start()
    else:
        for k in range(nt - 1):
            spread_direct(*x_spread, k, True).wait_recv()
            xs_copy(k + 1).start()
    cot_own.wait()
    cot_in.wait_recv()
    for k in range(nt):
        xs_in(k).wait_recv()

    last = nch - 1
    other = (1 - c) * tokens
    for i in range(last):
        if i > 0:
            ag_tick(i + 1, 0)
        sums(4 * i - 1)
        rows_pass(i, 1 - c)
        rows_pass(i, c)
        cols_pass(i)
        sums(4 * i)
        for s in range(1, nz):
            ag_tick(i + 1, s)
            if s < 3:
                sums(4 * i + s)
        ag_finish(i + 1)

    def sib_b(k):
        return remote(acco.at[slot(k)], sbr_b.at[slot(k)], S["sb_s"](0, k), S["sb_r"](0, k), sib)

    def sib_p(k):
        return remote(
            accp.at[half_rows(1 - c, k)], sbr_p.at[slot(k)], S["sb_s"](1, k), S["sb_r"](1, k), sib
        )

    for u in range(nz):
        for part in range(2):
            q_sib(part, u).wait_send()
    spread_end(*x_spread)
    reduce_end(*first_sum)
    for k in range(nt):
        xs_copy(k).wait_send()
    sums(4 * last - 1)
    rows_pass(last, 1 - c)
    for k in range(nt):
        sib_b(k).start()
    rows_pass(last, c)
    for k in range(nt):
        sib_b(k).wait_recv()

    def pair_b(m, carry):
        rows = pl.ds(mult(m, step), step)
        rsb[rows, :] = (accb[rows, :] + sbr_b[rows, :].astype(f32)).astype(bf16)
        return carry

    lax.fori_loop(0, tokens // step, pair_b, 0)
    back_sum = (rsb, 0, p2, 1)
    reduce_start(*back_sum)
    cols_pass(last)
    sums(4 * last)
    for k in range(nt):
        sib_p(k).start()
    reduce_mid(*back_sum)
    sums(4 * last + 1)
    reduce_wait(*back_sum)

    def second_back(m, carry):
        rows = pl.ds(mult(m, step), step)
        place_ = pl.ds(pl.multiple_of(c * tokens + t * ts + m * step, step), step)
        up = summed(rsb, 0, p2, m)
        v = resid[rows, :]
        scale = lax.rsqrt(jnp.mean(v * v, axis=-1, keepdims=True) + epsilon)
        weighted = up * gv[1:2, :]
        inner = jnp.mean(weighted * v, axis=-1, keepdims=True)
        grad = ct[place_, :].astype(f32) + scale * weighted - v * (scale * scale * scale) * inner
        accb[rows, :] = grad
        x[place_, :] = grad.astype(bf16)
        return carry + jnp.sum(up * v * scale, axis=0, keepdims=True)

    gain_two = lax.fori_loop(0, ts // step, second_back, jnp.zeros((1, width), f32))
    rg_spread = (x, c * tokens, x, c * tokens, 0)
    spread_start(*rg_spread)
    spread_mid(*rg_spread)
    sums(4 * last + 2)
    reduce_end(*back_sum)
    for k in range(nt):
        sib_p(k).wait_recv()

    def pair_p(m, carry):
        rows = pl.ds(mult(m, step), step)
        here = pl.ds(pl.multiple_of(c * tokens + m * step, step), step)
        rsb[rows, :] = (accp[here, :].astype(f32) + sbr_p[rows, :].astype(f32)).astype(bf16)
        return carry

    lax.fori_loop(0, tokens // step, pair_p, 0)

    spread_wait(*rg_spread)
    out_sum = (rsb, 0, p1, 2)
    reduce_start(*out_sum)
    sums(4 * last + 3)
    fin_start(0)

    def d_attended(m, carry):
        rows = pl.ds(mult(m, atile), atile)
        src = pl.ds(pl.multiple_of(c * tokens + m * atile, atile), atile)
        for j in range(2):
            total = jnp.zeros((atile, hc), f32)
            for k in range(dps):
                total = total + dot_nt(x[src, k * hc : (k + 1) * hc], aw[k // 2, k % 2, 3 + j])
            datt[rows, j * hc : (j + 1) * hc] = total.astype(bf16)
        for j in range(2):
            (ht, dgt)[j][:, rows] = att[rows, j * hc : (j + 1) * hc].T
        return carry

    lax.fori_loop(0, tokens // atile, d_attended, 0)

    def out_grads(k, carry):
        xs = x[core_rows(c), pl.ds(mult(k, hc), hc)]
        for j in range(2):
            aw[k // 2, k % 2, 3 + j] = dot((ht, dgt)[j][:, :tokens], xs).astype(bf16)
        return carry

    lax.fori_loop(0, dps, out_grads, 0)

    def a_src(part, u, core):
        return (aw.at[u, core, 3:5], aw.at[u, core, 0:3], gg.at[u, core])[part]

    def a_sib_ref(part):
        return (w.at[0, :, 1, 0:2], w.at[0, :, 0], gsib)[part]

    def a_sib(part):
        src = (aw.at[:, 1 - c, 3:5], aw.at[:, 1 - c, 0:3], gg.at[:, 1 - c])[part]
        return remote(src, a_sib_ref(part), S["as_s"](part), S["as_r"](part), sib)

    def a_land(part, direction, tau):
        line = (ru, rd)[direction]
        return (line.at[tau, 1, 0:2], line.at[tau, 0], (gru, grd)[direction].at[tau])[part]

    def a_line(part, tau, direction):
        return remote(
            a_src(part, rs_owner(tau, direction), c),
            a_land(part, direction, tau),
            S["ar_s"](part, direction, tau),
            S["ar_r"](part, direction, tau),
            (above, below)[direction],
        )

    def a_add(part, owner, got):
        if part == 2:
            gg[owner, c] = gg[owner, c] + got[...]
            return
        base, count = ((3, 2), (0, 3))[part]
        for j in range(count):
            both = aw[owner, c, base + j].astype(f32) + got[j].astype(f32)
            aw[owner, c, base + j] = both.astype(bf16)

    def a_pair(part):
        a_sib(part).wait_recv()

        def body(u, carry):
            a_add(part, u, (w.at[0, u, 1, 0:2], w.at[0, u, 0], gsib.at[u])[part])
            return carry

        lax.fori_loop(0, nz, body, 0)

    def a_tick(part, tau):
        for direction in range(2):
            if tau > 0:

                @pl.when(rs_valid(tau, direction) & (has_below, has_above)[direction])
                def _():
                    owner = rs_owner(tau, direction)
                    remote(
                        a_src(part, owner, c),
                        a_land(part, direction, tau - 1),
                        S["ar_s"](part, direction, tau - 1),
                        S["ar_r"](part, direction, tau - 1),
                        (below, above)[direction],
                    ).wait_recv()
                    a_add(part, owner, a_land(part, direction, tau - 1))

            if tau < nz - 1:

                @pl.when(rs_valid(tau, direction))
                def _():
                    if part == 0:
                        take_slot(direction, tau)
                    a_line(part, tau, direction).start()

    def a_finish(part):
        a_sib(part).wait_send()
        for tau in range(nz - 1):
            for direction in range(2):

                @pl.when(rs_valid(tau, direction))
                def _():
                    a_line(part, tau, direction).wait_send()

    fin_finish(0)
    free_first()
    pl.semaphore_wait(credit.at[2 * nz], 1)
    a_sib(0).start()
    tok_again = pltpu.make_async_copy(tok, sbr_b, S["tok"](1))
    tok_again.start()
    a_pair(0)
    sums(4 * last + 4)
    heads_backward()

    def attn_back(k, carry):
        total = jnp.zeros((tokens, hc), f32)
        for j in range(3):
            total = total + dot_nt(qkvb[:, j * hc : (j + 1) * hc], aw[k // 2, k % 2, j])
        x[pl.ds(mult(1 - c, tokens), tokens), pl.ds(mult(k, hc), hc)] = total.astype(bf16)
        return carry

    lax.fori_loop(0, dps, attn_back, 0)
    tail_sum = (x, other, p2, 3)
    reduce_start(*tail_sum)
    reduce_mid(*out_sum)
    sums(4 * last + 5)
    tok_again.wait()

    def own_back(rows):
        return x[pl.ds(pl.multiple_of(other + rows.start, step), step), :].astype(f32)

    gain_one = norm_rows(sbr_b, sbr_p, 0, own_back)
    for k in range(dps):
        cols = slice(k * hc, (k + 1) * hc)
        gg[k // 2, k % 2] = jnp.concatenate(
            [gain_one[:, cols], gain_two[:, cols], jnp.zeros((6, hc), f32)], axis=0
        )
    a_sib(2).start()
    for m in range(tokens // atile):
        for j in range(3):
            (ht, dgt, dut)[j][:, tokens + m * atile : tokens + (m + 1) * atile] = qkvb[
                m * atile : (m + 1) * atile, j * hc : (j + 1) * hc
            ].T

    def qkv_grads(k, carry):
        xs = sbr_p[:, pl.ds(mult(k, hc), hc)]
        for j in range(3):
            aw[k // 2, k % 2, j] = dot((ht, dgt, dut)[j][:, tokens:], xs).astype(bf16)
        return carry

    lax.fori_loop(0, dps, qkv_grads, 0)
    a_sib(1).start()
    sums(4 * last + 6)
    a_tick(0, 0)
    a_pair(1)
    a_pair(2)
    a_tick(1, 0)
    a_tick(2, 0)
    fin_start(1)

    reduce_mid(*tail_sum)
    reduce_wait(*out_sum)

    def finish_output(m, carry):
        rows = pl.ds(mult(m, step), step)
        where = pl.ds(pl.multiple_of(c * tokens + t * ts + m * step, step), step)
        accp[where, :] = (resid[rows, :] + summed(rsb, 0, p1, m)).astype(bf16)
        return carry

    lax.fori_loop(0, ts // step, finish_output, 0)
    out_spread = (accp, c * tokens, out, 0, 1)
    spread_start(*out_spread)
    put_out = pltpu.make_async_copy(accp.at[mine], out.at[slot(t)], S["loc"](0))
    put_out.start()
    sums(4 * last + 7)

    reduce_wait(*tail_sum)
    for k in range(nt):
        sib_p(k).wait_send()
    theirs = half_rows(1 - c, t)

    def finish_tokens(m, carry):
        rows = pl.ds(mult(m, step), step)
        up = summed(x, other, p2, m)
        v = sbr_b[pl.ds(pl.multiple_of(t * ts + m * step, step), step), :].astype(f32)
        scale = lax.rsqrt(jnp.mean(v * v, axis=-1, keepdims=True) + epsilon)
        weighted = up * gv[0:1, :]
        inner = jnp.mean(weighted * v, axis=-1, keepdims=True)
        grad = accb[rows, :] + scale * weighted - v * (scale * scale * scale) * inner
        accp[pl.ds(pl.multiple_of(other + t * ts + m * step, step), step), :] = grad.astype(bf16)
        return carry

    lax.fori_loop(0, ts // step, finish_tokens, 0)
    tok_spread = (accp, other, dtok, 0, 2)
    spread_start(*tok_spread)
    put_tok = pltpu.make_async_copy(accp.at[theirs], dtok.at[slot(t)], S["loc"](1))
    put_tok.start()
    fin_finish(1)
    spread_mid(*out_spread)
    spread_mid(*tok_spread)
    sums(4 * last + 8)
    for part in range(3):
        a_tick(part, 1)
    fin_start(2)
    fin_finish(2)
    sums(4 * last + 9)
    for s in range(2, nz):
        for part in range(3):
            a_tick(part, s)
        if s == nz - 2:
            fin_start(3)
    fin_finish(3)

    def gain_copy(k):
        return remote(gg.at[z, c], gt.at[t], S["gg_s"](k), S["gg_r"](k), (d, peer(k)))

    def gain_in(k):
        return remote(gg.at[z, c], gt.at[source(k)], S["gg_s"](k), S["gg_r"](k), (d, source(k)))

    for k in range(nt - 1):
        gain_copy(k).start()
    gt[t] = gg[z, c]

    base = ts
    for j in range(3):
        accb[base : base + hc, j * hc : (j + 1) * hc] = aw[z, c, j].astype(f32).T
    for j in range(2):
        accb[base : base + hc, (3 + j) * hc : (4 + j) * hc] = aw[z, c, 3 + j].astype(f32)
    put_qkv = pltpu.make_async_copy(accb.at[base : base + hc, 0 : 3 * hc], g_qkv, S["loc"](2))
    put_o = [
        pltpu.make_async_copy(
            accb.at[base : base + hc, (3 + j) * hc : (4 + j) * hc],
            g_out.at[j * hc : (j + 1) * hc],
            S["loc"](3 + j),
        )
        for j in range(2)
    ]
    put_qkv.start()
    for copy in put_o:
        copy.start()
    for k in range(nt - 1):
        gain_in(k).wait_recv()
    total = gt[0]
    for k in range(1, nt):
        total = total + gt[k]
    g_gains[...] = total

    for i in range(nch):
        for kind in range(3):
            sib_copy(i, kind).wait_send()
    cot_sib.wait_send()
    for part in range(3):
        a_finish(part)
    for k in range(nt - 1):
        gain_copy(k).wait_send()
    for k in range(nt):
        sib_b(k).wait_send()
    rs_end()
    reduce_end(*out_sum)
    reduce_end(*tail_sum)
    spread_wait(*out_spread)
    spread_wait(*tok_spread)
    for args in (rg_spread, out_spread, tok_spread):
        spread_end(*args)
    put_out.wait()
    put_tok.wait()
    put_qkv.wait()
    for copy in put_o:
        copy.wait()


def aw_cols(shard):
    return 3 * shard


def layer(tokens, cotangent, weights, positions, gain_a, gain_f, nz, nt):
    count, width = tokens.shape
    hc, hid = weights[2].shape
    nch = hid // (2 * hc)
    ts = count // nt
    sizes = (nz, nt, nch, count, width, hc)
    sems, _ = semaphores(nz, nt, nch)
    V = pltpu.VMEM
    recv = (nz - 1, 2, 3, hc, hc)
    S = jax.ShapeDtypeStruct
    return pl.pallas_call(
        functools.partial(layer_kernel, sizes),
        out_shape=(
            S((count, width), bf16),
            S((count, width), bf16),
            S((hc, 3 * hc), f32),
            S((2 * hc, hc), f32),
            S((hc, hid), f32),
            S((hc, hid), f32),
            S((hid, hc), f32),
            S((8, hc), f32),
        ),
        in_specs=[HBM] * 7 + [VMEM] * 3,
        out_specs=(HBM, HBM, HBM, HBM, HBM, HBM, HBM, VMEM),
        scratch_shapes=[
            V((nch, nz, 2, 3, hc, hc), bf16),
            V(recv, bf16),
            V(recv, bf16),
            V((2 * count, width), bf16),
            V((2 * count, width), bf16),
            V((2 * count, width), bf16),
            V((count, width), f32),
            V((count, width), bf16),
            V((hc, 2 * count), bf16),
            V((hc, 2 * count), bf16),
            V((hc, 2 * count), bf16),
            V((ts, width), f32),
            V((count, width), bf16),
            V((count, width), bf16),
            V((count, width), bf16),
            V((count, width), bf16),
            V((count, width), bf16),
            V((nz, 2, 5, hc, hc), bf16),
            V((count, 3 * hc), bf16),
            V((count, 2 * hc), bf16),
            V((count, 2 * hc), bf16),
            V((nch, 3, hc, hc), bf16),
            V((3, hc, hc), f32),
            V((nz, 2, 16, hc), bf16),
            V((16, width), f32),
            V((nz, 2, 8, hc), f32),
            V((nz, 8, hc), f32),
            V((nz - 1, 8, hc), f32),
            V((nz - 1, 8, hc), f32),
            V((nt, 8, hc), f32),
            V((count, LANES), f32),
            V((count, LANES), f32),
            pltpu.SemaphoreType.DMA((sems.count,)),
            pltpu.SemaphoreType.REGULAR((2 * nz + 1,)),
        ],
        compiler_params=pltpu.CompilerParams(
            collective_id=0, has_side_effects=True, vmem_limit_bytes=63 * 2**20
        ),
        name="layer",
    )(tokens, cotangent, *weights, positions, gain_a, gain_f)


def copy_kernel(count, parts, *refs):
    sources, gains = refs[:count], refs[count]
    results, gain_outs = refs[count + 1 : 2 * count + 1], refs[2 * count + 1 : 2 * count + 3]
    held, sem = refs[2 * count + 3 : 3 * count + 3], refs[-1]
    loads, stores = [], []
    for n in range(count):
        rows = sources[n].shape[0] // parts
        for k in range(parts):
            at = pl.ds(k * rows, rows)
            place = sem.at[n * parts + k]
            loads.append(pltpu.make_async_copy(sources[n].at[at], held[n].at[at], place))
            stores.append(pltpu.make_async_copy(held[n].at[at], results[n].at[at], place))
    for copy in loads:
        copy.start()
    for n in range(2):
        gain_outs[n][...] = gains[n, :]
    for load, store in zip(loads, stores):
        load.wait()
        store.start()
    for copy in stores:
        copy.wait()


def copied(arrays, gains):
    count, parts = len(arrays), 2
    shapes = [jax.ShapeDtypeStruct(a.shape, a.dtype) for a in arrays]
    return pl.pallas_call(
        functools.partial(copy_kernel, count, parts),
        out_shape=shapes + [jax.ShapeDtypeStruct(gains.shape[1:], f32)] * 2,
        in_specs=[HBM] * count + [VMEM],
        out_specs=[HBM] * count + [VMEM] * 2,
        scratch_shapes=[pltpu.VMEM(a.shape, a.dtype) for a in arrays]
        + [pltpu.SemaphoreType.DMA((count * parts,))],
        compiler_params=pltpu.CompilerParams(vmem_limit_bytes=60 * 2**20),
        name="results",
    )(*arrays, gains)


def local(tokens, positions, w_qkv, w_out, w_gate, w_up, w_down, gain_attn, gain_ffn, cotangent):
    nz = lax.axis_size("dp") // 2
    nt = lax.axis_size("tensor")
    results = layer(
        tokens,
        cotangent,
        (w_qkv, w_out, w_gate, w_up, w_down),
        positions.reshape(1, -1),
        gain_attn,
        gain_ffn,
        nz,
        nt,
    )
    return tuple(copied(results[:-1], results[-1]))


def solution(mesh):
    return jax.shard_map(
        local,
        mesh=mesh,
        in_specs=(
            P("dp", None),
            P("dp"),
            P("dp", "tensor"),
            P("tensor", "dp"),
            P("dp", "tensor"),
            P("dp", "tensor"),
            P("tensor", "dp"),
            P("dp"),
            P("dp"),
            P("dp", None),
        ),
        out_specs=(
            P("dp", None),
            P("dp", None),
            P("dp", "tensor"),
            P("tensor", "dp"),
            P("dp", "tensor"),
            P("dp", "tensor"),
            P("tensor", "dp"),
            P("dp"),
            P("dp"),
        ),
        check_vma=False,
    )
```

```python
import functools
import math

import jax
import jax.numpy as jnp
from jax import lax
from jax.experimental import pallas as pl
from jax.experimental.pallas import tpu as pltpu
from jax.sharding import PartitionSpec as P

HEADS = 32
KV_HEADS = 8
HD = 64
SEQ = 256
GROUPS = HEADS // KV_HEADS
LANES = 128

epsilon = 1e-05
rope_base = 500000.0
masked_score = -1e30

MESH = pl.DeviceIdType.MESH
HBM = pl.BlockSpec(memory_space=pl.ANY)
VMEM = pl.BlockSpec(memory_space=pltpu.VMEM)
bf16 = jnp.bfloat16
f32 = jnp.float32
NT_DIMS = (((1,), (1,)), ((), ()))


def remote(src, dst, send, recv, device):
    return pltpu.make_async_remote_copy(
        src_ref=src, dst_ref=dst, send_sem=send, recv_sem=recv, device_id=device, device_id_type=MESH
    )


def mult(value, factor):
    return pl.multiple_of(value * factor, factor)


def dot(a, b):
    return jnp.dot(a, b, preferred_element_type=f32)


def dot_nt(a, b):
    return lax.dot_general(a, b, NT_DIMS, preferred_element_type=f32)


def sums_plan(nz, nch):
    last = nch - 1
    if (nz, nch) != (4, 4):
        plan = {}
        for r in range(last + nz):
            hops = [(i, r - i, "all") for i in range(nch) if 0 <= r - i < nz]
            plan.setdefault(4 * r if r <= last else 4 * last + 3, []).extend(hops)
        return plan
    return {
        1: [(0, 0, "all")],
        2: [(0, 1, "all")],
        5: [(0, 2, "inner")],
        6: [(1, 0, "all")],
        7: [(0, 3, "mid")],
        9: [(1, 1, "all"), (2, 0, "all")],
        10: [("edge", 0), (1, 2, "inner"), (2, 1, "all")],
        13: [(0, 3, "end"), ("edge", 1), (3, 0, "all")],
        14: [(1, 3, "mid"), (2, 2, "inner")],
        16: [(3, 1, "all")],
        17: [(1, 3, "end"), ("edge", 2)],
        18: [(2, 3, "mid"), (3, 2, "inner")],
        19: [(2, 3, "end"), ("edge", 3)],
        21: [(3, 3, "mid"), (3, 3, "end")],
    }


class Sems:
    def __init__(self):
        self.count = 0
        self.ref = None

    def take(self, *dims):
        base = self.count
        self.count += math.prod(dims)

        def at(*index):
            flat = 0
            for size, place in zip(dims, index):
                flat = flat * size + place
            return self.ref.at[base + flat]

        return at


def semaphores(nz, nt, nch):
    s = Sems()
    names = {
        "own": s.take(nch, 3),
        "sib_s": s.take(nch, 3),
        "sib_r": s.take(nch, 3),
        "ag_s": s.take(nch, 2, nz),
        "ag_r": s.take(nch, 2, nz),
        "qown": s.take(5),
        "qa_s": s.take(2, 2, nz),
        "qa_r": s.take(2, 2, nz),
        "qs_s": s.take(2, nz),
        "qs_r": s.take(2, nz),
        "rs_s": s.take(2, nz),
        "rs_r": s.take(2, nz),
        "as_s": s.take(3),
        "as_r": s.take(3),
        "ar_s": s.take(3, 2, nz),
        "ar_r": s.take(3, 2, nz),
        "fin_s": s.take(nch),
        "fin_r": s.take(nch),
        "put": s.take(nch),
        "cot": s.take(3),
        "tok": s.take(3),
        "ps_s": s.take(4, max(nt, 6)),
        "ps_r": s.take(4, max(nt, 6)),
        "xs_s": s.take(nt),
        "xs_r": s.take(nt),
        "sb_s": s.take(2, nt),
        "sb_r": s.take(2, nt),
        "ga_s": s.take(4, max(nt, 6)),
        "ga_r": s.take(4, max(nt, 6)),
        "gg_s": s.take(nt),
        "gg_r": s.take(nt),
        "loc": s.take(5),
    }
    return s, names


def layer_kernel(
    sizes,
    tok,
    cot,
    w_qkv,
    w_out,
    w_gate,
    w_up,
    w_down,
    pos,
    gain_a,
    gain_f,
    out,
    dtok,
    g_attn,
    g_ffn,
    g_gains,
    w,
    ru,
    rd,
    x,
    ct,
    accp,
    accb,
    acco,
    ht,
    dgt,
    dut,
    resid,
    p1,
    p2,
    sbr_b,
    sbr_p,
    rsb,
    aw,
    qkvb,
    att,
    datt,
    gw,
    gv,
    gg,
    gsib,
    gru,
    grd,
    gt,
    cosine,
    sine,
    sem_ref,
    credit,
):
    nz, nt, nch, tokens, width, hc = sizes
    sems, S = semaphores(nz, nt, nch)
    sems.ref = sem_ref
    ts = tokens // nt
    dps = 2 * nz
    d = lax.axis_index("dp")
    t = lax.axis_index("tensor")
    z = d // 2
    c = d % 2
    sib = (2 * z + 1 - c, t)
    above = (d + 2, t)
    below = (d - 2, t)
    has_above = z < nz - 1
    has_below = z > 0
    seqs = tokens // SEQ
    kv_local = aw_cols(hc) // ((GROUPS + 2) * HD)
    head_cols = (GROUPS + 2) * HD

    def peer(k):
        return lax.rem(t + 1 + k, nt)

    def source(k):
        return lax.rem(t - 1 - k + nt, nt)

    barrier = pltpu.get_barrier_semaphore()
    for k in range(nt - 1):
        pl.semaphore_signal(barrier, inc=1, device_id=(d, peer(k)), device_id_type=MESH)
    pl.semaphore_signal(barrier, inc=1, device_id=sib, device_id_type=MESH)

    @pl.when(has_below)
    def _():
        pl.semaphore_signal(barrier, inc=1, device_id=below, device_id_type=MESH)

    @pl.when(has_above)
    def _():
        pl.semaphore_signal(barrier, inc=1, device_id=above, device_id_type=MESH)

    neighbours = jnp.where(has_below, 1, 0) + jnp.where(has_above, 1, 0)
    pl.semaphore_wait(barrier, nt + neighbours)

    def slot(index):
        return pl.ds(mult(index, ts), ts)

    def core_rows(core):
        return pl.ds(mult(core, tokens), tokens)

    def half_rows(core, index):
        return pl.ds(pl.multiple_of(core * tokens + index * ts, ts), ts)

    def ffn_source(i, core, kind):
        cols = pl.ds(mult(2 * i + core, hc), hc)
        return (w_gate.at[:, cols], w_up.at[:, cols], w_down.at[cols])[kind]

    def own_copy(i, kind):
        return pltpu.make_async_copy(ffn_source(i, c, kind), w.at[i, z, c, kind], S["own"](i, kind))

    def sib_copy(i, kind):
        return remote(
            ffn_source(i, 1 - c, kind), w.at[i, z, c, kind], S["sib_s"](i, kind), S["sib_r"](i, kind), sib
        )

    def sib_wait(i, kind):
        return remote(
            ffn_source(i, c, kind), w.at[i, z, 1 - c, kind], S["sib_s"](i, kind), S["sib_r"](i, kind), sib
        )

    qown = [
        pltpu.make_async_copy(w_qkv.at[:, j * hc : (j + 1) * hc], aw.at[z, c, j], S["qown"](j))
        for j in range(3)
    ] + [
        pltpu.make_async_copy(w_out.at[j * hc : (j + 1) * hc], aw.at[z, c, 3 + j], S["qown"](3 + j))
        for j in range(2)
    ]
    for copy in qown:
        copy.start()
    row16 = lax.broadcasted_iota(jnp.int32, (16, hc), 0)
    gw[z, c] = jnp.where(
        row16 == 0,
        gain_a[...].astype(f32).reshape(1, hc),
        jnp.where(row16 == 1, gain_f[...].astype(f32).reshape(1, hc), 0.0),
    ).astype(bf16)
    tok_all = pltpu.make_async_copy(tok, p2, S["tok"](0))
    tok_all.start()

    def q_ref(part, u, core):
        return (aw if part == 0 else gw).at[u, core]

    def q_line(part, s, direction):
        u = z - s if direction == 0 else z + s
        ref = q_ref(part, u, c)
        return remote(
            ref, ref, S["qa_s"](part, direction, s), S["qa_r"](part, direction, s), (above, below)[direction]
        )

    def q_arrive(part, s, direction):
        u = z - s if direction == 0 else z + s
        ref = q_ref(part, u, c)
        return remote(
            ref,
            ref,
            S["qa_s"](part, direction, s - 1),
            S["qa_r"](part, direction, s - 1),
            (below, above)[direction],
        )

    def q_sib(part, u):
        ref = q_ref(part, u, c)
        return remote(ref, ref, S["qs_s"](part, u), S["qs_r"](part, u), sib)

    def q_sib_in(part, u):
        ref = q_ref(part, u, 1 - c)
        return remote(ref, ref, S["qs_s"](part, u), S["qs_r"](part, u), sib)

    def line_valid(s, direction):
        return z - s >= 0 if direction == 0 else z + s <= nz - 1

    def line_sends(s, direction):
        return line_valid(s, direction) & (has_above if direction == 0 else has_below)

    def q_tick(s):
        if s == 0:
            for copy in qown:
                copy.wait()
        for direction in range(2):
            if s > 0:

                @pl.when(line_valid(s, direction))
                def _():
                    for part in range(2):
                        q_arrive(part, s, direction).wait_recv()

            if s < nz - 1:

                @pl.when(line_sends(s, direction))
                def _():
                    for part in range(2):
                        q_line(part, s, direction).start()

            if s > 0:

                @pl.when(line_valid(s, direction))
                def _():
                    for part in range(2):
                        q_sib(part, z - s if direction == 0 else z + s).start()

        if s == 0:
            for part in range(2):
                q_sib(part, z).start()

    def q_finish():
        for s in range(nz - 1):
            for direction in range(2):

                @pl.when(line_sends(s, direction))
                def _():
                    for part in range(2):
                        q_line(part, s, direction).wait_send()

        for u in range(nz):
            for part in range(2):
                q_sib_in(part, u).wait_recv()

    def ag_line(i, s, direction):
        unit = w.at[i, z - s if direction == 0 else z + s]
        return remote(
            unit, unit, S["ag_s"](i, direction, s), S["ag_r"](i, direction, s), (above, below)[direction]
        )

    def ag_arrive(i, s, direction):
        unit = w.at[i, z - s if direction == 0 else z + s]
        return remote(
            unit,
            unit,
            S["ag_s"](i, direction, s - 1),
            S["ag_r"](i, direction, s - 1),
            (below, above)[direction],
        )

    def ag_tick(i, s):
        if s == 0:
            for kind in range(3):
                own_copy(i, kind).wait()
                sib_wait(i, kind).wait_recv()
        for direction in range(2):
            if s > 0:

                @pl.when(line_valid(s, direction))
                def _():
                    ag_arrive(i, s, direction).wait_recv()

            if s < nz - 1:

                @pl.when(line_sends(s, direction))
                def _():
                    ag_line(i, s, direction).start()

    def ag_finish(i):
        for s in range(nz - 1):
            for direction in range(2):

                @pl.when(line_sends(s, direction))
                def _():
                    ag_line(i, s, direction).wait_send()

    def rs_owner(tau, direction):
        return nz - 1 + z - tau if direction == 0 else tau - (nz - 1 - z)

    def rs_valid(tau, direction):
        return z <= tau if direction == 0 else tau >= nz - 1 - z

    def rs_line(i, tau, direction):
        return remote(
            w.at[i, rs_owner(tau, direction)],
            (ru, rd)[direction].at[tau],
            S["rs_s"](direction, tau),
            S["rs_r"](direction, tau),
            (above, below)[direction],
        )

    def slot_credit(direction, tau):
        return credit.at[direction * nz + tau]

    def take_slot(direction, tau):
        pl.semaphore_wait(slot_credit(direction, tau), 1)

    def at_edge(direction):
        return z == (nz - 2, 1)[direction]

    def rs_send(i, tau, direction):
        if i > 0:
            rs_line(i - 1, tau, direction).wait_send()
            take_slot(direction, tau)
        rs_line(i, tau, direction).start()

    def rs_edge(i):
        for direction in range(2):

            @pl.when(at_edge(direction))
            def _():
                rs_send(i, nz - 2, direction)

    def rs_tick(i, tau, which):
        for direction in range(2):
            got = (ru, rd)[direction]
            back = (below, above)[direction]
            here = rs_valid(tau, direction)
            if which == "mid":
                here = here & has_below & has_above
            if which == "end":
                here = here & ~(has_below & has_above)
            if tau > 0:

                @pl.when(here & (has_below, has_above)[direction])
                def _():
                    owner = rs_owner(tau, direction)
                    remote(
                        w.at[i, owner],
                        got.at[tau - 1],
                        S["rs_s"](direction, tau - 1),
                        S["rs_r"](direction, tau - 1),
                        back,
                    ).wait_recv()

                    def add(k, carry):
                        core, kind = k // 3, k % 3
                        a = w[i, owner, core, kind].astype(f32)
                        b = got[tau - 1, core, kind].astype(f32)
                        w[i, owner, core, kind] = (a + b).astype(bf16)
                        return carry

                    lax.fori_loop(0, 6, add, 0)
                    pl.semaphore_signal(
                        slot_credit(direction, tau - 1), inc=1, device_id=back, device_id_type=MESH
                    )

            if tau < nz - 1:

                sends = here
                if which == "inner" and tau == nz - 2:
                    sends = here & ~at_edge(direction)

                @pl.when(sends)
                def _():
                    rs_send(i, tau, direction)

    def rs_end():
        for tau in range(nz - 1):
            for direction in range(2):

                @pl.when(rs_valid(tau, direction))
                def _():
                    rs_line(nch - 1, tau, direction).wait_send()

    def fin_own(i):
        return pltpu.make_async_copy(w.at[i, z, c], g_ffn.at[i, c], S["put"](i))

    def fin_sib(i):
        return remote(w.at[i, z, 1 - c], g_ffn.at[i, c], S["fin_s"](i), S["fin_r"](i), sib)

    def fin_in(i):
        return remote(w.at[i, z, c], g_ffn.at[i, 1 - c], S["fin_s"](i), S["fin_r"](i), sib)

    def fin_start(i):
        fin_own(i).start()
        fin_sib(i).start()

    def fin_finish(i):
        fin_own(i).wait()
        fin_sib(i).wait_send()

    def free_first():
        pl.semaphore_signal(credit.at[2 * nz], inc=1, device_id=sib, device_id_type=MESH)

    plan = sums_plan(nz, nch)

    def sums(place):
        for step_ in plan.get(place, ()):
            if step_[0] == "edge":
                rs_edge(step_[1])
            else:
                rs_tick(*step_)

    tile = min(256, tokens)

    def rows_pass(i, core):
        first = i == 0

        def rows_step(m, carry):
            local_rows = pl.ds(mult(m, tile), tile)
            rows = pl.ds(pl.multiple_of(core * tokens + m * tile, tile), tile)
            xm = x[rows, :]
            gate = dot(xm, w[i, :, :, 0].reshape(width, hc))
            up = dot(xm, w[i, :, :, 1].reshape(width, hc))
            dh = jnp.zeros((tile, hc), f32)
            for k in range(dps):
                dh = dh + dot_nt(ct[rows, k * hc : (k + 1) * hc], w[i, k // 2, k % 2, 2])
            sig = jax.nn.sigmoid(gate)
            act = gate * sig
            hidden = (act * up).astype(bf16)
            d_up = (dh * act).astype(bf16)
            d_gate = (dh * up * sig * (1.0 + gate * (1.0 - sig))).astype(bf16)
            ht[:, rows] = hidden.T
            dgt[:, rows] = d_gate.T
            dut[:, rows] = d_up.T
            mine_too = core is c
            for k in range(dps):
                cols = slice(k * hc, (k + 1) * hc)
                fwd = dot(hidden, w[i, k // 2, k % 2, 2])
                back = dot_nt(d_gate, w[i, k // 2, k % 2, 0]) + dot_nt(d_up, w[i, k // 2, k % 2, 1])
                if not first:
                    fwd = accp[rows, cols].astype(f32) + fwd
                    back = (accb if mine_too else acco)[local_rows, cols].astype(f32) + back
                accp[rows, cols] = fwd.astype(bf16)
                if mine_too:
                    accb[local_rows, cols] = back
                else:
                    acco[local_rows, cols] = back.astype(bf16)
            return carry

        lax.fori_loop(0, tokens // tile, rows_step, 0)

    def cols_pass(i):
        def cols_step(k, carry):
            cols = pl.ds(mult(k, hc), hc)
            xs = x[:, cols]
            chip, core = k // 2, k % 2
            w[i, chip, core, 0] = dot(dgt[...], xs).astype(bf16)
            w[i, chip, core, 1] = dot(dut[...], xs).astype(bf16)
            w[i, chip, core, 2] = dot(ht[...], ct[:, cols]).astype(bf16)
            return carry

        lax.fori_loop(0, dps, cols_step, 0)

    lane = lax.broadcasted_iota(jnp.int32, (1, LANES), 1)
    low_head = lane < HD
    low_half = lane % HD < HD // 2

    def turn(u, cos, sin):
        swapped = jnp.where(low_half, pltpu.roll(u, LANES - HD // 2, 1), pltpu.roll(u, HD // 2, 1))
        return u * cos + swapped * sin

    def turn_back(g, cos, sin):
        v = g * sin
        swapped = jnp.where(low_half, pltpu.roll(v, LANES - HD // 2, 1), pltpu.roll(v, HD // 2, 1))
        return g * cos + swapped

    def tables(rows, with_values):
        cos, sin = cosine[rows, :], sine[rows, :]
        if with_values:
            cos, sin = jnp.where(low_head, cos, 1.0), jnp.where(low_head, sin, 0.0)
        return cos, sin

    step = 32

    def norm_rows(src, dst, base, grad_sum):
        def body(m, carry):
            rows = pl.ds(mult(m, step), step)
            v = src[rows, :].astype(f32)
            scale = lax.rsqrt(jnp.mean(v * v, axis=-1, keepdims=True) + epsilon)
            v = v * scale
            dst[pl.ds(pl.multiple_of(base + m * step, step), step), :] = (v * gv[0:1, :]).astype(bf16)
            if grad_sum is None:
                return carry
            up = grad_sum(rows)
            return carry + jnp.sum(up * v, axis=0, keepdims=True)

        start = 0 if grad_sum is None else jnp.zeros((1, width), f32)
        return lax.fori_loop(0, tokens // step, body, start)

    chunks = aw_cols(hc) // LANES
    per_block = hc // LANES
    atile = min(256, tokens)

    def joined():
        def body(m, carry):
            rows = pl.ds(mult(m, atile), atile)
            src = pl.ds(pl.multiple_of(c * tokens + m * atile, atile), atile)
            xm = x[src, :]
            for j in range(3):
                block = dot(xm, aw[:, :, j].reshape(width, hc))
                for q in range(per_block):
                    index = j * per_block + q
                    cos, sin = tables(rows, index % 3 == 2)
                    u = block[:, q * LANES : (q + 1) * LANES]
                    qkvb[rows, index * LANES : (index + 1) * LANES] = turn(u, cos, sin).astype(bf16)
            return carry

        lax.fori_loop(0, tokens // atile, body, 0)

    row_id = lax.broadcasted_iota(jnp.int32, (SEQ, SEQ), 0)
    col_id = lax.broadcasted_iota(jnp.int32, (SEQ, SEQ), 1)
    keep = row_id >= col_id
    inv_root = 1.0 / math.sqrt(HD)

    def doubled(rows, base):
        kv = qkvb[rows, pl.ds(pl.multiple_of(base + GROUPS * HD, LANES), LANES)].astype(f32)
        other = pltpu.roll(kv, HD, 1)
        kk = jnp.where(low_head, kv, other).astype(bf16)
        vv = jnp.where(low_head, other, kv).astype(bf16)
        return kk, vv

    def softmax(qm, kk):
        scores = jnp.where(keep, dot_nt(qm, kk) * inv_root, masked_score)
        e = jnp.exp(scores - jnp.max(scores, axis=-1, keepdims=True))
        return e * (1.0 / jnp.sum(e, axis=-1, keepdims=True))

    def place(n):
        s, h = n // kv_local, n % kv_local
        rows = pl.ds(mult(s, SEQ), SEQ)
        return rows, h * head_cols, h * GROUPS * HD

    def heads_forward():
        def body(n, carry):
            rows, base, qbase = place(n)
            kk, vv = doubled(rows, base)
            for pair in range(GROUPS // 2):
                qp = qkvb[rows, pl.ds(pl.multiple_of(base + pair * LANES, LANES), LANES)]
                halves = []
                for half in range(2):
                    mask = low_head if half == 0 else ~low_head
                    qm = jnp.where(mask, qp.astype(f32), 0.0).astype(bf16)
                    halves.append(dot(softmax(qm, kk).astype(bf16), vv))
                att[rows, pl.ds(pl.multiple_of(qbase + pair * LANES, LANES), LANES)] = jnp.where(
                    low_head, halves[0], halves[1]
                ).astype(bf16)
            return carry

        lax.fori_loop(0, seqs * kv_local, body, 0)

    def heads_backward():
        def body(n, carry):
            rows, base, qbase = place(n)
            kk, vv = doubled(rows, base)
            dkk = jnp.zeros((SEQ, LANES), f32)
            dvv = jnp.zeros((SEQ, LANES), f32)
            cos, sin = tables(rows, False)
            for pair in range(GROUPS // 2):
                cols = pl.ds(pl.multiple_of(base + pair * LANES, LANES), LANES)
                acols = pl.ds(pl.multiple_of(qbase + pair * LANES, LANES), LANES)
                qp = qkvb[rows, cols].astype(f32)
                dp = datt[rows, acols].astype(f32)
                prod = dp * att[rows, acols].astype(f32)
                halves = []
                for half in range(2):
                    mask = low_head if half == 0 else ~low_head
                    qm = jnp.where(mask, qp, 0.0).astype(bf16)
                    dm = jnp.where(mask, dp, 0.0).astype(bf16)
                    probs = softmax(qm, kk)
                    delta = jnp.sum(jnp.where(mask, prod, 0.0), axis=-1, keepdims=True)
                    ds = (probs * (dot_nt(dm, vv) - delta) * inv_root).astype(bf16)
                    halves.append(dot(ds, kk))
                    dkk = dkk + dot(ds.T, qm)
                    dvv = dvv + dot(probs.astype(bf16).T, dm)
                dq = jnp.where(low_head, halves[0], halves[1])
                qkvb[rows, cols] = turn_back(dq, cos, sin).astype(bf16)
            dkk = dkk + pltpu.roll(dkk, HD, 1)
            dvv = dvv + pltpu.roll(dvv, HD, 1)
            cos, sin = tables(rows, True)
            qkvb[rows, pl.ds(pl.multiple_of(base + GROUPS * HD, LANES), LANES)] = turn_back(
                jnp.where(low_head, dkk, dvv), cos, sin
            ).astype(bf16)
            return carry

        lax.fori_loop(0, seqs * kv_local, body, 0)

    def out_weight(k):
        return aw[k // 2, k % 2, 3:5].reshape(2 * hc, hc)

    def attention_partial():
        def body(k, carry):
            cols = pl.ds(mult(k, hc), hc)
            rsb[:, cols] = dot(att[...], out_weight(k)).astype(bf16)
            return carry

        lax.fori_loop(0, dps, body, 0)

    square = nt == 4
    xp, yp, dg = t ^ 1, t ^ 2, t ^ 3
    half = ts // 2

    def part_rows(base, index, upper):
        return pl.ds(pl.multiple_of(base + index * ts + upper * half, half), half)

    def slice_rows(base, index):
        return pl.ds(pl.multiple_of(base + index * ts, ts), ts)

    def reduce_copy(src, base, land, which, n):
        rows = (
            part_rows(base, xp, 0),
            part_rows(base, dg, 0),
            part_rows(base, yp, 1),
            part_rows(base, dg, 1),
            part_rows(base, yp, 0),
            part_rows(base, xp, 1),
        )[n]
        to = (xp, xp, yp, yp, yp, xp)[n]
        return remote(
            src.at[rows],
            land.at[pl.ds(n * half, half)],
            S["ps_s"](which, n),
            S["ps_r"](which, n),
            (d, to),
        )

    def reduce_direct(src, base, land, which, k, arriving):
        frm = source(k)
        return remote(
            src.at[slice_rows(base, peer(k))],
            land.at[slot(frm if arriving else t)],
            S["ps_s"](which, k),
            S["ps_r"](which, k),
            (d, frm if arriving else peer(k)),
        )

    def reduce_start(src, base, land, which):
        if square:
            for n in range(4):
                reduce_copy(src, base, land, which, n).start()
        else:
            for k in range(nt - 1):
                reduce_direct(src, base, land, which, k, False).start()

    def reduce_mid(src, base, land, which):
        if not square:
            return
        for n, index, upper in ((1, yp, 0), (3, xp, 1)):
            reduce_copy(src, base, land, which, n).wait_recv()
            rows = part_rows(base, index, upper)
            both = src[rows, :].astype(f32) + land[n * half : (n + 1) * half, :].astype(f32)
            src[rows, :] = both.astype(bf16)
            reduce_copy(src, base, land, which, 4 if n == 1 else 5).start()

    def reduce_wait(src, base, land, which):
        if square:
            for n in (0, 2, 4, 5):
                reduce_copy(src, base, land, which, n).wait_recv()
        else:
            for k in range(nt - 1):
                reduce_direct(src, base, land, which, k, True).wait_recv()

    def reduce_end(src, base, land, which):
        if square:
            for n in range(6):
                reduce_copy(src, base, land, which, n).wait_send()
        else:
            for k in range(nt - 1):
                reduce_direct(src, base, land, which, k, False).wait_send()

    def summed(src, base, land, m):
        total = src[pl.ds(pl.multiple_of(base + t * ts + m * step, step), step), :].astype(f32)
        if square:
            upper = m // (half // step)
            inner = (m % (half // step)) * step
            for first in (2 * upper * half, (4 + upper) * half):
                total = total + land[pl.ds(pl.multiple_of(first + inner, step), step), :].astype(f32)
        else:
            for k in range(nt - 1):
                rows = pl.ds(pl.multiple_of(source(k) * ts + m * step, step), step)
                total = total + land[rows, :].astype(f32)
        return total

    def spread_copy(src, src_base, dst, dst_base, which, n):
        index, upper, to = (
            (t, 0, xp),
            (t, 1, xp),
            (t, 1, yp),
            (t, 0, yp),
            (xp, 0, yp),
            (yp, 1, xp),
        )[n]
        from_rows = part_rows(src_base, t, upper) if n < 4 else part_rows(dst_base, index, upper)
        return remote(
            (src if n < 4 else dst).at[from_rows],
            dst.at[part_rows(dst_base, index, upper)],
            S["ga_s"](which, n),
            S["ga_r"](which, n),
            (d, to),
        )

    def spread_arrive(src, src_base, dst, dst_base, which, n):
        index, upper, frm = (
            (xp, 0, xp),
            (xp, 1, xp),
            (yp, 1, yp),
            (yp, 0, yp),
            (dg, 0, yp),
            (dg, 1, xp),
        )[n]
        return remote(
            src.at[part_rows(src_base, t, upper)],
            dst.at[part_rows(dst_base, index, upper)],
            S["ga_s"](which, n),
            S["ga_r"](which, n),
            (d, frm),
        )

    def spread_direct(src, src_base, dst, dst_base, which, k, arriving):
        frm = source(k)
        return remote(
            src.at[slice_rows(src_base, t)],
            dst.at[slice_rows(dst_base, frm if arriving else t)],
            S["ga_s"](which, k),
            S["ga_r"](which, k),
            (d, frm if arriving else peer(k)),
        )

    def spread_start(*args):
        if square:
            for n in range(4):
                spread_copy(*args, n).start()
        else:
            for k in range(nt - 1):
                spread_direct(*args, k, False).start()

    def spread_mid(*args):
        if square:
            for n, onward in ((0, 4), (2, 5)):
                spread_arrive(*args, n).wait_recv()
                spread_copy(*args, onward).start()

    def spread_wait(*args):
        if square:
            for n in (1, 3, 4, 5):
                spread_arrive(*args, n).wait_recv()
        else:
            for k in range(nt - 1):
                spread_direct(*args, k, True).wait_recv()

    def spread_end(*args):
        if square:
            for n in range(6):
                spread_copy(*args, n).wait_send()
        else:
            for k in range(nt - 1):
                spread_direct(*args, k, False).wait_send()

    q_tick(0)
    for i in range(nch):
        for kind in range(3):
            own_copy(i, kind).start()
            sib_copy(i, kind).start()
    cot_own = pltpu.make_async_copy(cot, ct.at[core_rows(c)], S["cot"](0))
    cot_sib = remote(cot, ct.at[core_rows(c)], S["cot"](1), S["cot"](2), sib)
    cot_in = remote(cot, ct.at[core_rows(1 - c)], S["cot"](1), S["cot"](2), sib)
    cot_own.start()
    cot_sib.start()
    quarter = HD // 2
    exponent = lax.broadcasted_iota(jnp.int32, (quarter, 1), 0).astype(f32) * (2.0 / HD)
    angles = jnp.exp(exponent * -math.log(rope_base)) * pos[...].astype(f32)
    cos_rows, sin_rows = jnp.cos(angles), jnp.sin(angles)
    cosine[...] = jnp.concatenate([cos_rows] * (LANES // quarter), axis=0).T
    sine[...] = jnp.concatenate([-sin_rows, sin_rows] * (LANES // HD), axis=0).T
    for s in range(1, nz):
        if s == nz - 1:
            ag_tick(0, 0)
        q_tick(s)
    if nz == 1:
        ag_tick(0, 0)
    q_finish()
    for k in range(dps):
        gv[:, k * hc : (k + 1) * hc] = gw[k // 2, k % 2].astype(f32)
    tok_all.wait()
    norm_rows(p2, x, c * tokens, None)
    joined()
    heads_forward()
    if nz > 1:
        ag_tick(0, 1)
    attention_partial()
    first_sum = (rsb, 0, p1, 0)
    reduce_start(*first_sum)
    if nz > 2:
        ag_tick(0, 2)
    reduce_mid(*first_sum)
    if nz > 3:
        ag_tick(1, 0)
    reduce_wait(*first_sum)
    mine = half_rows(c, t)

    def second_norm(m, carry):
        rows = pl.ds(mult(m, step), step)
        trow = pl.ds(pl.multiple_of(t * ts + m * step, step), step)
        total = p2[trow, :].astype(f32) + summed(rsb, 0, p1, m)
        resid[rows, :] = total
        scale = lax.rsqrt(jnp.mean(total * total, axis=-1, keepdims=True) + epsilon)
        x[pl.ds(pl.multiple_of(c * tokens + t * ts + m * step, step), step), :] = (
            total * scale * gv[1:2, :]
        ).astype(bf16)
        return carry

    lax.fori_loop(0, ts // step, second_norm, 0)
    x_spread = (x, c * tokens, x, c * tokens, 3)

    def xs_index(k):
        if square:
            return (t, xp, yp, dg)[k]
        return lax.rem(t - k + nt, nt)

    def xs_copy(k):
        rows = half_rows(c, xs_index(k))
        return remote(x.at[rows], x.at[rows], S["xs_s"](k), S["xs_r"](k), sib)

    def xs_in(k):
        rows = half_rows(1 - c, xs_index(k))
        return remote(x.at[rows], x.at[rows], S["xs_s"](k), S["xs_r"](k), sib)

    spread_start(*x_spread)
    xs_copy(0).start()
    spread_mid(*x_spread)
    if square:
        spread_arrive(*x_spread, 1).wait_recv()
        xs_copy(1).start()
        spread_arrive(*x_spread, 3).wait_recv()
        xs_copy(2).start()
    for s in range(3, nz):
        ag_tick(0, s)
    ag_finish(0)
    if nz <= 3:
        ag_tick(1, 0)
    if square:
        for n in (4, 5):
            spread_arrive(*x_spread, n).wait_recv()
        xs_copy(3).start()
    else:
        for k in range(nt - 1):
            spread_direct(*x_spread, k, True).wait_recv()
            xs_copy(k + 1).start()
    cot_own.wait()
    cot_in.wait_recv()
    for k in range(nt):
        xs_in(k).wait_recv()

    last = nch - 1
    other = (1 - c) * tokens
    for i in range(last):
        if i > 0:
            ag_tick(i + 1, 0)
        sums(4 * i - 1)
        rows_pass(i, 1 - c)
        rows_pass(i, c)
        cols_pass(i)
        sums(4 * i)
        for s in range(1, nz):
            ag_tick(i + 1, s)
            if s < 3:
                sums(4 * i + s)
        ag_finish(i + 1)

    def sib_b(k):
        return remote(acco.at[slot(k)], sbr_b.at[slot(k)], S["sb_s"](0, k), S["sb_r"](0, k), sib)

    def sib_p(k):
        return remote(
            accp.at[half_rows(1 - c, k)], sbr_p.at[slot(k)], S["sb_s"](1, k), S["sb_r"](1, k), sib
        )

    for u in range(nz):
        for part in range(2):
            q_sib(part, u).wait_send()
    spread_end(*x_spread)
    reduce_end(*first_sum)
    for k in range(nt):
        xs_copy(k).wait_send()
    sums(4 * last - 1)
    rows_pass(last, 1 - c)
    for k in range(nt):
        sib_b(k).start()
    rows_pass(last, c)
    for k in range(nt):
        sib_b(k).wait_recv()

    def pair_b(m, carry):
        rows = pl.ds(mult(m, step), step)
        rsb[rows, :] = (accb[rows, :] + sbr_b[rows, :].astype(f32)).astype(bf16)
        return carry

    lax.fori_loop(0, tokens // step, pair_b, 0)
    back_sum = (rsb, 0, p2, 1)
    reduce_start(*back_sum)
    cols_pass(last)
    sums(4 * last)
    for k in range(nt):
        sib_p(k).start()
    reduce_mid(*back_sum)
    sums(4 * last + 1)
    reduce_wait(*back_sum)

    def second_back(m, carry):
        rows = pl.ds(mult(m, step), step)
        place_ = pl.ds(pl.multiple_of(c * tokens + t * ts + m * step, step), step)
        up = summed(rsb, 0, p2, m)
        v = resid[rows, :]
        scale = lax.rsqrt(jnp.mean(v * v, axis=-1, keepdims=True) + epsilon)
        weighted = up * gv[1:2, :]
        inner = jnp.mean(weighted * v, axis=-1, keepdims=True)
        grad = ct[place_, :].astype(f32) + scale * weighted - v * (scale * scale * scale) * inner
        accb[rows, :] = grad
        x[place_, :] = grad.astype(bf16)
        return carry + jnp.sum(up * v * scale, axis=0, keepdims=True)

    gain_two = lax.fori_loop(0, ts // step, second_back, jnp.zeros((1, width), f32))
    rg_spread = (x, c * tokens, x, c * tokens, 0)
    spread_start(*rg_spread)
    spread_mid(*rg_spread)
    sums(4 * last + 2)
    reduce_end(*back_sum)
    for k in range(nt):
        sib_p(k).wait_recv()

    def pair_p(m, carry):
        rows = pl.ds(mult(m, step), step)
        here = pl.ds(pl.multiple_of(c * tokens + m * step, step), step)
        rsb[rows, :] = (accp[here, :].astype(f32) + sbr_p[rows, :].astype(f32)).astype(bf16)
        return carry

    lax.fori_loop(0, tokens // step, pair_p, 0)

    spread_wait(*rg_spread)
    out_sum = (rsb, 0, p1, 2)
    reduce_start(*out_sum)
    sums(4 * last + 3)
    fin_start(0)

    def d_attended(m, carry):
        rows = pl.ds(mult(m, atile), atile)
        src = pl.ds(pl.multiple_of(c * tokens + m * atile, atile), atile)
        for j in range(2):
            total = jnp.zeros((atile, hc), f32)
            for k in range(dps):
                total = total + dot_nt(x[src, k * hc : (k + 1) * hc], aw[k // 2, k % 2, 3 + j])
            datt[rows, j * hc : (j + 1) * hc] = total.astype(bf16)
        for j in range(2):
            (ht, dgt)[j][:, rows] = att[rows, j * hc : (j + 1) * hc].T
        return carry

    lax.fori_loop(0, tokens // atile, d_attended, 0)

    def out_grads(k, carry):
        xs = x[core_rows(c), pl.ds(mult(k, hc), hc)]
        for j in range(2):
            aw[k // 2, k % 2, 3 + j] = dot((ht, dgt)[j][:, :tokens], xs).astype(bf16)
        return carry

    lax.fori_loop(0, dps, out_grads, 0)

    def a_src(part, u, core):
        return (aw.at[u, core, 3:5], aw.at[u, core, 0:3], gg.at[u, core])[part]

    def a_sib_ref(part):
        return (w.at[0, :, 1, 0:2], w.at[0, :, 0], gsib)[part]

    def a_sib(part):
        src = (aw.at[:, 1 - c, 3:5], aw.at[:, 1 - c, 0:3], gg.at[:, 1 - c])[part]
        return remote(src, a_sib_ref(part), S["as_s"](part), S["as_r"](part), sib)

    def a_land(part, direction, tau):
        line = (ru, rd)[direction]
        return (line.at[tau, 1, 0:2], line.at[tau, 0], (gru, grd)[direction].at[tau])[part]

    def a_line(part, tau, direction):
        return remote(
            a_src(part, rs_owner(tau, direction), c),
            a_land(part, direction, tau),
            S["ar_s"](part, direction, tau),
            S["ar_r"](part, direction, tau),
            (above, below)[direction],
        )

    def a_add(part, owner, got):
        if part == 2:
            gg[owner, c] = gg[owner, c] + got[...]
            return
        base, count = ((3, 2), (0, 3))[part]
        for j in range(count):
            both = aw[owner, c, base + j].astype(f32) + got[j].astype(f32)
            aw[owner, c, base + j] = both.astype(bf16)

    def a_pair(part):
        a_sib(part).wait_recv()

        def body(u, carry):
            a_add(part, u, (w.at[0, u, 1, 0:2], w.at[0, u, 0], gsib.at[u])[part])
            return carry

        lax.fori_loop(0, nz, body, 0)

    def a_tick(part, tau):
        for direction in range(2):
            if tau > 0:

                @pl.when(rs_valid(tau, direction) & (has_below, has_above)[direction])
                def _():
                    owner = rs_owner(tau, direction)
                    remote(
                        a_src(part, owner, c),
                        a_land(part, direction, tau - 1),
                        S["ar_s"](part, direction, tau - 1),
                        S["ar_r"](part, direction, tau - 1),
                        (below, above)[direction],
                    ).wait_recv()
                    a_add(part, owner, a_land(part, direction, tau - 1))

            if tau < nz - 1:

                @pl.when(rs_valid(tau, direction))
                def _():
                    if part == 0:
                        take_slot(direction, tau)
                    a_line(part, tau, direction).start()

    def a_finish(part):
        a_sib(part).wait_send()
        for tau in range(nz - 1):
            for direction in range(2):

                @pl.when(rs_valid(tau, direction))
                def _():
                    a_line(part, tau, direction).wait_send()

    fin_finish(0)
    free_first()
    pl.semaphore_wait(credit.at[2 * nz], 1)
    a_sib(0).start()
    tok_again = pltpu.make_async_copy(tok, sbr_b, S["tok"](1))
    tok_again.start()
    a_pair(0)
    sums(4 * last + 4)
    heads_backward()

    def attn_back(k, carry):
        total = jnp.zeros((tokens, hc), f32)
        for j in range(3):
            total = total + dot_nt(qkvb[:, j * hc : (j + 1) * hc], aw[k // 2, k % 2, j])
        x[pl.ds(mult(1 - c, tokens), tokens), pl.ds(mult(k, hc), hc)] = total.astype(bf16)
        return carry

    lax.fori_loop(0, dps, attn_back, 0)
    tail_sum = (x, other, p2, 3)
    reduce_start(*tail_sum)
    reduce_mid(*out_sum)
    sums(4 * last + 5)
    tok_again.wait()

    def own_back(rows):
        return x[pl.ds(pl.multiple_of(other + rows.start, step), step), :].astype(f32)

    gain_one = norm_rows(sbr_b, sbr_p, 0, own_back)
    for k in range(dps):
        cols = slice(k * hc, (k + 1) * hc)
        gg[k // 2, k % 2] = jnp.concatenate(
            [gain_one[:, cols], gain_two[:, cols], jnp.zeros((6, hc), f32)], axis=0
        )
    a_sib(2).start()
    for m in range(tokens // atile):
        for j in range(3):
            (ht, dgt, dut)[j][:, tokens + m * atile : tokens + (m + 1) * atile] = qkvb[
                m * atile : (m + 1) * atile, j * hc : (j + 1) * hc
            ].T

    def qkv_grads(k, carry):
        xs = sbr_p[:, pl.ds(mult(k, hc), hc)]
        for j in range(3):
            aw[k // 2, k % 2, j] = dot((ht, dgt, dut)[j][:, tokens:], xs).astype(bf16)
        return carry

    lax.fori_loop(0, dps, qkv_grads, 0)
    a_sib(1).start()
    sums(4 * last + 6)
    a_tick(0, 0)
    a_pair(1)
    a_pair(2)
    a_tick(1, 0)
    a_tick(2, 0)
    fin_start(1)

    reduce_mid(*tail_sum)
    reduce_wait(*out_sum)

    def finish_output(m, carry):
        rows = pl.ds(mult(m, step), step)
        where = pl.ds(pl.multiple_of(c * tokens + t * ts + m * step, step), step)
        accp[where, :] = (resid[rows, :] + summed(rsb, 0, p1, m)).astype(bf16)
        return carry

    lax.fori_loop(0, ts // step, finish_output, 0)
    out_spread = (accp, c * tokens, out, 0, 1)
    spread_start(*out_spread)
    put_out = pltpu.make_async_copy(accp.at[mine], out.at[slot(t)], S["loc"](0))
    put_out.start()
    sums(4 * last + 7)

    reduce_wait(*tail_sum)
    for k in range(nt):
        sib_p(k).wait_send()
    theirs = half_rows(1 - c, t)

    def finish_tokens(m, carry):
        rows = pl.ds(mult(m, step), step)
        up = summed(x, other, p2, m)
        v = sbr_b[pl.ds(pl.multiple_of(t * ts + m * step, step), step), :].astype(f32)
        scale = lax.rsqrt(jnp.mean(v * v, axis=-1, keepdims=True) + epsilon)
        weighted = up * gv[0:1, :]
        inner = jnp.mean(weighted * v, axis=-1, keepdims=True)
        grad = accb[rows, :] + scale * weighted - v * (scale * scale * scale) * inner
        accp[pl.ds(pl.multiple_of(other + t * ts + m * step, step), step), :] = grad.astype(bf16)
        return carry

    lax.fori_loop(0, ts // step, finish_tokens, 0)
    tok_spread = (accp, other, dtok, 0, 2)
    spread_start(*tok_spread)
    put_tok = pltpu.make_async_copy(accp.at[theirs], dtok.at[slot(t)], S["loc"](1))
    put_tok.start()
    fin_finish(1)
    spread_mid(*out_spread)
    spread_mid(*tok_spread)
    sums(4 * last + 8)
    for part in range(3):
        a_tick(part, 1)
    fin_start(2)
    fin_finish(2)
    sums(4 * last + 9)
    for s in range(2, nz):
        for part in range(3):
            a_tick(part, s)
        if s == nz - 2:
            fin_start(3)
    fin_finish(3)

    def gain_copy(k):
        return remote(gg.at[z, c], gt.at[t], S["gg_s"](k), S["gg_r"](k), (d, peer(k)))

    def gain_in(k):
        return remote(gg.at[z, c], gt.at[source(k)], S["gg_s"](k), S["gg_r"](k), (d, source(k)))

    for k in range(nt - 1):
        gain_copy(k).start()
    gt[t] = gg[z, c]

    put_attn = pltpu.make_async_copy(aw.at[z, c], g_attn, S["loc"](2))
    put_attn.start()
    for k in range(nt - 1):
        gain_in(k).wait_recv()
    total = gt[0]
    for k in range(1, nt):
        total = total + gt[k]
    g_gains[...] = total

    for i in range(nch):
        for kind in range(3):
            sib_copy(i, kind).wait_send()
    cot_sib.wait_send()
    for part in range(3):
        a_finish(part)
    for k in range(nt - 1):
        gain_copy(k).wait_send()
    for k in range(nt):
        sib_b(k).wait_send()
    rs_end()
    reduce_end(*out_sum)
    reduce_end(*tail_sum)
    spread_wait(*out_spread)
    spread_wait(*tok_spread)
    for args in (rg_spread, out_spread, tok_spread):
        spread_end(*args)
    put_out.wait()
    put_tok.wait()
    put_attn.wait()
    for i in range(nch):
        fin_in(i).wait_recv()


def aw_cols(shard):
    return 3 * shard


def layer(tokens, cotangent, weights, positions, gain_a, gain_f, nz, nt):
    count, width = tokens.shape
    hc, hid = weights[2].shape
    nch = hid // (2 * hc)
    ts = count // nt
    sizes = (nz, nt, nch, count, width, hc)
    sems, _ = semaphores(nz, nt, nch)
    V = pltpu.VMEM
    recv = (nz - 1, 2, 3, hc, hc)
    S = jax.ShapeDtypeStruct
    return pl.pallas_call(
        functools.partial(layer_kernel, sizes),
        out_shape=(
            S((count, width), bf16),
            S((count, width), bf16),
            S((5, hc, hc), bf16),
            S((nch, 2, 3, hc, hc), bf16),
            S((8, hc), f32),
        ),
        in_specs=[HBM] * 7 + [VMEM] * 3,
        out_specs=(HBM, HBM, HBM, HBM, VMEM),
        scratch_shapes=[
            V((nch, nz, 2, 3, hc, hc), bf16),
            V(recv, bf16),
            V(recv, bf16),
            V((2 * count, width), bf16),
            V((2 * count, width), bf16),
            V((2 * count, width), bf16),
            V((count, width), f32),
            V((count, width), bf16),
            V((hc, 2 * count), bf16),
            V((hc, 2 * count), bf16),
            V((hc, 2 * count), bf16),
            V((ts, width), f32),
            V((count, width), bf16),
            V((count, width), bf16),
            V((count, width), bf16),
            V((count, width), bf16),
            V((count, width), bf16),
            V((nz, 2, 5, hc, hc), bf16),
            V((count, 3 * hc), bf16),
            V((count, 2 * hc), bf16),
            V((count, 2 * hc), bf16),
            V((nz, 2, 16, hc), bf16),
            V((16, width), f32),
            V((nz, 2, 8, hc), f32),
            V((nz, 8, hc), f32),
            V((nz - 1, 8, hc), f32),
            V((nz - 1, 8, hc), f32),
            V((nt, 8, hc), f32),
            V((count, LANES), f32),
            V((count, LANES), f32),
            pltpu.SemaphoreType.DMA((sems.count,)),
            pltpu.SemaphoreType.REGULAR((2 * nz + 1,)),
        ],
        compiler_params=pltpu.CompilerParams(
            collective_id=0, has_side_effects=True, vmem_limit_bytes=63 * 2**20
        ),
        name="layer",
    )(tokens, cotangent, *weights, positions, gain_a, gain_f)


def results_kernel(
    out, dtok, attn, ffn, gains, *refs
):
    results, (rows_a, rows_b, attn_in, ffn_in, qkv, proj, gate, up, down, sem) = refs[:9], refs[9:]
    nch, _, _, hc, _ = ffn.shape
    pieces = nch * 2
    used = iter(range(sem.shape[0]))

    def copy(src, dst):
        return pltpu.make_async_copy(src, dst, sem.at[next(used)])

    loads = [copy(ffn.at[n // 2, n % 2], ffn_in.at[n]) for n in range(pieces)]
    load_attn = copy(attn, attn_in)
    parts = 2
    moves = []
    for src, held, dst in ((out, rows_a, results[0]), (dtok, rows_b, results[1])):
        count = src.shape[0] // parts
        for k in range(parts):
            at = pl.ds(k * count, count)
            moves.append((copy(src.at[at], held.at[at]), copy(held.at[at], dst.at[at])))
    for load in loads:
        load.start()
    load_attn.start()
    for load, _ in moves:
        load.start()
    stores = []

    def store(src, dst):
        stores.append(copy(src, dst))
        stores[-1].start()

    for n in range(pieces):
        loads[n].wait()
        at = pl.ds(n * hc, hc)
        gate[:, at] = ffn_in[n, 0].T.astype(f32)
        store(gate.at[:, at], results[4].at[:, at])
        up[:, at] = ffn_in[n, 1].T.astype(f32)
        store(up.at[:, at], results[5].at[:, at])
        down[at, :] = ffn_in[n, 2].astype(f32)
        store(down.at[at], results[6].at[at])
        if n % 2 == 1 and moves:
            load, onward = moves.pop(0)
            load.wait()
            onward.start()
            stores.append(onward)
    for load, onward in moves:
        load.wait()
        onward.start()
        stores.append(onward)
    load_attn.wait()
    for j in range(3):
        qkv[:, j * hc : (j + 1) * hc] = attn_in[j].T.astype(f32)
    store(qkv, results[2])
    for j in range(2):
        proj[j * hc : (j + 1) * hc, :] = attn_in[3 + j].astype(f32)
    store(proj, results[3])
    for n in range(2):
        results[7 + n][...] = gains[n, :]
    for one in stores:
        one.wait()


def finished(out, dtok, attn, ffn, gains):
    count, width = out.shape
    nch, _, _, hc, _ = ffn.shape
    hid = nch * 2 * hc
    S = jax.ShapeDtypeStruct
    V = pltpu.VMEM
    grads = [(hc, 3 * hc), (2 * hc, hc), (hc, hid), (hc, hid), (hid, hc)]
    return pl.pallas_call(
        results_kernel,
        out_shape=[S((count, width), bf16)] * 2 + [S(g, f32) for g in grads] + [S((hc,), f32)] * 2,
        in_specs=[HBM] * 4 + [VMEM],
        out_specs=[HBM] * 7 + [VMEM] * 2,
        scratch_shapes=[
            V((count, width), bf16),
            V((count, width), bf16),
            V((5, hc, hc), bf16),
            V((nch * 2, 3, hc, hc), bf16),
        ]
        + [V(g, f32) for g in grads]
        + [pltpu.SemaphoreType.DMA((nch * 2 * 4 + 16,))],
        compiler_params=pltpu.CompilerParams(vmem_limit_bytes=60 * 2**20),
        name="results",
    )(out, dtok, attn, ffn, gains)


def local(tokens, positions, w_qkv, w_out, w_gate, w_up, w_down, gain_attn, gain_ffn, cotangent):
    nz = lax.axis_size("dp") // 2
    nt = lax.axis_size("tensor")
    results = layer(
        tokens,
        cotangent,
        (w_qkv, w_out, w_gate, w_up, w_down),
        positions.reshape(1, -1),
        gain_attn,
        gain_ffn,
        nz,
        nt,
    )
    return tuple(finished(*results))


def solution(mesh):
    return jax.shard_map(
        local,
        mesh=mesh,
        in_specs=(
            P("dp", None),
            P("dp"),
            P("dp", "tensor"),
            P("tensor", "dp"),
            P("dp", "tensor"),
            P("dp", "tensor"),
            P("tensor", "dp"),
            P("dp"),
            P("dp"),
            P("dp", None),
        ),
        out_specs=(
            P("dp", None),
            P("dp", None),
            P("dp", "tensor"),
            P("tensor", "dp"),
            P("dp", "tensor"),
            P("dp", "tensor"),
            P("tensor", "dp"),
            P("dp"),
            P("dp"),
        ),
        check_vma=False,
    )
```

```python
import functools
import math

import jax
import jax.numpy as jnp
from jax import lax
from jax.experimental import pallas as pl
from jax.experimental.pallas import tpu as pltpu
from jax.sharding import PartitionSpec as P

HEADS = 32
KV_HEADS = 8
HD = 64
SEQ = 256
GROUPS = HEADS // KV_HEADS
LANES = 128

epsilon = 1e-05
rope_base = 500000.0
masked_score = -1e30

MESH = pl.DeviceIdType.MESH
HBM = pl.BlockSpec(memory_space=pl.ANY)
VMEM = pl.BlockSpec(memory_space=pltpu.VMEM)
bf16 = jnp.bfloat16
f32 = jnp.float32
NT_DIMS = (((1,), (1,)), ((), ()))


def remote(src, dst, send, recv, device):
    return pltpu.make_async_remote_copy(
        src_ref=src, dst_ref=dst, send_sem=send, recv_sem=recv, device_id=device, device_id_type=MESH
    )


def mult(value, factor):
    return pl.multiple_of(value * factor, factor)


def dot(a, b):
    return jnp.dot(a, b, preferred_element_type=f32)


def dot_nt(a, b):
    return lax.dot_general(a, b, NT_DIMS, preferred_element_type=f32)


def sums_plan(nz, nch):
    last = nch - 1
    if (nz, nch) != (4, 4):
        plan = {}
        for r in range(last + nz):
            hops = [(i, r - i, "all") for i in range(nch) if 0 <= r - i < nz]
            plan.setdefault(4 * r if r <= last else 4 * last + 3, []).extend(hops)
        return plan
    return {
        1: [(0, 0, "all")],
        2: [(0, 1, "all")],
        5: [(0, 2, "inner")],
        6: [(1, 0, "all")],
        7: [(0, 3, "mid")],
        9: [(1, 1, "all"), (2, 0, "all")],
        10: [("edge", 0), (1, 2, "inner"), (2, 1, "all")],
        13: [(0, 3, "end"), ("edge", 1), (3, 0, "all")],
        14: [(1, 3, "mid"), (2, 2, "inner")],
        16: [(3, 1, "all")],
        17: [(1, 3, "end"), ("edge", 2)],
        18: [(2, 3, "mid"), (3, 2, "inner")],
        19: [(2, 3, "end"), ("edge", 3)],
        21: [(3, 3, "mid"), (3, 3, "end")],
    }


class Sems:
    def __init__(self):
        self.count = 0
        self.ref = None

    def take(self, *dims):
        base = self.count
        self.count += math.prod(dims)

        def at(*index):
            flat = 0
            for size, place in zip(dims, index):
                flat = flat * size + place
            return self.ref.at[base + flat]

        return at


def semaphores(nz, nt, nch):
    s = Sems()
    names = {
        "own": s.take(nch, 3),
        "sib_s": s.take(nch, 3),
        "sib_r": s.take(nch, 3),
        "ag_s": s.take(nch, 2, nz),
        "ag_r": s.take(nch, 2, nz),
        "qown": s.take(5),
        "qa_s": s.take(2, 2, nz),
        "qa_r": s.take(2, 2, nz),
        "qs_s": s.take(2, nz),
        "qs_r": s.take(2, nz),
        "rs_s": s.take(2, nz),
        "rs_r": s.take(2, nz),
        "as_s": s.take(3),
        "as_r": s.take(3),
        "ar_s": s.take(3, 2, nz),
        "ar_r": s.take(3, 2, nz),
        "fin_s": s.take(nch),
        "fin_r": s.take(nch),
        "put": s.take(nch),
        "cot": s.take(3),
        "tok": s.take(3),
        "ps_s": s.take(4, max(nt, 6)),
        "ps_r": s.take(4, max(nt, 6)),
        "xs_s": s.take(nt),
        "xs_r": s.take(nt),
        "sb_s": s.take(2, nt),
        "sb_r": s.take(2, nt),
        "ga_s": s.take(4, max(nt, 6)),
        "ga_r": s.take(4, max(nt, 6)),
        "gg_s": s.take(nt),
        "gg_r": s.take(nt),
        "loc": s.take(5),
    }
    return s, names


def layer_kernel(
    sizes,
    tok,
    cot,
    w_qkv,
    w_out,
    w_gate,
    w_up,
    w_down,
    pos,
    gain_a,
    gain_f,
    out,
    dtok,
    g_attn,
    g_ffn,
    g_gains,
    w,
    ru,
    rd,
    x,
    ct,
    accp,
    accb,
    acco,
    ht,
    dgt,
    dut,
    resid,
    p1,
    p2,
    sbr_b,
    sbr_p,
    rsb,
    aw,
    qkvb,
    att,
    datt,
    gw,
    gv,
    gg,
    gsib,
    gru,
    grd,
    gt,
    cosine,
    sine,
    sem_ref,
    credit,
):
    nz, nt, nch, tokens, width, hc = sizes
    sems, S = semaphores(nz, nt, nch)
    sems.ref = sem_ref
    ts = tokens // nt
    dps = 2 * nz
    d = lax.axis_index("dp")
    t = lax.axis_index("tensor")
    z = d // 2
    c = d % 2
    sib = (2 * z + 1 - c, t)
    above = (d + 2, t)
    below = (d - 2, t)
    has_above = z < nz - 1
    has_below = z > 0
    seqs = tokens // SEQ
    kv_local = aw_cols(hc) // ((GROUPS + 2) * HD)
    head_cols = (GROUPS + 2) * HD

    def peer(k):
        return lax.rem(t + 1 + k, nt)

    def source(k):
        return lax.rem(t - 1 - k + nt, nt)

    barrier = pltpu.get_barrier_semaphore()
    for k in range(nt - 1):
        pl.semaphore_signal(barrier, inc=1, device_id=(d, peer(k)), device_id_type=MESH)
    pl.semaphore_signal(barrier, inc=1, device_id=sib, device_id_type=MESH)

    @pl.when(has_below)
    def _():
        pl.semaphore_signal(barrier, inc=1, device_id=below, device_id_type=MESH)

    @pl.when(has_above)
    def _():
        pl.semaphore_signal(barrier, inc=1, device_id=above, device_id_type=MESH)

    neighbours = jnp.where(has_below, 1, 0) + jnp.where(has_above, 1, 0)
    pl.semaphore_wait(barrier, nt + neighbours)

    def slot(index):
        return pl.ds(mult(index, ts), ts)

    def core_rows(core):
        return pl.ds(mult(core, tokens), tokens)

    def half_rows(core, index):
        return pl.ds(pl.multiple_of(core * tokens + index * ts, ts), ts)

    def ffn_source(i, core, kind):
        cols = pl.ds(mult(2 * i + core, hc), hc)
        return (w_gate.at[:, cols], w_up.at[:, cols], w_down.at[cols])[kind]

    def own_copy(i, kind):
        return pltpu.make_async_copy(ffn_source(i, c, kind), w.at[i, z, c, kind], S["own"](i, kind))

    def sib_copy(i, kind):
        return remote(
            ffn_source(i, 1 - c, kind), w.at[i, z, c, kind], S["sib_s"](i, kind), S["sib_r"](i, kind), sib
        )

    def sib_wait(i, kind):
        return remote(
            ffn_source(i, c, kind), w.at[i, z, 1 - c, kind], S["sib_s"](i, kind), S["sib_r"](i, kind), sib
        )

    qown = [
        pltpu.make_async_copy(w_qkv.at[:, j * hc : (j + 1) * hc], aw.at[z, c, j], S["qown"](j))
        for j in range(3)
    ] + [
        pltpu.make_async_copy(w_out.at[j * hc : (j + 1) * hc], aw.at[z, c, 3 + j], S["qown"](3 + j))
        for j in range(2)
    ]
    for copy in qown:
        copy.start()
    row16 = lax.broadcasted_iota(jnp.int32, (16, hc), 0)
    gw[z, c] = jnp.where(
        row16 == 0,
        gain_a[...].astype(f32).reshape(1, hc),
        jnp.where(row16 == 1, gain_f[...].astype(f32).reshape(1, hc), 0.0),
    ).astype(bf16)
    tok_all = pltpu.make_async_copy(tok, p2, S["tok"](0))
    tok_all.start()

    def q_ref(part, u, core):
        return (aw if part == 0 else gw).at[u, core]

    def q_line(part, s, direction):
        u = z - s if direction == 0 else z + s
        ref = q_ref(part, u, c)
        return remote(
            ref, ref, S["qa_s"](part, direction, s), S["qa_r"](part, direction, s), (above, below)[direction]
        )

    def q_arrive(part, s, direction):
        u = z - s if direction == 0 else z + s
        ref = q_ref(part, u, c)
        return remote(
            ref,
            ref,
            S["qa_s"](part, direction, s - 1),
            S["qa_r"](part, direction, s - 1),
            (below, above)[direction],
        )

    def q_sib(part, u):
        ref = q_ref(part, u, c)
        return remote(ref, ref, S["qs_s"](part, u), S["qs_r"](part, u), sib)

    def q_sib_in(part, u):
        ref = q_ref(part, u, 1 - c)
        return remote(ref, ref, S["qs_s"](part, u), S["qs_r"](part, u), sib)

    def line_valid(s, direction):
        return z - s >= 0 if direction == 0 else z + s <= nz - 1

    def line_sends(s, direction):
        return line_valid(s, direction) & (has_above if direction == 0 else has_below)

    def q_tick(s):
        if s == 0:
            for copy in qown:
                copy.wait()
        for direction in range(2):
            if s > 0:

                @pl.when(line_valid(s, direction))
                def _():
                    for part in range(2):
                        q_arrive(part, s, direction).wait_recv()

            if s < nz - 1:

                @pl.when(line_sends(s, direction))
                def _():
                    for part in range(2):
                        q_line(part, s, direction).start()

            if s > 0:

                @pl.when(line_valid(s, direction))
                def _():
                    for part in range(2):
                        q_sib(part, z - s if direction == 0 else z + s).start()

        if s == 0:
            for part in range(2):
                q_sib(part, z).start()

    def q_finish():
        for s in range(nz - 1):
            for direction in range(2):

                @pl.when(line_sends(s, direction))
                def _():
                    for part in range(2):
                        q_line(part, s, direction).wait_send()

        for u in range(nz):
            for part in range(2):
                q_sib_in(part, u).wait_recv()

    def ag_line(i, s, direction):
        unit = w.at[i, z - s if direction == 0 else z + s]
        return remote(
            unit, unit, S["ag_s"](i, direction, s), S["ag_r"](i, direction, s), (above, below)[direction]
        )

    def ag_arrive(i, s, direction):
        unit = w.at[i, z - s if direction == 0 else z + s]
        return remote(
            unit,
            unit,
            S["ag_s"](i, direction, s - 1),
            S["ag_r"](i, direction, s - 1),
            (below, above)[direction],
        )

    def ag_tick(i, s):
        if s == 0:
            for kind in range(3):
                own_copy(i, kind).wait()
                sib_wait(i, kind).wait_recv()
        for direction in range(2):
            if s > 0:

                @pl.when(line_valid(s, direction))
                def _():
                    ag_arrive(i, s, direction).wait_recv()

            if s < nz - 1:

                @pl.when(line_sends(s, direction))
                def _():
                    ag_line(i, s, direction).start()

    def ag_finish(i):
        for s in range(nz - 1):
            for direction in range(2):

                @pl.when(line_sends(s, direction))
                def _():
                    ag_line(i, s, direction).wait_send()

    def rs_owner(tau, direction):
        return nz - 1 + z - tau if direction == 0 else tau - (nz - 1 - z)

    def rs_valid(tau, direction):
        return z <= tau if direction == 0 else tau >= nz - 1 - z

    def rs_line(i, tau, direction):
        return remote(
            w.at[i, rs_owner(tau, direction)],
            (ru, rd)[direction].at[tau],
            S["rs_s"](direction, tau),
            S["rs_r"](direction, tau),
            (above, below)[direction],
        )

    def slot_credit(direction, tau):
        return credit.at[direction * nz + tau]

    def take_slot(direction, tau):
        pl.semaphore_wait(slot_credit(direction, tau), 1)

    def at_edge(direction):
        return z == (nz - 2, 1)[direction]

    def rs_send(i, tau, direction):
        if i > 0:
            rs_line(i - 1, tau, direction).wait_send()
            take_slot(direction, tau)
        rs_line(i, tau, direction).start()

    def rs_edge(i):
        for direction in range(2):

            @pl.when(at_edge(direction))
            def _():
                rs_send(i, nz - 2, direction)

    def rs_tick(i, tau, which):
        for direction in range(2):
            got = (ru, rd)[direction]
            back = (below, above)[direction]
            here = rs_valid(tau, direction)
            if which == "mid":
                here = here & has_below & has_above
            if which == "end":
                here = here & ~(has_below & has_above)
            if tau > 0:

                @pl.when(here & (has_below, has_above)[direction])
                def _():
                    owner = rs_owner(tau, direction)
                    remote(
                        w.at[i, owner],
                        got.at[tau - 1],
                        S["rs_s"](direction, tau - 1),
                        S["rs_r"](direction, tau - 1),
                        back,
                    ).wait_recv()

                    def add(k, carry):
                        core, kind = k // 3, k % 3
                        a = w[i, owner, core, kind].astype(f32)
                        b = got[tau - 1, core, kind].astype(f32)
                        w[i, owner, core, kind] = (a + b).astype(bf16)
                        return carry

                    lax.fori_loop(0, 6, add, 0)
                    pl.semaphore_signal(
                        slot_credit(direction, tau - 1), inc=1, device_id=back, device_id_type=MESH
                    )

            if tau < nz - 1:

                sends = here
                if which == "inner" and tau == nz - 2:
                    sends = here & ~at_edge(direction)

                @pl.when(sends)
                def _():
                    rs_send(i, tau, direction)

    def rs_end():
        for tau in range(nz - 1):
            for direction in range(2):

                @pl.when(rs_valid(tau, direction))
                def _():
                    rs_line(nch - 1, tau, direction).wait_send()

    def fin_own(i):
        return pltpu.make_async_copy(w.at[i, z, c], g_ffn.at[i, c], S["put"](i))

    def fin_sib(i):
        return remote(w.at[i, z, 1 - c], g_ffn.at[i, c], S["fin_s"](i), S["fin_r"](i), sib)

    def fin_in(i):
        return remote(w.at[i, z, c], g_ffn.at[i, 1 - c], S["fin_s"](i), S["fin_r"](i), sib)

    def fin_start(i):
        fin_own(i).start()
        fin_sib(i).start()

    def fin_finish(i):
        fin_own(i).wait()
        fin_sib(i).wait_send()

    def free_first():
        pl.semaphore_signal(credit.at[2 * nz], inc=1, device_id=sib, device_id_type=MESH)

    plan = sums_plan(nz, nch)

    def sums(place):
        for step_ in plan.get(place, ()):
            if step_[0] == "edge":
                rs_edge(step_[1])
            else:
                rs_tick(*step_)

    tile = min(256, tokens)

    def rows_pass(i, core):
        first = i == 0

        def rows_step(m, carry):
            local_rows = pl.ds(mult(m, tile), tile)
            rows = pl.ds(pl.multiple_of(core * tokens + m * tile, tile), tile)
            xm = x[rows, :]
            gate = dot(xm, w[i, :, :, 0].reshape(width, hc))
            up = dot(xm, w[i, :, :, 1].reshape(width, hc))
            dh = jnp.zeros((tile, hc), f32)
            for k in range(dps):
                dh = dh + dot_nt(ct[rows, k * hc : (k + 1) * hc], w[i, k // 2, k % 2, 2])
            sig = jax.nn.sigmoid(gate)
            act = gate * sig
            hidden = (act * up).astype(bf16)
            d_up = (dh * act).astype(bf16)
            d_gate = (dh * up * sig * (1.0 + gate * (1.0 - sig))).astype(bf16)
            ht[:, rows] = hidden.T
            dgt[:, rows] = d_gate.T
            dut[:, rows] = d_up.T
            mine_too = core is c
            for k in range(dps):
                cols = slice(k * hc, (k + 1) * hc)
                fwd = dot(hidden, w[i, k // 2, k % 2, 2])
                back = dot_nt(d_gate, w[i, k // 2, k % 2, 0]) + dot_nt(d_up, w[i, k // 2, k % 2, 1])
                if not first:
                    fwd = accp[rows, cols].astype(f32) + fwd
                    back = (accb if mine_too else acco)[local_rows, cols].astype(f32) + back
                accp[rows, cols] = fwd.astype(bf16)
                if mine_too:
                    accb[local_rows, cols] = back
                else:
                    acco[local_rows, cols] = back.astype(bf16)
            return carry

        lax.fori_loop(0, tokens // tile, rows_step, 0)

    def cols_pass(i):
        def cols_step(k, carry):
            cols = pl.ds(mult(k, hc), hc)
            xs = x[:, cols]
            chip, core = k // 2, k % 2
            w[i, chip, core, 0] = dot(dgt[...], xs).astype(bf16)
            w[i, chip, core, 1] = dot(dut[...], xs).astype(bf16)
            w[i, chip, core, 2] = dot(ht[...], ct[:, cols]).astype(bf16)
            return carry

        lax.fori_loop(0, dps, cols_step, 0)

    lane = lax.broadcasted_iota(jnp.int32, (1, LANES), 1)
    low_head = lane < HD
    low_half = lane % HD < HD // 2

    def turn(u, cos, sin):
        swapped = jnp.where(low_half, pltpu.roll(u, LANES - HD // 2, 1), pltpu.roll(u, HD // 2, 1))
        return u * cos + swapped * sin

    def turn_back(g, cos, sin):
        v = g * sin
        swapped = jnp.where(low_half, pltpu.roll(v, LANES - HD // 2, 1), pltpu.roll(v, HD // 2, 1))
        return g * cos + swapped

    def tables(rows, with_values):
        cos, sin = cosine[rows, :], sine[rows, :]
        if with_values:
            cos, sin = jnp.where(low_head, cos, 1.0), jnp.where(low_head, sin, 0.0)
        return cos, sin

    step = 32

    def norm_rows(src, dst, base, grad_sum):
        def body(m, carry):
            rows = pl.ds(mult(m, step), step)
            v = src[rows, :].astype(f32)
            scale = lax.rsqrt(jnp.mean(v * v, axis=-1, keepdims=True) + epsilon)
            v = v * scale
            dst[pl.ds(pl.multiple_of(base + m * step, step), step), :] = (v * gv[0:1, :]).astype(bf16)
            if grad_sum is None:
                return carry
            up = grad_sum(rows)
            return carry + jnp.sum(up * v, axis=0, keepdims=True)

        start = 0 if grad_sum is None else jnp.zeros((1, width), f32)
        return lax.fori_loop(0, tokens // step, body, start)

    chunks = aw_cols(hc) // LANES
    per_block = hc // LANES
    atile = min(256, tokens)

    def joined():
        def body(m, carry):
            rows = pl.ds(mult(m, atile), atile)
            src = pl.ds(pl.multiple_of(c * tokens + m * atile, atile), atile)
            xm = x[src, :]
            for j in range(3):
                block = dot(xm, aw[:, :, j].reshape(width, hc))
                for q in range(per_block):
                    index = j * per_block + q
                    cos, sin = tables(rows, index % 3 == 2)
                    u = block[:, q * LANES : (q + 1) * LANES]
                    qkvb[rows, index * LANES : (index + 1) * LANES] = turn(u, cos, sin).astype(bf16)
            return carry

        lax.fori_loop(0, tokens // atile, body, 0)

    row_id = lax.broadcasted_iota(jnp.int32, (SEQ, SEQ), 0)
    col_id = lax.broadcasted_iota(jnp.int32, (SEQ, SEQ), 1)
    keep = row_id >= col_id
    inv_root = 1.0 / math.sqrt(HD)

    def doubled(rows, base):
        kv = qkvb[rows, pl.ds(pl.multiple_of(base + GROUPS * HD, LANES), LANES)].astype(f32)
        other = pltpu.roll(kv, HD, 1)
        kk = jnp.where(low_head, kv, other).astype(bf16)
        vv = jnp.where(low_head, other, kv).astype(bf16)
        return kk, vv

    def softmax(qm, kk):
        scores = jnp.where(keep, dot_nt(qm, kk) * inv_root, masked_score)
        e = jnp.exp(scores - jnp.max(scores, axis=-1, keepdims=True))
        return e * (1.0 / jnp.sum(e, axis=-1, keepdims=True))

    def place(n):
        s, h = n // kv_local, n % kv_local
        rows = pl.ds(mult(s, SEQ), SEQ)
        return rows, h * head_cols, h * GROUPS * HD

    def heads_forward():
        def body(n, carry):
            rows, base, qbase = place(n)
            kk, vv = doubled(rows, base)
            for pair in range(GROUPS // 2):
                qp = qkvb[rows, pl.ds(pl.multiple_of(base + pair * LANES, LANES), LANES)]
                halves = []
                for half in range(2):
                    mask = low_head if half == 0 else ~low_head
                    qm = jnp.where(mask, qp.astype(f32), 0.0).astype(bf16)
                    halves.append(dot(softmax(qm, kk).astype(bf16), vv))
                att[rows, pl.ds(pl.multiple_of(qbase + pair * LANES, LANES), LANES)] = jnp.where(
                    low_head, halves[0], halves[1]
                ).astype(bf16)
            return carry

        lax.fori_loop(0, seqs * kv_local, body, 0)

    def heads_backward():
        def body(n, carry):
            rows, base, qbase = place(n)
            kk, vv = doubled(rows, base)
            dkk = jnp.zeros((SEQ, LANES), f32)
            dvv = jnp.zeros((SEQ, LANES), f32)
            cos, sin = tables(rows, False)
            for pair in range(GROUPS // 2):
                cols = pl.ds(pl.multiple_of(base + pair * LANES, LANES), LANES)
                acols = pl.ds(pl.multiple_of(qbase + pair * LANES, LANES), LANES)
                qp = qkvb[rows, cols].astype(f32)
                dp = datt[rows, acols].astype(f32)
                prod = dp * att[rows, acols].astype(f32)
                halves = []
                for half in range(2):
                    mask = low_head if half == 0 else ~low_head
                    qm = jnp.where(mask, qp, 0.0).astype(bf16)
                    dm = jnp.where(mask, dp, 0.0).astype(bf16)
                    probs = softmax(qm, kk)
                    delta = jnp.sum(jnp.where(mask, prod, 0.0), axis=-1, keepdims=True)
                    ds = (probs * (dot_nt(dm, vv) - delta) * inv_root).astype(bf16)
                    halves.append(dot(ds, kk))
                    dkk = dkk + dot(ds.T, qm)
                    dvv = dvv + dot(probs.astype(bf16).T, dm)
                dq = jnp.where(low_head, halves[0], halves[1])
                qkvb[rows, cols] = turn_back(dq, cos, sin).astype(bf16)
            dkk = dkk + pltpu.roll(dkk, HD, 1)
            dvv = dvv + pltpu.roll(dvv, HD, 1)
            cos, sin = tables(rows, True)
            qkvb[rows, pl.ds(pl.multiple_of(base + GROUPS * HD, LANES), LANES)] = turn_back(
                jnp.where(low_head, dkk, dvv), cos, sin
            ).astype(bf16)
            return carry

        lax.fori_loop(0, seqs * kv_local, body, 0)

    def out_weight(k):
        return aw[k // 2, k % 2, 3:5].reshape(2 * hc, hc)

    def attention_partial():
        def body(k, carry):
            cols = pl.ds(mult(k, hc), hc)
            rsb[:, cols] = dot(att[...], out_weight(k)).astype(bf16)
            return carry

        lax.fori_loop(0, dps, body, 0)

    square = nt == 4
    xp, yp, dg = t ^ 1, t ^ 2, t ^ 3
    half = ts // 2

    def part_rows(base, index, upper):
        return pl.ds(pl.multiple_of(base + index * ts + upper * half, half), half)

    def slice_rows(base, index):
        return pl.ds(pl.multiple_of(base + index * ts, ts), ts)

    def reduce_copy(src, base, land, which, n):
        rows = (
            part_rows(base, xp, 0),
            part_rows(base, dg, 0),
            part_rows(base, yp, 1),
            part_rows(base, dg, 1),
            part_rows(base, yp, 0),
            part_rows(base, xp, 1),
        )[n]
        to = (xp, xp, yp, yp, yp, xp)[n]
        return remote(
            src.at[rows],
            land.at[pl.ds(n * half, half)],
            S["ps_s"](which, n),
            S["ps_r"](which, n),
            (d, to),
        )

    def reduce_direct(src, base, land, which, k, arriving):
        frm = source(k)
        return remote(
            src.at[slice_rows(base, peer(k))],
            land.at[slot(frm if arriving else t)],
            S["ps_s"](which, k),
            S["ps_r"](which, k),
            (d, frm if arriving else peer(k)),
        )

    def reduce_start(src, base, land, which):
        if square:
            for n in range(4):
                reduce_copy(src, base, land, which, n).start()
        else:
            for k in range(nt - 1):
                reduce_direct(src, base, land, which, k, False).start()

    def reduce_mid(src, base, land, which):
        if not square:
            return
        for n, index, upper in ((1, yp, 0), (3, xp, 1)):
            reduce_copy(src, base, land, which, n).wait_recv()
            rows = part_rows(base, index, upper)
            both = src[rows, :].astype(f32) + land[n * half : (n + 1) * half, :].astype(f32)
            src[rows, :] = both.astype(bf16)
            reduce_copy(src, base, land, which, 4 if n == 1 else 5).start()

    def reduce_wait(src, base, land, which):
        if square:
            for n in (0, 2, 4, 5):
                reduce_copy(src, base, land, which, n).wait_recv()
        else:
            for k in range(nt - 1):
                reduce_direct(src, base, land, which, k, True).wait_recv()

    def reduce_end(src, base, land, which):
        if square:
            for n in range(6):
                reduce_copy(src, base, land, which, n).wait_send()
        else:
            for k in range(nt - 1):
                reduce_direct(src, base, land, which, k, False).wait_send()

    def summed(src, base, land, m):
        total = src[pl.ds(pl.multiple_of(base + t * ts + m * step, step), step), :].astype(f32)
        if square:
            upper = m // (half // step)
            inner = (m % (half // step)) * step
            for first in (2 * upper * half, (4 + upper) * half):
                total = total + land[pl.ds(pl.multiple_of(first + inner, step), step), :].astype(f32)
        else:
            for k in range(nt - 1):
                rows = pl.ds(pl.multiple_of(source(k) * ts + m * step, step), step)
                total = total + land[rows, :].astype(f32)
        return total

    def spread_copy(src, src_base, dst, dst_base, which, n):
        index, upper, to = (
            (t, 0, xp),
            (t, 1, xp),
            (t, 1, yp),
            (t, 0, yp),
            (xp, 0, yp),
            (yp, 1, xp),
        )[n]
        from_rows = part_rows(src_base, t, upper) if n < 4 else part_rows(dst_base, index, upper)
        return remote(
            (src if n < 4 else dst).at[from_rows],
            dst.at[part_rows(dst_base, index, upper)],
            S["ga_s"](which, n),
            S["ga_r"](which, n),
            (d, to),
        )

    def spread_arrive(src, src_base, dst, dst_base, which, n):
        index, upper, frm = (
            (xp, 0, xp),
            (xp, 1, xp),
            (yp, 1, yp),
            (yp, 0, yp),
            (dg, 0, yp),
            (dg, 1, xp),
        )[n]
        return remote(
            src.at[part_rows(src_base, t, upper)],
            dst.at[part_rows(dst_base, index, upper)],
            S["ga_s"](which, n),
            S["ga_r"](which, n),
            (d, frm),
        )

    def spread_direct(src, src_base, dst, dst_base, which, k, arriving):
        frm = source(k)
        return remote(
            src.at[slice_rows(src_base, t)],
            dst.at[slice_rows(dst_base, frm if arriving else t)],
            S["ga_s"](which, k),
            S["ga_r"](which, k),
            (d, frm if arriving else peer(k)),
        )

    def spread_start(*args):
        if square:
            for n in range(4):
                spread_copy(*args, n).start()
        else:
            for k in range(nt - 1):
                spread_direct(*args, k, False).start()

    def spread_mid(*args):
        if square:
            for n, onward in ((0, 4), (2, 5)):
                spread_arrive(*args, n).wait_recv()
                spread_copy(*args, onward).start()

    def spread_wait(*args):
        if square:
            for n in (1, 3, 4, 5):
                spread_arrive(*args, n).wait_recv()
        else:
            for k in range(nt - 1):
                spread_direct(*args, k, True).wait_recv()

    def spread_end(*args):
        if square:
            for n in range(6):
                spread_copy(*args, n).wait_send()
        else:
            for k in range(nt - 1):
                spread_direct(*args, k, False).wait_send()

    q_tick(0)
    for i in range(nch):
        for kind in range(3):
            own_copy(i, kind).start()
            sib_copy(i, kind).start()
    cot_own = pltpu.make_async_copy(cot, ct.at[core_rows(c)], S["cot"](0))
    cot_sib = remote(cot, ct.at[core_rows(c)], S["cot"](1), S["cot"](2), sib)
    cot_in = remote(cot, ct.at[core_rows(1 - c)], S["cot"](1), S["cot"](2), sib)
    cot_own.start()
    cot_sib.start()
    quarter = HD // 2
    exponent = lax.broadcasted_iota(jnp.int32, (quarter, 1), 0).astype(f32) * (2.0 / HD)
    angles = jnp.exp(exponent * -math.log(rope_base)) * pos[...].astype(f32)
    cos_rows, sin_rows = jnp.cos(angles), jnp.sin(angles)
    cosine[...] = jnp.concatenate([cos_rows] * (LANES // quarter), axis=0).T
    sine[...] = jnp.concatenate([-sin_rows, sin_rows] * (LANES // HD), axis=0).T
    for s in range(1, nz):
        if s == nz - 1:
            ag_tick(0, 0)
        q_tick(s)
    if nz == 1:
        ag_tick(0, 0)
    q_finish()
    for k in range(dps):
        gv[:, k * hc : (k + 1) * hc] = gw[k // 2, k % 2].astype(f32)
    tok_all.wait()
    norm_rows(p2, x, c * tokens, None)
    joined()
    heads_forward()
    if nz > 1:
        ag_tick(0, 1)
    attention_partial()
    first_sum = (rsb, 0, p1, 0)
    reduce_start(*first_sum)
    if nz > 2:
        ag_tick(0, 2)
    reduce_mid(*first_sum)
    if nz > 3:
        ag_tick(1, 0)
    reduce_wait(*first_sum)
    mine = half_rows(c, t)

    def second_norm(m, carry):
        rows = pl.ds(mult(m, step), step)
        trow = pl.ds(pl.multiple_of(t * ts + m * step, step), step)
        total = p2[trow, :].astype(f32) + summed(rsb, 0, p1, m)
        resid[rows, :] = total
        scale = lax.rsqrt(jnp.mean(total * total, axis=-1, keepdims=True) + epsilon)
        x[pl.ds(pl.multiple_of(c * tokens + t * ts + m * step, step), step), :] = (
            total * scale * gv[1:2, :]
        ).astype(bf16)
        return carry

    lax.fori_loop(0, ts // step, second_norm, 0)
    x_spread = (x, c * tokens, x, c * tokens, 3)

    def xs_index(k):
        if square:
            return (t, xp, yp, dg)[k]
        return lax.rem(t - k + nt, nt)

    def xs_copy(k):
        rows = half_rows(c, xs_index(k))
        return remote(x.at[rows], x.at[rows], S["xs_s"](k), S["xs_r"](k), sib)

    def xs_in(k):
        rows = half_rows(1 - c, xs_index(k))
        return remote(x.at[rows], x.at[rows], S["xs_s"](k), S["xs_r"](k), sib)

    spread_start(*x_spread)
    xs_copy(0).start()
    spread_mid(*x_spread)
    if square:
        spread_arrive(*x_spread, 1).wait_recv()
        xs_copy(1).start()
        spread_arrive(*x_spread, 3).wait_recv()
        xs_copy(2).start()
    for s in range(3, nz):
        ag_tick(0, s)
    ag_finish(0)
    if nz <= 3:
        ag_tick(1, 0)
    if square:
        for n in (4, 5):
            spread_arrive(*x_spread, n).wait_recv()
        xs_copy(3).start()
    else:
        for k in range(nt - 1):
            spread_direct(*x_spread, k, True).wait_recv()
            xs_copy(k + 1).start()
    cot_own.wait()
    cot_in.wait_recv()
    for k in range(nt):
        xs_in(k).wait_recv()

    last = nch - 1
    other = (1 - c) * tokens
    for i in range(last):
        if i > 0:
            ag_tick(i + 1, 0)
        sums(4 * i - 1)
        rows_pass(i, 1 - c)
        rows_pass(i, c)
        cols_pass(i)
        sums(4 * i)
        for s in range(1, nz):
            ag_tick(i + 1, s)
            if s < 3:
                sums(4 * i + s)
        ag_finish(i + 1)

    def sib_b(k):
        return remote(acco.at[slot(k)], sbr_b.at[slot(k)], S["sb_s"](0, k), S["sb_r"](0, k), sib)

    def sib_p(k):
        return remote(
            accp.at[half_rows(1 - c, k)], sbr_p.at[slot(k)], S["sb_s"](1, k), S["sb_r"](1, k), sib
        )

    for u in range(nz):
        for part in range(2):
            q_sib(part, u).wait_send()
    spread_end(*x_spread)
    reduce_end(*first_sum)
    for k in range(nt):
        xs_copy(k).wait_send()
    sums(4 * last - 1)
    rows_pass(last, 1 - c)
    for k in range(nt):
        sib_b(k).start()
    rows_pass(last, c)
    for k in range(nt):
        sib_b(k).wait_recv()

    def pair_b(m, carry):
        rows = pl.ds(mult(m, step), step)
        rsb[rows, :] = (accb[rows, :] + sbr_b[rows, :].astype(f32)).astype(bf16)
        return carry

    lax.fori_loop(0, tokens // step, pair_b, 0)
    back_sum = (rsb, 0, p2, 1)
    reduce_start(*back_sum)
    cols_pass(last)
    sums(4 * last)
    for k in range(nt):
        sib_p(k).start()
    reduce_mid(*back_sum)
    sums(4 * last + 1)
    reduce_wait(*back_sum)

    def second_back(m, carry):
        rows = pl.ds(mult(m, step), step)
        place_ = pl.ds(pl.multiple_of(c * tokens + t * ts + m * step, step), step)
        up = summed(rsb, 0, p2, m)
        v = resid[rows, :]
        scale = lax.rsqrt(jnp.mean(v * v, axis=-1, keepdims=True) + epsilon)
        weighted = up * gv[1:2, :]
        inner = jnp.mean(weighted * v, axis=-1, keepdims=True)
        grad = ct[place_, :].astype(f32) + scale * weighted - v * (scale * scale * scale) * inner
        accb[rows, :] = grad
        x[place_, :] = grad.astype(bf16)
        return carry + jnp.sum(up * v * scale, axis=0, keepdims=True)

    gain_two = lax.fori_loop(0, ts // step, second_back, jnp.zeros((1, width), f32))
    rg_spread = (x, c * tokens, x, c * tokens, 0)
    spread_start(*rg_spread)
    spread_mid(*rg_spread)
    sums(4 * last + 2)
    reduce_end(*back_sum)
    for k in range(nt):
        sib_p(k).wait_recv()

    def pair_p(m, carry):
        rows = pl.ds(mult(m, step), step)
        here = pl.ds(pl.multiple_of(c * tokens + m * step, step), step)
        rsb[rows, :] = (accp[here, :].astype(f32) + sbr_p[rows, :].astype(f32)).astype(bf16)
        return carry

    lax.fori_loop(0, tokens // step, pair_p, 0)

    spread_wait(*rg_spread)
    out_sum = (rsb, 0, p1, 2)
    reduce_start(*out_sum)
    sums(4 * last + 3)
    fin_start(0)

    def d_attended(m, carry):
        rows = pl.ds(mult(m, atile), atile)
        src = pl.ds(pl.multiple_of(c * tokens + m * atile, atile), atile)
        for j in range(2):
            total = jnp.zeros((atile, hc), f32)
            for k in range(dps):
                total = total + dot_nt(x[src, k * hc : (k + 1) * hc], aw[k // 2, k % 2, 3 + j])
            datt[rows, j * hc : (j + 1) * hc] = total.astype(bf16)
        for j in range(2):
            (ht, dgt)[j][:, rows] = att[rows, j * hc : (j + 1) * hc].T
        return carry

    lax.fori_loop(0, tokens // atile, d_attended, 0)

    def out_grads(k, carry):
        xs = x[core_rows(c), pl.ds(mult(k, hc), hc)]
        for j in range(2):
            aw[k // 2, k % 2, 3 + j] = dot((ht, dgt)[j][:, :tokens], xs).astype(bf16)
        return carry

    lax.fori_loop(0, dps, out_grads, 0)

    def a_src(part, u, core):
        return (aw.at[u, core, 3:5], aw.at[u, core, 0:3], gg.at[u, core])[part]

    def a_sib_ref(part):
        return (w.at[0, :, 1, 0:2], w.at[0, :, 0], gsib)[part]

    def a_sib(part):
        src = (aw.at[:, 1 - c, 3:5], aw.at[:, 1 - c, 0:3], gg.at[:, 1 - c])[part]
        return remote(src, a_sib_ref(part), S["as_s"](part), S["as_r"](part), sib)

    def a_land(part, direction, tau):
        line = (ru, rd)[direction]
        return (line.at[tau, 1, 0:2], line.at[tau, 0], (gru, grd)[direction].at[tau])[part]

    def a_line(part, tau, direction):
        return remote(
            a_src(part, rs_owner(tau, direction), c),
            a_land(part, direction, tau),
            S["ar_s"](part, direction, tau),
            S["ar_r"](part, direction, tau),
            (above, below)[direction],
        )

    def a_add(part, owner, got):
        if part == 2:
            gg[owner, c] = gg[owner, c] + got[...]
            return
        base, count = ((3, 2), (0, 3))[part]
        for j in range(count):
            both = aw[owner, c, base + j].astype(f32) + got[j].astype(f32)
            aw[owner, c, base + j] = both.astype(bf16)

    def a_pair(part):
        a_sib(part).wait_recv()

        def body(u, carry):
            a_add(part, u, (w.at[0, u, 1, 0:2], w.at[0, u, 0], gsib.at[u])[part])
            return carry

        lax.fori_loop(0, nz, body, 0)

    def a_tick(part, tau):
        for direction in range(2):
            if tau > 0:

                @pl.when(rs_valid(tau, direction) & (has_below, has_above)[direction])
                def _():
                    owner = rs_owner(tau, direction)
                    remote(
                        a_src(part, owner, c),
                        a_land(part, direction, tau - 1),
                        S["ar_s"](part, direction, tau - 1),
                        S["ar_r"](part, direction, tau - 1),
                        (below, above)[direction],
                    ).wait_recv()
                    a_add(part, owner, a_land(part, direction, tau - 1))

            if tau < nz - 1:

                @pl.when(rs_valid(tau, direction))
                def _():
                    if part == 0:
                        take_slot(direction, tau)
                    a_line(part, tau, direction).start()

    def a_finish(part):
        a_sib(part).wait_send()
        for tau in range(nz - 1):
            for direction in range(2):

                @pl.when(rs_valid(tau, direction))
                def _():
                    a_line(part, tau, direction).wait_send()

    fin_finish(0)
    free_first()
    pl.semaphore_wait(credit.at[2 * nz], 1)
    a_sib(0).start()
    tok_again = pltpu.make_async_copy(tok, sbr_b, S["tok"](1))
    tok_again.start()
    sums(4 * last + 4)
    heads_backward()
    a_pair(0)

    def attn_back(k, carry):
        total = jnp.zeros((tokens, hc), f32)
        for j in range(3):
            total = total + dot_nt(qkvb[:, j * hc : (j + 1) * hc], aw[k // 2, k % 2, j])
        x[pl.ds(mult(1 - c, tokens), tokens), pl.ds(mult(k, hc), hc)] = total.astype(bf16)
        return carry

    lax.fori_loop(0, dps, attn_back, 0)
    tail_sum = (x, other, p2, 3)
    reduce_start(*tail_sum)
    reduce_mid(*out_sum)
    sums(4 * last + 5)
    tok_again.wait()

    def own_back(rows):
        return x[pl.ds(pl.multiple_of(other + rows.start, step), step), :].astype(f32)

    gain_one = norm_rows(sbr_b, sbr_p, 0, own_back)
    for k in range(dps):
        cols = slice(k * hc, (k + 1) * hc)
        gg[k // 2, k % 2] = jnp.concatenate(
            [gain_one[:, cols], gain_two[:, cols], jnp.zeros((6, hc), f32)], axis=0
        )
    a_sib(2).start()
    for m in range(tokens // atile):
        for j in range(3):
            (ht, dgt, dut)[j][:, tokens + m * atile : tokens + (m + 1) * atile] = qkvb[
                m * atile : (m + 1) * atile, j * hc : (j + 1) * hc
            ].T

    def qkv_grads(k, carry):
        xs = sbr_p[:, pl.ds(mult(k, hc), hc)]
        for j in range(3):
            aw[k // 2, k % 2, j] = dot((ht, dgt, dut)[j][:, tokens:], xs).astype(bf16)
        return carry

    lax.fori_loop(0, dps, qkv_grads, 0)
    a_sib(1).start()
    sums(4 * last + 6)
    a_tick(0, 0)
    reduce_mid(*tail_sum)
    a_pair(1)
    a_pair(2)
    a_tick(1, 0)
    a_tick(2, 0)
    fin_start(1)

    reduce_wait(*out_sum)

    def finish_output(m, carry):
        rows = pl.ds(mult(m, step), step)
        where = pl.ds(pl.multiple_of(c * tokens + t * ts + m * step, step), step)
        accp[where, :] = (resid[rows, :] + summed(rsb, 0, p1, m)).astype(bf16)
        return carry

    lax.fori_loop(0, ts // step, finish_output, 0)
    out_spread = (accp, c * tokens, out, 0, 1)
    spread_start(*out_spread)
    put_out = pltpu.make_async_copy(accp.at[mine], out.at[slot(t)], S["loc"](0))
    put_out.start()
    sums(4 * last + 7)

    reduce_wait(*tail_sum)
    for k in range(nt):
        sib_p(k).wait_send()
    theirs = half_rows(1 - c, t)

    def finish_tokens(m, carry):
        rows = pl.ds(mult(m, step), step)
        up = summed(x, other, p2, m)
        v = sbr_b[pl.ds(pl.multiple_of(t * ts + m * step, step), step), :].astype(f32)
        scale = lax.rsqrt(jnp.mean(v * v, axis=-1, keepdims=True) + epsilon)
        weighted = up * gv[0:1, :]
        inner = jnp.mean(weighted * v, axis=-1, keepdims=True)
        grad = accb[rows, :] + scale * weighted - v * (scale * scale * scale) * inner
        accp[pl.ds(pl.multiple_of(other + t * ts + m * step, step), step), :] = grad.astype(bf16)
        return carry

    lax.fori_loop(0, ts // step, finish_tokens, 0)
    tok_spread = (accp, other, dtok, 0, 2)
    spread_start(*tok_spread)
    put_tok = pltpu.make_async_copy(accp.at[theirs], dtok.at[slot(t)], S["loc"](1))
    put_tok.start()
    fin_finish(1)
    spread_mid(*out_spread)
    spread_mid(*tok_spread)
    sums(4 * last + 8)
    for part in range(3):
        a_tick(part, 1)
    fin_start(2)
    fin_finish(2)
    sums(4 * last + 9)
    for s in range(2, nz):
        for part in range(3):
            a_tick(part, s)
        if s == nz - 2:
            fin_start(3)
    fin_finish(3)

    def gain_copy(k):
        return remote(gg.at[z, c], gt.at[t], S["gg_s"](k), S["gg_r"](k), (d, peer(k)))

    def gain_in(k):
        return remote(gg.at[z, c], gt.at[source(k)], S["gg_s"](k), S["gg_r"](k), (d, source(k)))

    for k in range(nt - 1):
        gain_copy(k).start()
    gt[t] = gg[z, c]

    put_attn = pltpu.make_async_copy(aw.at[z, c], g_attn, S["loc"](2))
    put_attn.start()
    for k in range(nt - 1):
        gain_in(k).wait_recv()
    total = gt[0]
    for k in range(1, nt):
        total = total + gt[k]
    g_gains[...] = total

    for i in range(nch):
        for kind in range(3):
            sib_copy(i, kind).wait_send()
    cot_sib.wait_send()
    for part in range(3):
        a_finish(part)
    for k in range(nt - 1):
        gain_copy(k).wait_send()
    for k in range(nt):
        sib_b(k).wait_send()
    rs_end()
    reduce_end(*out_sum)
    reduce_end(*tail_sum)
    spread_wait(*out_spread)
    spread_wait(*tok_spread)
    for args in (rg_spread, out_spread, tok_spread):
        spread_end(*args)
    put_out.wait()
    put_tok.wait()
    put_attn.wait()
    for i in range(nch):
        fin_in(i).wait_recv()


def aw_cols(shard):
    return 3 * shard


def layer(tokens, cotangent, weights, positions, gain_a, gain_f, nz, nt):
    count, width = tokens.shape
    hc, hid = weights[2].shape
    nch = hid // (2 * hc)
    ts = count // nt
    sizes = (nz, nt, nch, count, width, hc)
    sems, _ = semaphores(nz, nt, nch)
    V = pltpu.VMEM
    recv = (nz - 1, 2, 3, hc, hc)
    S = jax.ShapeDtypeStruct
    return pl.pallas_call(
        functools.partial(layer_kernel, sizes),
        out_shape=(
            S((count, width), bf16),
            S((count, width), bf16),
            S((5, hc, hc), bf16),
            S((nch, 2, 3, hc, hc), bf16),
            S((8, hc), f32),
        ),
        in_specs=[HBM] * 7 + [VMEM] * 3,
        out_specs=(HBM, HBM, HBM, HBM, VMEM),
        scratch_shapes=[
            V((nch, nz, 2, 3, hc, hc), bf16),
            V(recv, bf16),
            V(recv, bf16),
            V((2 * count, width), bf16),
            V((2 * count, width), bf16),
            V((2 * count, width), bf16),
            V((count, width), f32),
            V((count, width), bf16),
            V((hc, 2 * count), bf16),
            V((hc, 2 * count), bf16),
            V((hc, 2 * count), bf16),
            V((ts, width), f32),
            V((count, width), bf16),
            V((count, width), bf16),
            V((count, width), bf16),
            V((count, width), bf16),
            V((count, width), bf16),
            V((nz, 2, 5, hc, hc), bf16),
            V((count, 3 * hc), bf16),
            V((count, 2 * hc), bf16),
            V((count, 2 * hc), bf16),
            V((nz, 2, 16, hc), bf16),
            V((16, width), f32),
            V((nz, 2, 8, hc), f32),
            V((nz, 8, hc), f32),
            V((nz - 1, 8, hc), f32),
            V((nz - 1, 8, hc), f32),
            V((nt, 8, hc), f32),
            V((count, LANES), f32),
            V((count, LANES), f32),
            pltpu.SemaphoreType.DMA((sems.count,)),
            pltpu.SemaphoreType.REGULAR((2 * nz + 1,)),
        ],
        compiler_params=pltpu.CompilerParams(
            collective_id=0, has_side_effects=True, vmem_limit_bytes=63 * 2**20
        ),
        name="layer",
    )(tokens, cotangent, *weights, positions, gain_a, gain_f)


def results_kernel(
    out, dtok, attn, ffn, gains, *refs
):
    results, (rows_a, rows_b, attn_in, ffn_in, qkv, proj, gate, up, down, sem) = refs[:9], refs[9:]
    nch, _, _, hc, _ = ffn.shape
    pieces = nch * 2
    used = iter(range(sem.shape[0]))

    def copy(src, dst):
        return pltpu.make_async_copy(src, dst, sem.at[next(used)])

    loads = [copy(ffn.at[n // 2, n % 2], ffn_in.at[n]) for n in range(pieces)]
    load_attn = copy(attn, attn_in)
    parts = 2
    moves = []
    for src, held, dst in ((out, rows_a, results[0]), (dtok, rows_b, results[1])):
        count = src.shape[0] // parts
        for k in range(parts):
            at = pl.ds(k * count, count)
            moves.append((copy(src.at[at], held.at[at]), copy(held.at[at], dst.at[at])))
    for load in loads:
        load.start()
    load_attn.start()
    for load, _ in moves:
        load.start()
    stores = []

    def store(src, dst):
        stores.append(copy(src, dst))
        stores[-1].start()

    for n in range(pieces):
        loads[n].wait()
        at = pl.ds(n * hc, hc)
        gate[:, at] = ffn_in[n, 0].T.astype(f32)
        store(gate.at[:, at], results[4].at[:, at])
        up[:, at] = ffn_in[n, 1].T.astype(f32)
        store(up.at[:, at], results[5].at[:, at])
        down[at, :] = ffn_in[n, 2].astype(f32)
        store(down.at[at], results[6].at[at])
        if n % 2 == 1 and moves:
            load, onward = moves.pop(0)
            load.wait()
            onward.start()
            stores.append(onward)
    for load, onward in moves:
        load.wait()
        onward.start()
        stores.append(onward)
    load_attn.wait()
    for j in range(3):
        qkv[:, j * hc : (j + 1) * hc] = attn_in[j].T.astype(f32)
    store(qkv, results[2])
    for j in range(2):
        proj[j * hc : (j + 1) * hc, :] = attn_in[3 + j].astype(f32)
    store(proj, results[3])
    for n in range(2):
        results[7 + n][...] = gains[n, :]
    for one in stores:
        one.wait()


def finished(out, dtok, attn, ffn, gains):
    count, width = out.shape
    nch, _, _, hc, _ = ffn.shape
    hid = nch * 2 * hc
    S = jax.ShapeDtypeStruct
    V = pltpu.VMEM
    grads = [(hc, 3 * hc), (2 * hc, hc), (hc, hid), (hc, hid), (hid, hc)]
    return pl.pallas_call(
        results_kernel,
        out_shape=[S((count, width), bf16)] * 2 + [S(g, f32) for g in grads] + [S((hc,), f32)] * 2,
        in_specs=[HBM] * 4 + [VMEM],
        out_specs=[HBM] * 7 + [VMEM] * 2,
        scratch_shapes=[
            V((count, width), bf16),
            V((count, width), bf16),
            V((5, hc, hc), bf16),
            V((nch * 2, 3, hc, hc), bf16),
        ]
        + [V(g, f32) for g in grads]
        + [pltpu.SemaphoreType.DMA((nch * 2 * 4 + 16,))],
        compiler_params=pltpu.CompilerParams(vmem_limit_bytes=60 * 2**20),
        name="results",
    )(out, dtok, attn, ffn, gains)


def local(tokens, positions, w_qkv, w_out, w_gate, w_up, w_down, gain_attn, gain_ffn, cotangent):
    nz = lax.axis_size("dp") // 2
    nt = lax.axis_size("tensor")
    results = layer(
        tokens,
        cotangent,
        (w_qkv, w_out, w_gate, w_up, w_down),
        positions.reshape(1, -1),
        gain_attn,
        gain_ffn,
        nz,
        nt,
    )
    return tuple(finished(*results))


def solution(mesh):
    return jax.shard_map(
        local,
        mesh=mesh,
        in_specs=(
            P("dp", None),
            P("dp"),
            P("dp", "tensor"),
            P("tensor", "dp"),
            P("dp", "tensor"),
            P("dp", "tensor"),
            P("tensor", "dp"),
            P("dp"),
            P("dp"),
            P("dp", None),
        ),
        out_specs=(
            P("dp", None),
            P("dp", None),
            P("dp", "tensor"),
            P("tensor", "dp"),
            P("dp", "tensor"),
            P("dp", "tensor"),
            P("tensor", "dp"),
            P("dp"),
            P("dp"),
        ),
        check_vma=False,
    )
```
